256 devices in a mesh: grow: 16 (over x, z_lo, core), cy: 4 (over y), cz: 4 (over z_hi).
Axes of the slice: x: 4, y: 4, z: 8 (z_hi: 4, z_lo: 2; z = z_hi * 2 + z_lo), core: 2. Of those that a mesh axis runs over, the one named last changes fastest.
Arguments:
- labels: int32 [64, 512, 512], P('grow', 'cy', 'cz'), may hold values 0 or 1
- roughness: float32 [64, 512, 512], P('grow', 'cy', 'cz'), may hold values from 0 to 1
- potential: float32 [64, 512, 512], P('grow', 'cy', 'cz'), may hold values from 0 to 1
- displacement: float32 [3, 64, 512, 512], P(None, 'grow', 'cy', 'cz'), may hold values from -1.8 to 1.8
Outputs:
- phase_out: float32 [64, 512, 512], P('grow', 'cy', 'cz')
- potential_out: float32 [64, 512, 512], P('grow', 'cy', 'cz')
- displacement_out: float32 [3, 64, 512, 512], P(None, 'grow', 'cy', 'cz')
The draws below stay inside these ranges and needn't reach their ends.
All inputs are finite; a program needn't handle non-finite values. No bound on the sum of `labels` on one device may be relied on, other than what follows from the above.
Results may differ from the reference program's by a relative error of at most 0.00002.
Values sent between devices are 32-bit elements; how exact they have to be, the bound alone decides.
A program may use at most 64 MiB of HBM per device.

```python
import jax
import jax.numpy as jnp

STEPS = 2
SWEEPS = 3
NX = 64
NY = 512
NZ = 512
SHIFT = 4


def set_ends(result, own_key, least, top_value):
    spot = [jax.random.randint(jax.random.fold_in(own_key, axis), (), 0, length) for axis, length in enumerate(result.shape)]
    widest = result.shape.index(max(result.shape))
    beside = spot[:widest] + [(spot[widest] + 1) % result.shape[widest]] + spot[widest + 1:]
    return result.at[tuple(spot)].set(least).at[tuple(beside)].set(top_value)


def block_scale(stream_key, shape, cuts, smallest, high):
    loudness, own = 1.0, jax.random.fold_in(stream_key, 6)
    for dim, parts in cuts:
        draws = jnp.exp(jax.random.uniform(jax.random.fold_in(own, dim), (parts,), jnp.float32, smallest / len(cuts), high / len(cuts)))
        loudness = loudness * jnp.repeat(draws, shape[dim] // parts).reshape([-1 if axis == dim else 1 for axis in range(len(shape))])
    return loudness


def bell_draw(own_key, dims, deviation, most, shards=(), held_as=jnp.bfloat16):
    gain = block_scale(own_key, dims, shards, -0.22, 0.18) if shards else 1.0
    values = jax.random.normal(own_key, dims, jnp.float32) * deviation * gain
    return jnp.minimum(jnp.maximum(values, -most), most).astype(held_as)


def setup_inputs(seed: int = 0) -> dict:
    key_of = jax.random.split(jax.random.key(seed), 5)
    labels = set_ends((jax.random.randint(key_of[0], (NX, NY, NZ), 0, 3) < 1).astype(jnp.int32), jax.random.fold_in(key_of[0], 1), 0, 1)
    roughness = jnp.clip(1.0 * jax.random.uniform(key_of[1], (NX, NY, NZ), jnp.float32) ** block_scale(key_of[1], (NX, NY, NZ), ((0, 16), (1, 4), (2, 4)), -0.2, 0.2), 0.0, 1.0)
    potential = jnp.clip(1.0 * jax.random.uniform(key_of[2], (NX, NY, NZ), jnp.float32) ** block_scale(key_of[2], (NX, NY, NZ), ((0, 16), (1, 4), (2, 4)), -0.2, 0.2), 0.0, 1.0)
    displacement = bell_draw(key_of[3], (3, NX, NY, NZ), 0.3, 1.8, ((1, 16), (2, 4), (3, 4)), jnp.float32)
    return dict(labels=labels, roughness=roughness, potential=potential, displacement=displacement)


TAU_P = 0.15
TAU_U = 0.08
SHEAR = 1.0
LAME_FIRST = 1.5
STIFF = 6.5
EIGEN = 0.1
COND_EL = 0.1
COND_LI = 0.9
V_HIGH = 1.0
TIME_STEP = 0.05
REST = 0.5
OMEGA_THIRD = 0.1
RATE = 0.5


def unit(direction, sign):
    offsets = [0, 0, 0]
    offsets[direction] = sign
    return offsets


def offset(field, offsets):
    lead_dims = field.ndim - 3
    slices = [slice(None)] * lead_dims
    for direction in range(3):
        extent = field.shape[lead_dims + direction]
        slices.append(slice(1 + offsets[direction], extent - 1 + offsets[direction]))
    return field[tuple(slices)]


def centre(field):
    return offset(field, (0, 0, 0))


def laplace(field):
    total = -6.0 * centre(field)
    for direction in range(3):
        total = total + offset(field, unit(direction, 1)) + offset(field, unit(direction, -1))
    return total


def interp(phase):
    return phase * phase * (3.0 - 2.0 * phase)


def interp_slope(phase):
    return 6.0 * phase * (1.0 - phase)


def potential_sweep(potential_pad, conduct_pad):
    here = centre(potential_pad)
    conduct_here = centre(conduct_pad)
    flux = jnp.zeros_like(here)
    for direction in range(3):
        for sign in (1, -1):
            moved = unit(direction, sign)
            flux = flux + 0.5 * (offset(conduct_pad, moved) + conduct_here) * (offset(potential_pad, moved) - here)
    return here + TAU_P * flux


def cross_term(field, first, second):
    total = jnp.zeros_like(centre(field))
    for sign_first in (1, -1):
        for sign_second in (1, -1):
            offsets = [0, 0, 0]
            offsets[first] = sign_first
            offsets[second] = sign_second
            total = total + (sign_first * sign_second) * offset(field, offsets)
    return 0.25 * total


def elastic_sweep(disp_pad, interp_pad):
    updated = []
    for component in range(3):
        own = disp_pad[component]
        grad_div = offset(own, unit(component, 1)) - 2.0 * centre(own) + offset(own, unit(component, -1))
        for other in range(3):
            if other != component:
                grad_div = grad_div + cross_term(disp_pad[other], component, other)
        slope = 0.5 * (offset(interp_pad, unit(component, 1)) - offset(interp_pad, unit(component, -1)))
        force = SHEAR * laplace(own) + (LAME_FIRST + SHEAR) * grad_div - STIFF * EIGEN * slope
        updated.append(centre(own) + TAU_U * force)
    return jnp.stack(updated)


def divergence(disp_pad):
    total = jnp.zeros_like(centre(disp_pad[0]))
    for component in range(3):
        total = total + 0.5 * (offset(disp_pad[component], unit(component, 1)) - offset(disp_pad[component], unit(component, -1)))
    return total


def phase_update(phase_pad, potential, div_disp):
    phase = centre(phase_pad)
    trace = STIFF * (div_disp - 3.0 * EIGEN * interp(phase))
    over = potential - REST + OMEGA_THIRD * trace
    drive = jnp.exp(over) - jnp.exp(-over)
    change = laplace(phase_pad) - 2.0 * phase * (1.0 - phase) * (1.0 - 2.0 * phase) - RATE * interp_slope(phase) * drive
    return phase + TIME_STEP * change


def pad_cells(field, width, low, high):
    lead_dims = field.ndim - 3
    widths = [(0, 0)] * lead_dims + [(width, width), (0, 0), (0, 0)]
    values = [(0.0, 0.0)] * lead_dims + [(low, high), (0.0, 0.0), (0.0, 0.0)]
    field = jnp.pad(field, widths, constant_values=values)
    widths = [(0, 0)] * lead_dims + [(0, 0), (width, width), (width, width)]
    return jnp.pad(field, widths, mode="wrap")


def reference(labels, roughness, potential, displacement):
    mark = labels.astype(jnp.float32)
    phase = mark * (1.0 - 0.3 * roughness) + (1.0 - mark) * (0.3 * roughness)
    for step_index in range(STEPS):
        phase_pad = pad_cells(phase, 1, 1.0, 0.0)
        interp_pad = interp(phase_pad)
        conduct_pad = COND_EL + COND_LI * interp_pad
        for repeat in range(SWEEPS):
            potential = potential_sweep(pad_cells(potential, 1, 0.0, V_HIGH), conduct_pad)
        for repeat in range(SWEEPS):
            displacement = elastic_sweep(pad_cells(displacement, 1, 0.0, 0.0), interp_pad)
        div_disp = divergence(pad_cells(displacement, 1, 0.0, 0.0))
        phase = phase_update(phase_pad, potential, div_disp)
    phase_out = jnp.concatenate([phase[SHIFT:], jnp.zeros((SHIFT, NY, NZ), jnp.float32)], axis=0)
    potential_out = jnp.concatenate([potential[SHIFT:], jnp.full((SHIFT, NY, NZ), V_HIGH, jnp.float32)], axis=0)
    displacement_out = jnp.concatenate([displacement[:, SHIFT:], jnp.zeros((3, SHIFT, NY, NZ), jnp.float32)], axis=1)
    return phase_out, potential_out, displacement_out
```

```python
import functools

import jax
import jax.numpy as jnp
from jax import lax
from jax.experimental import pallas as pl
from jax.experimental.pallas import tpu as pltpu
from jax.sharding import PartitionSpec as P

MESH = pl.DeviceIdType.MESH
LANES = 128
TOP = 8
CHUNK = 32
LEVELS = 7
COPIES = 160


class Wires:
    def __init__(self, send_sem, recv_sem, place):
        self.send_sem, self.recv_sem = send_sem, recv_sem
        self.g, self.y, self.z, self.ng, self.ny, self.nz = place
        self.count = 0
        self.pending = []

    def send(self, src, dst, dg, dy, dz):
        index = self.count
        self.count += 1
        target = (
            self.g + dg,
            lax.rem(self.y + dy + self.ny, self.ny),
            lax.rem(self.z + dz + self.nz, self.nz),
        )
        copy = pltpu.make_async_remote_copy(
            src_ref=src,
            dst_ref=dst,
            send_sem=self.send_sem.at[index],
            recv_sem=self.recv_sem.at[index],
            device_id=target,
            device_id_type=MESH,
        )
        self.when_valid(dg, copy.start)
        self.pending.append((dg, copy))
        return (dg, copy)

    def when_valid(self, dg, action):
        if dg == 0:
            action()
        else:
            ok = self.g + dg >= 0 if dg < 0 else self.g + dg < self.ng
            pl.when(ok)(action)

    def receive(self, messages):
        for dg, copy in messages:
            self.when_valid(-dg, copy.wait_recv)

    def drain(self):
        for dg, copy in self.pending:
            self.when_valid(dg, copy.wait_send)


def kernel(
    ng, ny, nz,
    lab, rough, pot, disp,
    ph_out, pot_out, u_out,
    UE, CE, RCU, SCU, PH, RCP, SCP,
    HH, CC, GZ, CZP, CZM, PZ, ZB, SB, PZP, PZM, TS, TT, HT,
    send_sem, recv_sem,
):
    g, y, z = lax.axis_index("grow"), lax.axis_index("cy"), lax.axis_index("cz")
    wires = Wires(send_sem, recv_sem, (g, y, z, ng, ny, nz))
    slab = lab.shape[0]
    rows = lab.shape[1]
    low, high = TOP - 1, TOP + rows
    own = slice(TOP, TOP + rows)
    pairs = 4 * slab

    barrier = pltpu.get_barrier_semaphore()
    around = [(a, b) for a in (-1, 0, 1) for b in (-1, 0, 1)]
    partners = [(0, a, b) for a, b in around if (a, b) != (0, 0)]
    partners += [(s, a, b) for s in (-1, 1) for a, b in around]
    partners += [(-2, 0, 0), (2, 0, 0)]
    for dg, dy, dz in partners:
        def greet(dg=dg, dy=dy, dz=dz):
            pl.semaphore_signal(
                barrier,
                inc=1,
                device_id=(
                    g + dg,
                    lax.rem(y + dy + ny, ny),
                    lax.rem(z + dz + nz, nz),
                ),
                device_id_type=MESH,
            )
        wires.when_valid(dg, greet)

    for c in range(3):
        for p in range(slab):
            UE[0, c, 1 + p, own, :] = disp[c, p]
    for p in range(slab):
        UE[0, 3, 1 + p, own, :] = pot[p]
        mark = lab[p].astype(jnp.float32)
        part = 0.3 * rough[p]
        PH[0, 1 + p, own, :] = mark * (1.0 - part) + (1.0 - mark) * part

    plane_shape = UE.shape[3:]

    @pl.when(g == 0)
    def _():
        for level in range(4):
            for f in range(4):
                UE[level, f, 0] = jnp.zeros(plane_shape, jnp.float32)
            RCU[level, 2] = jnp.zeros(RCU.shape[2:], jnp.float32)
        PH[0, 0] = jnp.ones(plane_shape, jnp.float32)

    @pl.when(g == ng - 1)
    def _():
        for level in range(LEVELS):
            for f in range(4):
                value = 1.0 if f == 3 else 0.0
                for p in (5, 6):
                    UE[level, f, p] = jnp.full(plane_shape, value, jnp.float32)
            CE[level, :, :, 4] = jnp.zeros((2, 3, 16, LANES), jnp.float32)
            for side in range(2):
                RCU[level, 1, side, 0 : 3 * slab] = jnp.zeros((3 * slab, LANES), jnp.float32)
                RCU[level, 1, side, 3 * slab : pairs] = jnp.ones((slab, LANES), jnp.float32)
        PH[0, 5] = jnp.zeros(plane_shape, jnp.float32)
        for p in range(5, 10):
            PH[1, p] = jnp.zeros(plane_shape, jnp.float32)
        RCP[1, 1] = jnp.zeros(RCP.shape[2:], jnp.float32)

    @pl.when(g == ng - 2)
    def _():
        PH[1, 9] = jnp.zeros(plane_shape, jnp.float32)

    lane = lax.broadcasted_iota(jnp.int32, (CHUNK, LANES), 1)
    lane_row = lax.broadcasted_iota(jnp.int32, (1, LANES), 1)
    chunks = [(TOP + start, start) for start in range(0, rows, CHUNK)]

    def pack(planes):
        for at, start in chunks:
            tile = None
            for k, (ref, index) in enumerate(planes):
                moved = pltpu.roll(ref[index + (pl.ds(at, CHUNK), slice(None))], 2 * k + 1, 1)
                tile = moved if tile is None else jnp.where(lane // 2 == k, moved, tile)
            TS[pl.ds(start, CHUNK), :] = tile
        TT[...] = jnp.transpose(TS[...])

    def send_level(level, slide):
        pack([(UE, (level, f, 1 + p)) for f in range(4) for p in range(slab)])
        SCU[level, 1] = TT[pl.ds(0, pairs, stride=2), :]
        SCU[level, 0] = TT[pl.ds(1, pairs, stride=2), :]
        edge = ((-1, TOP, high), (1, TOP + rows - 1, low))
        flat, far = [], []

        def row(dy, fields, here, there, dg):
            (_, src, dst) = edge[0] if dy < 0 else edge[1]
            return wires.send(
                UE.at[level, fields, here, pl.ds(src, 1)],
                UE.at[level, fields, there, pl.ds(dst, 1)],
                dg, dy, 0,
            )

        def corner(dy, dz, here, there, dg):
            src, dst = (TOP, TOP) if dy < 0 else (TOP + rows - 1, TOP - 1)
            return wires.send(
                UE.at[level, pl.ds(0, 3), here, pl.ds(src, 1)],
                CE.at[level, 0 if dz > 0 else 1, :, there, pl.ds(dst, 1)],
                dg, dy, dz,
            )

        def column(dz, slot, dg):
            return wires.send(
                SCU.at[level, 0 if dz < 0 else 1],
                RCU.at[level, slot, 1 if dz < 0 else 0],
                dg, 0, dz,
            )

        every = pl.ds(0, 4)
        mine = pl.ds(1, slab)
        for dz in (-1, 1):
            flat.append(column(dz, 0, 0))
        for dy in (-1, 1):
            flat.append(row(dy, every, mine, mine, 0))
            for dz in (-1, 1):
                flat.append(corner(dy, dz, mine, pl.ds(0, slab), 0))
        if slide:
            two = pl.ds(1, 2), pl.ds(5, 2)
            for dz in (-1, 1):
                far.append(column(dz, 1, -1))
            for dy in (-1, 1):
                far.append(row(dy, every, *two, -1))
                for dz in (-1, 1):
                    far.append(corner(dy, dz, pl.ds(1, 1), pl.ds(4, 1), -1))
            far.append(
                wires.send(
                    UE.at[level, :, pl.ds(1, 2), pl.ds(TOP, rows)],
                    UE.at[level, :, pl.ds(5, 2), pl.ds(TOP, rows)],
                    -1, 0, 0,
                )
            )
        else:
            for dg, here, there, slot in ((-1, 1, 5, 1), (1, 4, 0, 2)):
                for dz in (-1, 1):
                    far.append(column(dz, slot, dg))
                for dy in (-1, 1):
                    far.append(row(dy, pl.ds(0, 2), pl.ds(here, 1), pl.ds(there, 1), dg))
            for dg, here, there in ((-1, 1, 5), (1, 4, 0)):
                far.append(
                    wires.send(
                        UE.at[level, :, pl.ds(here, 1), pl.ds(TOP, rows)],
                        UE.at[level, :, pl.ds(there, 1), pl.ds(TOP, rows)],
                        dg, 0, 0,
                    )
                )
        return flat, far

    def unpack(level, slots):
        for slot in slots:
            TS[pl.ds(32 * slot, pairs, stride=2), :] = RCU[level, slot, 1]
            TS[pl.ds(32 * slot + 1, pairs, stride=2), :] = RCU[level, slot, 0]
        HT[...] = jnp.transpose(TS[...])

    def pair_lane(f, p):
        if 1 <= p <= slab:
            return 2 * (f * slab + p - 1)
        if p > slab:
            return 32 + 2 * (f * slab + p - 5)
        return 64 + 2 * (f * slab + slab - 1)

    def sides(values, halo_ref, start, at_lane):
        halo = pltpu.roll(halo_ref[pl.ds(start, CHUNK), :], (2 * LANES - at_lane - 1) % LANES, 1)
        behind = jnp.where(lane == 0, halo, pltpu.roll(values, 1, 1))
        ahead = jnp.where(lane == LANES - 1, halo, pltpu.roll(values, LANES - 1, 1))
        return behind, ahead

    def lateral(level, f, p, centre, slope):
        for at, start in chunks:
            values = UE[level, f, p, pl.ds(at, CHUNK), :]
            behind, ahead = sides(values, HT, start, pair_lane(f, p))
            if f == 3:
                PZP[p, pl.ds(start, CHUNK), :] = ahead
                PZM[p, pl.ds(start, CHUNK), :] = behind
            else:
                if slope:
                    ZB[f, p, pl.ds(at, CHUNK), :] = ahead - behind
                if centre:
                    SB[f, p, pl.ds(start, CHUNK), :] = ahead + behind

    def lateral_row(level, f, p, at, corner_at):
        values = UE[level, f, p, pl.ds(at, 1), :]
        left = CE[level, 0, f, p - 1, pl.ds(corner_at, 1), :]
        right = CE[level, 1, f, p - 1, pl.ds(corner_at, 1), :]
        behind = jnp.where(lane_row == 0, pltpu.roll(left, 1, 1), pltpu.roll(values, 1, 1))
        ahead = jnp.where(
            lane_row == LANES - 1,
            pltpu.roll(right, LANES - 1, 1),
            pltpu.roll(values, LANES - 1, 1),
        )
        ZB[f, p, pl.ds(at, 1), :] = ahead - behind

    def sweep(level, base, hbase, offset):
        for p in range(base - 1, base + slab + 1):
            centre = base <= p < base + slab
            lateral(level, 0, p, centre, True)
            lateral(level, 2, p, centre, True)
            if centre:
                lateral(level, 1, p, True, True)
                lateral(level, 3, p, True, False)
                for f in (1, 2):
                    lateral_row(level, f, p, low, TOP - 1)
                    lateral_row(level, f, p, high, TOP)

        @pl.loop(0, slab)
        def _(j):
            p = base + j
            hp = hbase + j
            beyond = g * slab + offset + j >= ng * slab
            for at, start in chunks:
                here = pl.ds(at, CHUNK)
                above, below = pl.ds(at + 1, CHUNK), pl.ds(at - 1, CHUNK)
                flat = pl.ds(start, CHUNK)
                ux, uy, uz = (UE[level, c, p, here, :] for c in range(3))
                pair_x = [UE[level, c, p + 1, here, :] + UE[level, c, p - 1, here, :] for c in range(3)]
                pair_y = [UE[level, c, p, above, :] + UE[level, c, p, below, :] for c in range(3)]
                pair_z = [SB[c, p, flat, :] for c in range(3)]

                def divided_yz(q, hq):
                    return (
                        UE[level, 1, q, above, :] - UE[level, 1, q, below, :]
                        + ZB[2, q, here, :] - HH[hq, here, :]
                    )

                def divided_xz(at_rows):
                    return (
                        UE[level, 0, p + 1, at_rows, :] - UE[level, 0, p - 1, at_rows, :]
                        + ZB[2, p, at_rows, :] - HH[hp, at_rows, :]
                    )

                cross_x = divided_yz(p + 1, hp + 1) - divided_yz(p - 1, hp - 1)
                cross_y = divided_xz(above) - divided_xz(below)
                cross_z = (
                    ZB[0, p + 1, here, :] - ZB[0, p - 1, here, :]
                    + ZB[1, p, above, :] - ZB[1, p, below, :]
                    - GZ[hp, flat, :]
                )
                new_x = 0.12 * ux + 0.28 * pair_x[0] + 0.08 * (pair_y[0] + pair_z[0]) + 0.05 * cross_x
                new_y = 0.12 * uy + 0.28 * pair_y[1] + 0.08 * (pair_x[1] + pair_z[1]) + 0.05 * cross_y
                new_z = 0.12 * uz + 0.28 * pair_z[2] + 0.08 * (pair_x[2] + pair_y[2]) + 0.05 * cross_z
                v = UE[level, 3, p, here, :]
                c = CC[hp, here, :]
                flux = CZP[hp, flat, :] * (PZP[p, flat, :] - v) + CZM[hp, flat, :] * (PZM[p, flat, :] - v)
                for q, hq, r in ((p + 1, hp + 1, here), (p - 1, hp - 1, here), (p, hp, above), (p, hp, below)):
                    flux = flux + (CC[hq, r, :] + c) * (UE[level, 3, q, r, :] - v)
                new_v = v + flux
                if offset:
                    new_x = jnp.where(beyond, 0.0, new_x)
                    new_y = jnp.where(beyond, 0.0, new_y)
                    new_z = jnp.where(beyond, 0.0, new_z)
                    new_v = jnp.where(beyond, 1.0, new_v)
                for f, value in enumerate((new_x, new_y, new_z, new_v)):
                    UE[level + 1, f, 1 + j, here, :] = value

    def h_of(phase):
        return phase * phase * (3.0 - 2.0 * phase)

    def send_phase(step):
        pack([(PH, (step, 1 + p)) for p in range(slab)])
        SCP[step, 1, 0:slab] = TT[pl.ds(0, slab, stride=2), :]
        SCP[step, 0, 0:slab] = TT[pl.ds(1, slab, stride=2), :]
        flat, far = [], []
        slots = ((0, flat, 0), (-1, far, slab)) if step else ((0, flat, 0),)
        for dg, messages, move in slots:
            for dz in (-1, 1):
                messages.append(
                    wires.send(
                        SCP.at[step, 0 if dz < 0 else 1, pl.ds(0, slab)],
                        RCP.at[step, -dg, 1 if dz < 0 else 0, pl.ds(0, slab)],
                        dg, 0, dz,
                    )
                )
            for dy, src, dst in ((-1, TOP, high), (1, TOP + rows - 1, low)):
                messages.append(
                    wires.send(
                        PH.at[step, pl.ds(1, slab), pl.ds(src, 1)],
                        PH.at[step, pl.ds(1 + move, slab), pl.ds(dst, 1)],
                        dg, dy, 0,
                    )
                )
        planes = ((-1, 1, 5, slab), (-2, 1, 9, 1)) if step else ((-1, 1, 5, 1), (1, 4, 0, 1))
        for dg, src, dst, count in planes:
            far.append(
                wires.send(
                    PH.at[step, pl.ds(src, count), pl.ds(TOP, rows)],
                    PH.at[step, pl.ds(dst, count), pl.ds(TOP, rows)],
                    dg, 0, 0,
                )
            )
        return flat, far

    def derive(step, centres, beside):
        slots = (0, 1) if step else (0,)
        for slot in slots:
            TS[pl.ds(8 * slot, slab, stride=2), :] = RCP[step, slot, 1, 0:slab]
            TS[pl.ds(8 * slot + 1, slab, stride=2), :] = RCP[step, slot, 0, 0:slab]
        HT[...] = jnp.transpose(TS[...])
        for p in sorted(centres + beside):
            for at, start in chunks:
                phase = PH[step, p, pl.ds(at, CHUNK), :]
                h = h_of(phase)
                c = 0.0075 + 0.0675 * h
                HH[p, pl.ds(at, CHUNK), :] = 0.52 * h
                CC[p, pl.ds(at, CHUNK), :] = c
                if p in centres:
                    behind, ahead = sides(phase, HT, start, 2 * (p - 1))
                    h_behind, h_ahead = h_of(behind), h_of(ahead)
                    flat = pl.ds(start, CHUNK)
                    GZ[p, flat, :] = 0.52 * (h_ahead - h_behind)
                    CZP[p, flat, :] = c + (0.0075 + 0.0675 * h_ahead)
                    CZM[p, flat, :] = c + (0.0075 + 0.0675 * h_behind)
                    PZ[p, flat, :] = ahead + behind
            if p in centres:
                for at in (low, high):
                    h = h_of(PH[step, p, pl.ds(at, 1), :])
                    HH[p, pl.ds(at, 1), :] = 0.52 * h
                    CC[p, pl.ds(at, 1), :] = 0.0075 + 0.0675 * h

    def phase_update(step, level, base, hbase, offset, store):
        @pl.loop(0, slab)
        def _(j):
            p = base + j
            hp = hbase + j
            beyond = g * slab + offset + j >= ng * slab
            for at, start in chunks:
                here = pl.ds(at, CHUNK)
                above, below = pl.ds(at + 1, CHUNK), pl.ds(at - 1, CHUNK)
                flat = pl.ds(start, CHUNK)
                twice = (
                    UE[level, 0, p + 1, here, :] - UE[level, 0, p - 1, here, :]
                    + UE[level, 1, p, above, :] - UE[level, 1, p, below, :]
                    + ZB[2, p, here, :]
                )
                over = UE[level, 3, p, here, :] - 0.5 + 0.325 * twice - 0.375 * HH[hp, here, :]
                drive = jnp.exp(over) - jnp.exp(-over)
                phase = PH[step, hp, here, :]
                around = (
                    PH[step, hp + 1, here, :] + PH[step, hp - 1, here, :]
                    + PH[step, hp, above, :] + PH[step, hp, below, :]
                    + PZ[hp, flat, :] - 6.0 * phase
                )
                well = phase * (1.0 - phase)
                change = around - well * (2.0 * (1.0 - 2.0 * phase) + 3.0 * drive)
                value = phase + 0.05 * change
                if offset:
                    value = jnp.where(beyond, 0.0, value)
                store(j, at, start, value)

    count = len([p for p in partners if p[0] == 0])
    total = count + sum(
        9 * jnp.where(ok, 1, 0) for ok in (g > 0, g < ng - 1)
    ) + sum(jnp.where(ok, 1, 0) for ok in (g > 1, g < ng - 2))
    pl.semaphore_wait(barrier, total)

    phase_flat, phase_far = send_phase(0)
    flat, far = send_level(0, False)
    wires.receive(phase_flat)
    wires.receive(phase_far)
    derive(0, [1, 2, 3, 4], [0, 5])
    for level in range(3):
        wires.receive(flat)
        wires.receive(far)
        unpack(level, (0, 1, 2))
        sweep(level, 1, 1, 0)
        if level < 2:
            flat, far = send_level(level + 1, False)

    up = [
        wires.send(
            UE.at[3, 0, 4, pl.ds(TOP, rows)],
            UE.at[3, 0, 0, pl.ds(TOP, rows)],
            1, 0, 0,
        )
    ]
    flat, far = send_level(3, True)
    wires.receive(up)
    wires.receive(flat)
    wires.receive(far)
    unpack(3, (0, 1))
    for p in range(1, 5):
        lateral(3, 2, p, False, True)

    def keep(j, at, start, value):
        PH[1, 1 + j, pl.ds(at, CHUNK), :] = value

    phase_update(0, 3, 1, 1, 0, keep)

    phase_flat, phase_far = send_phase(1)
    wires.receive(phase_flat)
    wires.receive(phase_far)
    derive(1, [2, 3, 4, 5, 6, 7, 8], [1, 9])
    for level in (3, 4, 5):
        if level > 3:
            wires.receive(flat)
            wires.receive(far)
        unpack(level, (0, 1))
        sweep(level, 2, level - 1, level - 2)
        if level < 5:
            flat, far = send_level(level + 1, True)

    flat, far = send_level(6, True)
    wires.receive(flat)
    wires.receive(far)
    unpack(6, (0, 1))
    for p in range(2, 6):
        lateral(6, 2, p, False, True)

    def finish(j, at, start, value):
        ph_out[j, pl.ds(start, CHUNK), :] = value

    phase_update(1, 6, 2, 5, 4, finish)
    for p in range(slab):
        pot_out[p] = UE[6, 3, 2 + p, own, :]
        for c in range(3):
            u_out[c, p] = UE[6, c, 2 + p, own, :]
    wires.drain()


def solution(mesh):
    ng, ny, nz = (mesh.shape[a] for a in ("grow", "cy", "cz"))

    def shards(labels, roughness, potential, displacement):
        slab, rows, lanes = labels.shape
        tall = rows + 2 * TOP
        f32 = jnp.float32
        vmem = pl.BlockSpec(memory_space=pltpu.VMEM)
        scratch = [
            (LEVELS, 4, slab + 3, tall, lanes),
            (LEVELS, 2, 3, slab + 1, 16, lanes),
            (LEVELS, 3, 2, 4 * slab, lanes),
            (LEVELS, 2, 4 * slab, lanes),
            (2, 10, tall, lanes),
            (2, 2, 2, 8, lanes),
            (2, 2, 8, lanes),
            (10, tall, lanes),
            (10, tall, lanes),
            (10, rows, lanes),
            (10, rows, lanes),
            (10, rows, lanes),
            (10, rows, lanes),
            (3, slab + 3, tall, lanes),
            (3, slab + 3, rows, lanes),
            (slab + 3, rows, lanes),
            (slab + 3, rows, lanes),
            (lanes, lanes),
            (lanes, lanes),
            (lanes, lanes),
        ]
        return pl.pallas_call(
            functools.partial(kernel, ng, ny, nz),
            out_shape=(
                jax.ShapeDtypeStruct(labels.shape, f32),
                jax.ShapeDtypeStruct(labels.shape, f32),
                jax.ShapeDtypeStruct(displacement.shape, f32),
            ),
            in_specs=[vmem] * 4,
            out_specs=(vmem,) * 3,
            scratch_shapes=[pltpu.VMEM(shape, f32) for shape in scratch]
            + [
                pltpu.SemaphoreType.DMA((COPIES,)),
                pltpu.SemaphoreType.DMA((COPIES,)),
            ],
            compiler_params=pltpu.CompilerParams(
                collective_id=0,
                has_side_effects=True,
                vmem_limit_bytes=60 * 1024 * 1024,
            ),
            name="filament",
        )(labels, roughness, potential, displacement)

    placed = P("grow", "cy", "cz")
    vector = P(None, "grow", "cy", "cz")
    return jax.shard_map(
        shards,
        mesh=mesh,
        in_specs=(placed, placed, placed, vector),
        out_specs=(placed, placed, vector),
        check_vma=False,
    )
```

```python
import functools

import jax
import jax.numpy as jnp
from jax import lax
from jax.experimental import pallas as pl
from jax.experimental.pallas import tpu as pltpu
from jax.sharding import PartitionSpec as P

MESH = pl.DeviceIdType.MESH
LANES = 128
TOP = 8
CHUNK = 32
LEVELS = 7
COPIES = 134


class Wires:
    def __init__(self, send_sem, recv_sem, place):
        self.send_sem, self.recv_sem = send_sem, recv_sem
        self.g, self.y, self.z, self.ng, self.ny, self.nz = place
        self.count = 0
        self.pending = []

    def send(self, src, dst, dg, dy, dz):
        index = self.count
        self.count += 1
        target = (
            self.g + dg,
            lax.rem(self.y + dy + self.ny, self.ny),
            lax.rem(self.z + dz + self.nz, self.nz),
        )
        copy = pltpu.make_async_remote_copy(
            src_ref=src,
            dst_ref=dst,
            send_sem=self.send_sem.at[index],
            recv_sem=self.recv_sem.at[index],
            device_id=target,
            device_id_type=MESH,
        )
        self.when_valid(dg, copy.start)
        self.pending.append((dg, copy))
        return (dg, copy)

    def when_valid(self, dg, action):
        if dg == 0:
            action()
        else:
            ok = self.g + dg >= 0 if dg < 0 else self.g + dg < self.ng
            pl.when(ok)(action)

    def receive(self, messages):
        for dg, copy in messages:
            self.when_valid(-dg, copy.wait_recv)

    def drain(self):
        for dg, copy in self.pending:
            self.when_valid(dg, copy.wait_send)


def kernel(
    ng, ny, nz,
    lab, rough, pot, disp,
    out,
    UE, CE, RCU, SCU, PH, RCP, SCP,
    HH, CC, GZ, CZP, CZM, PZ, ZB, SB, PZP, PZM, TS, TT, HT, HP,
    send_sem, recv_sem, load_sem,
):
    g, y, z = lax.axis_index("grow"), lax.axis_index("cy"), lax.axis_index("cz")
    wires = Wires(send_sem, recv_sem, (g, y, z, ng, ny, nz))
    slab = lab.shape[0]
    rows = lab.shape[1]
    low, high = TOP - 1, TOP + rows
    own = pl.ds(TOP, rows)
    pairs = 4 * slab
    f32 = jnp.float32

    barrier = pltpu.get_barrier_semaphore()
    around = [(a, b) for a in (-1, 0, 1) for b in (-1, 0, 1)]
    partners = [(0, a, b) for a, b in around if (a, b) != (0, 0)]
    partners += [(s, a, b) for s in (-1, 1) for a, b in around]
    partners += [(-2, 0, 0), (2, 0, 0)]
    for dg, dy, dz in partners:
        def greet(dg=dg, dy=dy, dz=dz):
            pl.semaphore_signal(
                barrier,
                inc=1,
                device_id=(
                    g + dg,
                    lax.rem(y + dy + ny, ny),
                    lax.rem(z + dz + nz, nz),
                ),
                device_id_type=MESH,
            )
        wires.when_valid(dg, greet)

    loads = [
        pltpu.make_async_copy(
            disp, UE.at[0, pl.ds(0, 3), pl.ds(1, slab), own], load_sem.at[0]
        ),
        pltpu.make_async_copy(pot, UE.at[0, 3, pl.ds(1, slab), own], load_sem.at[1]),
    ]
    for load in loads:
        load.start()
    for p in range(slab):
        mark = lab[p].astype(f32)
        part = 0.3 * rough[p]
        PH[0, 1 + p, own, :] = mark * (1.0 - part) + (1.0 - mark) * part

    plane_shape = UE.shape[3:]

    def pin_outside():
        @pl.when(g == 0)
        def _():
            for level in range(4):
                for f in range(4):
                    UE[level, f, 0] = jnp.zeros(plane_shape, f32)
                RCU[level, 2] = jnp.zeros(RCU.shape[2:], f32)
            PH[0, 0] = jnp.ones(plane_shape, f32)

        @pl.when(g == ng - 1)
        def _():
            is_pot = lax.broadcasted_iota(jnp.int32, (pairs, LANES), 0) % 4 == 3
            for level in range(LEVELS):
                for f in range(4):
                    for p in (5, 6):
                        UE[level, f, p] = jnp.full(plane_shape, 1.0 if f == 3 else 0.0, f32)
                CE[level, :, :, 4] = jnp.zeros((2, 3, 16, LANES), f32)
                for side in range(2):
                    RCU[level, 1, side] = jnp.where(is_pot, 1.0, 0.0)
            PH[0, 5] = jnp.zeros(plane_shape, f32)
            for p in range(5, 10):
                PH[1, p] = jnp.zeros(plane_shape, f32)
            RCP[1, 1] = jnp.zeros(RCP.shape[2:], f32)

        @pl.when(g == ng - 2)
        def _():
            PH[1, 9] = jnp.zeros(plane_shape, f32)

    lane = lax.broadcasted_iota(jnp.int32, (CHUNK, LANES), 1)
    lane_row = lax.broadcasted_iota(jnp.int32, (1, LANES), 1)
    chunks = [(TOP + start, start) for start in range(0, rows, CHUNK)]

    def pack(planes):
        for at, start in chunks:
            tile = None
            for k, ref, index in planes:
                moved = pltpu.roll(ref[index + (pl.ds(at, CHUNK), slice(None))], 2 * k + 1, 1)
                tile = moved if tile is None else jnp.where(lane // 2 == k, moved, tile)
            TS[pl.ds(start, CHUNK), :] = tile
        TT[...] = jnp.transpose(TS[...])

    def pack_level(level, planes):
        pack([(4 * (p - 1) + f, UE, (level, f, p)) for p in planes for f in range(4)])
        for p in planes:
            first = 4 * (p - 1)
            for side in (0, 1):
                SCU[level, side, pl.ds(first, 4)] = TT[pl.ds(2 * first + 1 - side, 4, stride=2), :]

    def row(level, dy, fields, here, there, dg):
        src, dst = (TOP, high) if dy < 0 else (TOP + rows - 1, low)
        return wires.send(
            UE.at[level, fields, here, pl.ds(src, 1)],
            UE.at[level, fields, there, pl.ds(dst, 1)],
            dg, dy, 0,
        )

    def corner(level, dy, dz, here, there, dg):
        src, dst = (TOP, TOP) if dy < 0 else (TOP + rows - 1, TOP - 1)
        return wires.send(
            UE.at[level, pl.ds(0, 3), here, pl.ds(src, 1)],
            CE.at[level, 0 if dz > 0 else 1, :, there, pl.ds(dst, 1)],
            dg, dy, dz,
        )

    def column(level, dz, slot, which, dg):
        return wires.send(
            SCU.at[level, 0 if dz < 0 else 1, which],
            RCU.at[level, slot, 1 if dz < 0 else 0, which],
            dg, 0, dz,
        )

    def planes(level, fields, here, there, dg):
        return wires.send(
            UE.at[level, fields, here, own], UE.at[level, fields, there, own], dg, 0, 0
        )

    every, mine = pl.ds(0, 4), pl.ds(1, slab)

    def send_flat(level, corners=True):
        sent = [column(level, dz, 0, pl.ds(0, pairs), 0) for dz in (-1, 1)]
        for dy in (-1, 1):
            sent.append(row(level, dy, every if corners else pl.ds(1, 1), mine, mine, 0))
            if corners:
                for dz in (-1, 1):
                    sent.append(corner(level, dy, dz, mine, pl.ds(0, slab), 0))
        return sent

    def send_both_ways(level):
        sent = []
        for dg, here, there, slot in ((-1, 1, 5, 1), (1, 4, 0, 2)):
            for dz in (-1, 1):
                sent.append(column(level, dz, slot, pl.ds(4 * (here - 1), 4), dg))
            for dy in (-1, 1):
                sent.append(row(level, dy, pl.ds(0, 2), pl.ds(here, 1), pl.ds(there, 1), dg))
        for dg, here, there in ((-1, 1, 5), (1, 4, 0)):
            sent.append(planes(level, every, pl.ds(here, 1), pl.ds(there, 1), dg))
        return sent

    def send_rims_back(level):
        two = pl.ds(1, 2), pl.ds(5, 2)
        sent = [column(level, dz, 1, pl.ds(0, 8), -1) for dz in (-1, 1)]
        for dy in (-1, 1):
            sent.append(row(level, dy, every, *two, -1))
            for dz in (-1, 1):
                sent.append(corner(level, dy, dz, pl.ds(1, 1), pl.ds(4, 1), -1))
        return sent

    def send_planes_back(level):
        return [planes(level, every, pl.ds(1, 2), pl.ds(5, 2), -1)]

    def unpack(level, slot, count):
        first, size = count
        TS[pl.ds(2 * first, size, stride=2), :] = RCU[level, slot, 1, pl.ds(first, size)]
        TS[pl.ds(2 * first + 1, size, stride=2), :] = RCU[level, slot, 0, pl.ds(first, size)]
        HT[slot] = jnp.transpose(TS[...])

    def halo_lane(f, p):
        if p == 0:
            return 2, 2 * (pairs - 4 + f)
        if p <= slab:
            return 0, 2 * (4 * (p - 1) + f)
        return 1, 2 * (4 * (p - 5) + f)

    def sides(values, halo, at_lane):
        halo = pltpu.roll(halo, (2 * LANES - at_lane - 1) % LANES, 1)
        behind = jnp.where(lane == 0, halo, pltpu.roll(values, 1, 1))
        ahead = jnp.where(lane == LANES - 1, halo, pltpu.roll(values, LANES - 1, 1))
        return behind, ahead

    def lateral(level, f, p, centre):
        slot, at_lane = halo_lane(f, p)
        for at, start in chunks:
            flat = pl.ds(start, CHUNK)
            values = UE[level, f, p, pl.ds(at, CHUNK), :]
            behind, ahead = sides(values, HT[slot, flat, :], at_lane)
            if f == 3:
                PZP[p, flat, :] = ahead
                PZM[p, flat, :] = behind
            else:
                ZB[f, p, pl.ds(at, CHUNK), :] = ahead - behind
                if centre:
                    SB[f, p, flat, :] = ahead + behind

    def lateral_row(level, f, p, at, corner_at):
        values = UE[level, f, p, pl.ds(at, 1), :]
        left = CE[level, 0, f, p - 1, pl.ds(corner_at, 1), :]
        right = CE[level, 1, f, p - 1, pl.ds(corner_at, 1), :]
        behind = jnp.where(lane_row == 0, pltpu.roll(left, 1, 1), pltpu.roll(values, 1, 1))
        ahead = jnp.where(
            lane_row == LANES - 1,
            pltpu.roll(right, LANES - 1, 1),
            pltpu.roll(values, LANES - 1, 1),
        )
        ZB[f, p, pl.ds(at, 1), :] = ahead - behind

    ready = set()

    def once(*key):
        fresh = key not in ready
        ready.add(key)
        return fresh

    def sweep(level, base, hbase, offset, js):
        inside = range(base, base + slab)
        for p in range(min(js) + base - 1, max(js) + base + 2):
            centre = p - base in js
            wanted = (0, 1, 2, 3) if centre else (0, 2)
            if not centre and p - 1 - base not in js and p + 1 - base not in js:
                continue
            for f in wanted:
                if once("side", level, f, p):
                    lateral(level, f, p, p in inside)
            if centre:
                for f in (1, 2):
                    lateral_row(level, f, p, low, TOP - 1)
                    lateral_row(level, f, p, high, TOP)

        @pl.loop(0, len(js))
        def _(i):
            j = js[0] + i * (js[1] - js[0])
            p = base + j
            hp = hbase + j
            beyond = g * slab + offset + j >= ng * slab
            for at, start in chunks:
                here = pl.ds(at, CHUNK)
                above, below = pl.ds(at + 1, CHUNK), pl.ds(at - 1, CHUNK)
                flat = pl.ds(start, CHUNK)
                ux, uy, uz = (UE[level, c, p, here, :] for c in range(3))
                pair_x = [UE[level, c, p + 1, here, :] + UE[level, c, p - 1, here, :] for c in range(3)]
                pair_y = [UE[level, c, p, above, :] + UE[level, c, p, below, :] for c in range(3)]
                pair_z = [SB[c, p, flat, :] for c in range(3)]

                def divided_yz(q, hq):
                    return (
                        UE[level, 1, q, above, :] - UE[level, 1, q, below, :]
                        + ZB[2, q, here, :] - HH[hq, here, :]
                    )

                def divided_xz(at_rows):
                    return (
                        UE[level, 0, p + 1, at_rows, :] - UE[level, 0, p - 1, at_rows, :]
                        + ZB[2, p, at_rows, :] - HH[hp, at_rows, :]
                    )

                cross_x = divided_yz(p + 1, hp + 1) - divided_yz(p - 1, hp - 1)
                cross_y = divided_xz(above) - divided_xz(below)
                cross_z = (
                    ZB[0, p + 1, here, :] - ZB[0, p - 1, here, :]
                    + ZB[1, p, above, :] - ZB[1, p, below, :]
                    - GZ[hp, flat, :]
                )
                new_x = 0.12 * ux + 0.28 * pair_x[0] + 0.08 * (pair_y[0] + pair_z[0]) + 0.05 * cross_x
                new_y = 0.12 * uy + 0.28 * pair_y[1] + 0.08 * (pair_x[1] + pair_z[1]) + 0.05 * cross_y
                new_z = 0.12 * uz + 0.28 * pair_z[2] + 0.08 * (pair_x[2] + pair_y[2]) + 0.05 * cross_z
                v = UE[level, 3, p, here, :]
                c = CC[hp, here, :]
                flux = CZP[hp, flat, :] * (PZP[p, flat, :] - v) + CZM[hp, flat, :] * (PZM[p, flat, :] - v)
                for q, hq, r in ((p + 1, hp + 1, here), (p - 1, hp - 1, here), (p, hp, above), (p, hp, below)):
                    flux = flux + (CC[hq, r, :] + c) * (UE[level, 3, q, r, :] - v)
                new_v = v + flux
                if offset:
                    new_x = jnp.where(beyond, 0.0, new_x)
                    new_y = jnp.where(beyond, 0.0, new_y)
                    new_z = jnp.where(beyond, 0.0, new_z)
                    new_v = jnp.where(beyond, 1.0, new_v)
                for f, value in enumerate((new_x, new_y, new_z, new_v)):
                    UE[level + 1, f, 1 + j, here, :] = value

    def h_of(phase):
        return phase * phase * (3.0 - 2.0 * phase)

    def pack_phase(step):
        pack([(p, PH, (step, 1 + p)) for p in range(slab)])
        SCP[step, 1] = TT[pl.ds(0, slab, stride=2), :]
        SCP[step, 0] = TT[pl.ds(1, slab, stride=2), :]

    def send_phase_rims(step, dg):
        sent = []
        for dz in (-1, 1):
            sent.append(
                wires.send(
                    SCP.at[step, 0 if dz < 0 else 1],
                    RCP.at[step, -dg, 1 if dz < 0 else 0],
                    dg, 0, dz,
                )
            )
        for dy, src, dst in ((-1, TOP, high), (1, TOP + rows - 1, low)):
            sent.append(
                wires.send(
                    PH.at[step, pl.ds(1, slab), pl.ds(src, 1)],
                    PH.at[step, pl.ds(1 - dg * slab, slab), pl.ds(dst, 1)],
                    dg, dy, 0,
                )
            )
        return sent

    def send_phase_planes(step, moves):
        return [
            wires.send(
                PH.at[step, pl.ds(src, count), own], PH.at[step, pl.ds(dst, count), own], dg, 0, 0
            )
            for dg, src, dst, count in moves
        ]

    def unpack_phase(step, slot):
        TS[pl.ds(0, slab, stride=2), :] = RCP[step, slot, 1]
        TS[pl.ds(1, slab, stride=2), :] = RCP[step, slot, 0]
        HP[slot] = jnp.transpose(TS[...])

    def derive(step, p, centre):
        slot = 0 if p <= slab else 1
        for at, start in chunks:
            flat = pl.ds(start, CHUNK)
            phase = PH[step, p, pl.ds(at, CHUNK), :]
            h = h_of(phase)
            c = 0.0075 + 0.0675 * h
            HH[p, pl.ds(at, CHUNK), :] = 0.52 * h
            CC[p, pl.ds(at, CHUNK), :] = c
            if centre:
                behind, ahead = sides(phase, HP[slot, flat, :], 2 * (p - 1 - slot * slab))
                h_behind, h_ahead = h_of(behind), h_of(ahead)
                GZ[p, flat, :] = 0.52 * (h_ahead - h_behind)
                CZP[p, flat, :] = c + (0.0075 + 0.0675 * h_ahead)
                CZM[p, flat, :] = c + (0.0075 + 0.0675 * h_behind)
                PZ[p, flat, :] = ahead + behind
        if centre:
            for at in (low, high):
                h = h_of(PH[step, p, pl.ds(at, 1), :])
                HH[p, pl.ds(at, 1), :] = 0.52 * h
                CC[p, pl.ds(at, 1), :] = 0.0075 + 0.0675 * h

    def phase_update(step, level, base, hbase, offset, js, store):
        for j in js:
            if once("side", level, 2, base + j):
                lateral(level, 2, base + j, True)

        @pl.loop(0, len(js))
        def _(i):
            j = js[0] + i * (js[1] - js[0])
            p = base + j
            hp = hbase + j
            beyond = g * slab + offset + j >= ng * slab
            for at, start in chunks:
                here = pl.ds(at, CHUNK)
                above, below = pl.ds(at + 1, CHUNK), pl.ds(at - 1, CHUNK)
                flat = pl.ds(start, CHUNK)
                twice = (
                    UE[level, 0, p + 1, here, :] - UE[level, 0, p - 1, here, :]
                    + UE[level, 1, p, above, :] - UE[level, 1, p, below, :]
                    + ZB[2, p, here, :]
                )
                over = UE[level, 3, p, here, :] - 0.5 + 0.325 * twice - 0.375 * HH[hp, here, :]
                drive = jnp.exp(over) - jnp.exp(-over)
                phase = PH[step, hp, here, :]
                nearby = (
                    PH[step, hp + 1, here, :] + PH[step, hp - 1, here, :]
                    + PH[step, hp, above, :] + PH[step, hp, below, :]
                    + PZ[hp, flat, :] - 6.0 * phase
                )
                well = phase * (1.0 - phase)
                change = nearby - well * (2.0 * (1.0 - 2.0 * phase) + 3.0 * drive)
                value = phase + 0.05 * change
                if offset:
                    value = jnp.where(beyond, 0.0, value)
                store(j, at, start, value)

    count = len([p for p in partners if p[0] == 0])
    total = count + sum(
        9 * jnp.where(ok, 1, 0) for ok in (g > 0, g < ng - 1)
    ) + sum(jnp.where(ok, 1, 0) for ok in (g > 1, g < ng - 2))
    pack_phase(0)
    for load in loads:
        load.wait()
    pack_level(0, (1, 2, 3, 4))
    pl.semaphore_wait(barrier, total)

    phase_flat = send_phase_rims(0, 0)
    flat = send_flat(0)
    phase_far = send_phase_planes(0, ((-1, 1, 5, 1), (1, 4, 0, 1)))
    far = send_both_ways(0)
    pin_outside()
    wires.receive(phase_flat)
    unpack_phase(0, 0)
    for p in (1, 2, 3, 4):
        derive(0, p, True)
    for level in range(3):
        wires.receive(flat)
        unpack(level, 0, (0, pairs))
        sweep(level, 1, 1, 0, (1, 2))
        pack_level(level + 1, (2, 3))
        if level == 0:
            wires.receive(phase_far)
            derive(0, 0, False)
            derive(0, 5, False)
        wires.receive(far)
        unpack(level, 1, (0, 4))
        unpack(level, 2, (pairs - 4, 4))
        sweep(level, 1, 1, 0, (0, 3))
        pack_level(level + 1, (1, 4))
        flat = send_flat(level + 1)
        if level < 2:
            far = send_both_ways(level + 1)

    ends = [
        planes(3, 0, 4, 0, 1),
        planes(3, 0, 1, 5, -1),
    ]
    far = send_rims_back(3)
    far.append(planes(3, pl.ds(1, 3), pl.ds(1, 2), pl.ds(5, 2), -1))
    far.append(planes(3, 0, 2, 6, -1))
    wires.receive(flat)
    unpack(3, 0, (0, pairs))

    def keep(j, at, start, value):
        PH[1, 1 + j, pl.ds(at, CHUNK), :] = value

    phase_update(0, 3, 1, 1, 0, (1, 2), keep)
    wires.receive(ends)
    phase_update(0, 3, 1, 1, 0, (0, 3), keep)
    pack_phase(1)
    phase_flat = send_phase_rims(1, 0)
    phase_far = send_phase_rims(1, -1)
    phase_far += send_phase_planes(1, ((-1, 1, 5, slab), (-2, 1, 9, 1)))

    wires.receive(phase_flat)
    unpack_phase(1, 0)
    derive(1, 1, False)
    for p in (2, 3, 4):
        derive(1, p, True)
    for level in (3, 4, 5):
        hbase, offset = level - 1, level - 2
        if level > 3:
            wires.receive(flat)
            unpack(level, 0, (0, pairs))
        sweep(level, 2, hbase, offset, (0, 1))
        pack_level(level + 1, (1, 2))
        if level < 5:
            next_far = send_rims_back(level + 1) + send_planes_back(level + 1)
        else:
            next_far = [column(6, dz, 1, pl.ds(0, 4), -1) for dz in (-1, 1)]
            for dy in (-1, 1):
                next_far.append(row(6, dy, pl.ds(1, 1), pl.ds(1, 1), pl.ds(5, 1), -1))
            next_far.append(planes(6, every, 1, 5, -1))
            next_far.append(planes(6, 0, 2, 6, -1))
        if level == 3:
            wires.receive(phase_far)
            unpack_phase(1, 1)
            for p in (5, 6, 7, 8):
                derive(1, p, True)
            derive(1, 9, False)
        wires.receive(far)
        unpack(level, 1, (0, 8))
        sweep(level, 2, hbase, offset, (2, 3))
        pack_level(level + 1, (3, 4))
        flat = send_flat(level + 1, level < 5)
        far = next_far

    def finish(j, at, start, value):
        out[0, j, pl.ds(start, CHUNK), :] = value

    def hand_over(p):
        out[1, p - 2] = UE[6, 3, p, own, :]
        for c in range(3):
            out[2 + c, p - 2] = UE[6, c, p, own, :]

    for p in range(2, 5):
        hand_over(p)
    wires.receive(flat)
    unpack(6, 0, (0, pairs))
    phase_update(1, 6, 2, 5, 4, (0, 1), finish)
    wires.receive(far)
    unpack(6, 1, (0, 4))
    hand_over(5)
    phase_update(1, 6, 2, 5, 4, (2, 3), finish)
    wires.drain()
    assert wires.count == COPIES, wires.count


def deliver(packed, phase, potential, displacement):
    phase[...] = packed[0]
    potential[...] = packed[1]
    for c in range(3):
        displacement[c] = packed[2 + c]


def solution(mesh):
    ng, ny, nz = (mesh.shape[a] for a in ("grow", "cy", "cz"))

    def shards(labels, roughness, potential, displacement):
        slab, rows, lanes = labels.shape
        tall = rows + 2 * TOP
        f32 = jnp.float32
        vmem = pl.BlockSpec(memory_space=pltpu.VMEM)
        anywhere = pl.BlockSpec(memory_space=pl.ANY)
        scratch = [
            (LEVELS, 4, slab + 3, tall, lanes),
            (LEVELS, 2, 3, slab + 1, 16, lanes),
            (LEVELS, 3, 2, 4 * slab, lanes),
            (LEVELS, 2, 4 * slab, lanes),
            (2, 10, tall, lanes),
            (2, 2, 2, slab, lanes),
            (2, 2, slab, lanes),
            (10, tall, lanes),
            (10, tall, lanes),
            (10, rows, lanes),
            (10, rows, lanes),
            (10, rows, lanes),
            (10, rows, lanes),
            (3, slab + 3, tall, lanes),
            (3, slab + 3, rows, lanes),
            (slab + 3, rows, lanes),
            (slab + 3, rows, lanes),
            (lanes, lanes),
            (lanes, lanes),
            (3, lanes, lanes),
            (2, lanes, lanes),
        ]
        packed = pl.pallas_call(
            functools.partial(kernel, ng, ny, nz),
            out_shape=jax.ShapeDtypeStruct((5,) + labels.shape, f32),
            in_specs=[vmem, vmem, anywhere, anywhere],
            out_specs=vmem,
            scratch_shapes=[pltpu.VMEM(shape, f32) for shape in scratch]
            + [
                pltpu.SemaphoreType.DMA((COPIES,)),
                pltpu.SemaphoreType.DMA((COPIES,)),
                pltpu.SemaphoreType.DMA((2,)),
            ],
            compiler_params=pltpu.CompilerParams(
                collective_id=0,
                has_side_effects=True,
                vmem_limit_bytes=40 * 1024 * 1024,
            ),
            name="filament",
        )(labels, roughness, potential, displacement)
        return pl.pallas_call(
            deliver,
            out_shape=(
                jax.ShapeDtypeStruct(labels.shape, f32),
                jax.ShapeDtypeStruct(labels.shape, f32),
                jax.ShapeDtypeStruct(displacement.shape, f32),
            ),
            in_specs=[vmem],
            out_specs=(vmem,) * 3,
            name="deliver",
        )(packed)

    placed = P("grow", "cy", "cz")
    vector = P(None, "grow", "cy", "cz")
    return jax.shard_map(
        shards,
        mesh=mesh,
        in_specs=(placed, placed, placed, vector),
        out_specs=(placed, placed, vector),
        check_vma=False,
    )
```

```python
import functools

import jax
import jax.numpy as jnp
from jax import lax
from jax.experimental import pallas as pl
from jax.experimental.pallas import tpu as pltpu
from jax.sharding import PartitionSpec as P

MESH = pl.DeviceIdType.MESH
LANES = 128
TOP = 8
CHUNK = 32
LEVELS = 7
COPIES = 175


class Wires:
    def __init__(self, send_sem, recv_sem, place):
        self.send_sem, self.recv_sem = send_sem, recv_sem
        self.g, self.y, self.z, self.ng, self.ny, self.nz = place
        self.count = 0
        self.pending = []

    def send(self, src, dst, dg, dy, dz):
        index = self.count
        self.count += 1
        target = (
            self.g + dg,
            lax.rem(self.y + dy + self.ny, self.ny),
            lax.rem(self.z + dz + self.nz, self.nz),
        )
        copy = pltpu.make_async_remote_copy(
            src_ref=src,
            dst_ref=dst,
            send_sem=self.send_sem.at[index],
            recv_sem=self.recv_sem.at[index],
            device_id=target,
            device_id_type=MESH,
        )
        self.when_valid(dg, copy.start)
        self.pending.append((dg, copy))
        return (dg, copy)

    def when_valid(self, dg, action):
        if dg == 0:
            action()
        else:
            ok = self.g + dg >= 0 if dg < 0 else self.g + dg < self.ng
            pl.when(ok)(action)

    def receive(self, messages):
        for dg, copy in messages:
            self.when_valid(-dg, copy.wait_recv)

    def drain(self):
        for dg, copy in self.pending:
            self.when_valid(dg, copy.wait_send)


def kernel(
    ng, ny, nz,
    lab, rough, pot, disp,
    out,
    UE, CE, RCU, SCU, PH, RCP, SCP,
    HH, CC, GZ, CZP, CZM, PZ, ZB, SB, PZP, PZM, TS, TT, HT, HP,
    LAB, ROU,
    send_sem, recv_sem, load_sem,
):
    g, y, z = lax.axis_index("grow"), lax.axis_index("cy"), lax.axis_index("cz")
    wires = Wires(send_sem, recv_sem, (g, y, z, ng, ny, nz))
    slab = lab.shape[0]
    rows = lab.shape[1]
    low, high = TOP - 1, TOP + rows
    own = pl.ds(TOP, rows)
    pairs = 4 * slab
    f32 = jnp.float32

    barrier = pltpu.get_barrier_semaphore()
    around = [(a, b) for a in (-1, 0, 1) for b in (-1, 0, 1)]
    partners = [(0, a, b) for a, b in around if (a, b) != (0, 0)]
    partners += [(s, a, b) for s in (-1, 1) for a, b in around]
    partners += [(-2, 0, 0), (2, 0, 0)]
    for dg, dy, dz in partners:
        def greet(dg=dg, dy=dy, dz=dz):
            pl.semaphore_signal(
                barrier,
                inc=1,
                device_id=(
                    g + dg,
                    lax.rem(y + dy + ny, ny),
                    lax.rem(z + dz + nz, nz),
                ),
                device_id_type=MESH,
            )
        wires.when_valid(dg, greet)

    loads = [
        pltpu.make_async_copy(
            disp, UE.at[0, pl.ds(0, 3), pl.ds(1, slab), own], load_sem.at[0]
        ),
        pltpu.make_async_copy(pot, UE.at[0, 3, pl.ds(1, slab), own], load_sem.at[1]),
        pltpu.make_async_copy(lab, LAB, load_sem.at[2]),
        pltpu.make_async_copy(rough, ROU, load_sem.at[3]),
    ]
    for load in loads:
        load.start()
    loads[2].wait()
    loads[3].wait()
    for p in range(slab):
        mark = LAB[p].astype(f32)
        part = 0.3 * ROU[p]
        PH[0, 1 + p, own, :] = mark * (1.0 - part) + (1.0 - mark) * part

    plane_shape = UE.shape[3:]

    def pin_outside():
        @pl.when(g == 0)
        def _():
            for level in range(4):
                for f in range(4):
                    UE[level, f, 0] = jnp.zeros(plane_shape, f32)
                RCU[level, 2] = jnp.zeros(RCU.shape[2:], f32)
            PH[0, 0] = jnp.ones(plane_shape, f32)

        @pl.when(g == ng - 1)
        def _():
            is_pot = lax.broadcasted_iota(jnp.int32, (pairs, LANES), 0) >= 3 * slab
            for level in range(LEVELS):
                for f in range(4):
                    for p in (5, 6):
                        UE[level, f, p] = jnp.full(plane_shape, 1.0 if f == 3 else 0.0, f32)
                CE[level, :, :, 4] = jnp.zeros((2, 3, 16, LANES), f32)
                for side in range(2):
                    RCU[level, 1, side] = jnp.where(is_pot, 1.0, 0.0)
            PH[0, 5] = jnp.zeros(plane_shape, f32)
            for p in range(5, 10):
                PH[1, p] = jnp.zeros(plane_shape, f32)
            RCP[1, 1] = jnp.zeros(RCP.shape[2:], f32)

        @pl.when(g == ng - 2)
        def _():
            PH[1, 9] = jnp.zeros(plane_shape, f32)

    lane = lax.broadcasted_iota(jnp.int32, (CHUNK, LANES), 1)
    lane_row = lax.broadcasted_iota(jnp.int32, (1, LANES), 1)
    chunks = [(TOP + start, start) for start in range(0, rows, CHUNK)]

    def pack(planes):
        for at, start in chunks:
            tile = None
            for k, ref, index in planes:
                moved = pltpu.roll(ref[index + (pl.ds(at, CHUNK), slice(None))], 2 * k + 1, 1)
                tile = moved if tile is None else jnp.where(lane // 2 == k, moved, tile)
            TS[pl.ds(start, CHUNK), :] = tile
        TT[...] = jnp.transpose(TS[...])

    def pair(f, q):
        return 3 * slab + q - 1 if f == 3 else 3 * (q - 1) + f

    def pack_level(level, planes, fields=(0, 1, 2, 3)):
        pack([(pair(f, q), UE, (level, f, q)) for q in planes for f in fields])
        for q in planes:
            for f in fields:
                if f in (0, 3):
                    first, size = pair(f, q), 1 if f == 3 else 3
                    for side in (0, 1):
                        SCU[level, side, pl.ds(first, size)] = TT[
                            pl.ds(2 * first + 1 - side, size, stride=2), :
                        ]

    def row(level, dy, fields, here, there, dg):
        src, dst = (TOP, high) if dy < 0 else (TOP + rows - 1, low)
        return wires.send(
            UE.at[level, fields, here, pl.ds(src, 1)],
            UE.at[level, fields, there, pl.ds(dst, 1)],
            dg, dy, 0,
        )

    def corner(level, dy, dz, here, there, dg):
        src, dst = (TOP, TOP) if dy < 0 else (TOP + rows - 1, TOP - 1)
        return wires.send(
            UE.at[level, pl.ds(0, 3), here, pl.ds(src, 1)],
            CE.at[level, 0 if dz > 0 else 1, :, there, pl.ds(dst, 1)],
            dg, dy, dz,
        )

    def column(level, dz, slot, which, dg):
        return wires.send(
            SCU.at[level, 0 if dz < 0 else 1, which],
            RCU.at[level, slot, 1 if dz < 0 else 0, which],
            dg, 0, dz,
        )

    def planes(level, fields, here, there, dg):
        return wires.send(
            UE.at[level, fields, here, own], UE.at[level, fields, there, own], dg, 0, 0
        )

    every, mine = pl.ds(0, 4), pl.ds(1, slab)
    u_fields, v_field = pl.ds(0, 3), pl.ds(3, 1)
    u_pairs, v_pairs = pl.ds(0, 3 * slab), pl.ds(3 * slab, slab)

    def send_flat_u(level):
        sent = [column(level, dz, 0, u_pairs, 0) for dz in (-1, 1)]
        for dy in (-1, 1):
            sent.append(row(level, dy, u_fields, mine, mine, 0))
            for dz in (-1, 1):
                sent.append(corner(level, dy, dz, mine, pl.ds(0, slab), 0))
        return sent

    def send_flat_v(level):
        sent = [column(level, dz, 0, v_pairs, 0) for dz in (-1, 1)]
        return sent + [row(level, dy, v_field, mine, mine, 0) for dy in (-1, 1)]

    def send_both_ways_u(level):
        sent = []
        for dg, here, there, slot in ((-1, 1, 5, 1), (1, 4, 0, 2)):
            for dz in (-1, 1):
                sent.append(column(level, dz, slot, pl.ds(3 * (here - 1), 3), dg))
            for dy in (-1, 1):
                sent.append(row(level, dy, pl.ds(0, 2), pl.ds(here, 1), pl.ds(there, 1), dg))
        for dg, here, there in ((-1, 1, 5), (1, 4, 0)):
            sent.append(planes(level, u_fields, here, there, dg))
        return sent

    def send_both_ways_v(level):
        return [planes(level, 3, here, there, dg) for dg, here, there in ((-1, 1, 5), (1, 4, 0))]

    def send_rims_back(level):
        two = pl.ds(1, 2), pl.ds(5, 2)
        sent = []
        for dz in (-1, 1):
            sent.append(column(level, dz, 1, pl.ds(0, 6), -1))
            sent.append(column(level, dz, 1, pl.ds(3 * slab, 2), -1))
        for dy in (-1, 1):
            sent.append(row(level, dy, every, *two, -1))
            for dz in (-1, 1):
                sent.append(corner(level, dy, dz, pl.ds(1, 1), pl.ds(4, 1), -1))
        return sent

    def unpack(level, slot, first, size):
        TS[pl.ds(2 * first, size, stride=2), :] = RCU[level, slot, 1, pl.ds(first, size)]
        TS[pl.ds(2 * first + 1, size, stride=2), :] = RCU[level, slot, 0, pl.ds(first, size)]
        HT[slot if first < 3 * slab else 3 + slot] = jnp.transpose(TS[...])

    def halo_lane(f, p):
        slot, q = (2, slab) if p == 0 else (0, p) if p <= slab else (1, p - slab)
        return slot + (3 if f == 3 else 0), 2 * pair(f, q)

    def sides(values, halo, at_lane):
        halo = pltpu.roll(halo, (2 * LANES - at_lane - 1) % LANES, 1)
        behind = jnp.where(lane == 0, halo, pltpu.roll(values, 1, 1))
        ahead = jnp.where(lane == LANES - 1, halo, pltpu.roll(values, LANES - 1, 1))
        return behind, ahead

    def lateral(level, f, p, centre):
        slot, at_lane = halo_lane(f, p)
        for at, start in chunks:
            flat = pl.ds(start, CHUNK)
            values = UE[level, f, p, pl.ds(at, CHUNK), :]
            behind, ahead = sides(values, HT[slot, flat, :], at_lane)
            if f == 3:
                PZP[p, flat, :] = ahead
                PZM[p, flat, :] = behind
            else:
                ZB[f, p, pl.ds(at, CHUNK), :] = ahead - behind
                if centre:
                    SB[f, p, flat, :] = ahead + behind

    def lateral_row(level, f, p, at, corner_at):
        values = UE[level, f, p, pl.ds(at, 1), :]
        left = CE[level, 0, f, p - 1, pl.ds(corner_at, 1), :]
        right = CE[level, 1, f, p - 1, pl.ds(corner_at, 1), :]
        behind = jnp.where(lane_row == 0, pltpu.roll(left, 1, 1), pltpu.roll(values, 1, 1))
        ahead = jnp.where(
            lane_row == LANES - 1,
            pltpu.roll(right, LANES - 1, 1),
            pltpu.roll(values, LANES - 1, 1),
        )
        ZB[f, p, pl.ds(at, 1), :] = ahead - behind

    ready = set()

    def once(*key):
        fresh = key not in ready
        ready.add(key)
        return fresh

    def sweep(level, base, hbase, offset, js, displace=True, relax=True):
        inside = range(base, base + slab)
        for p in range(min(js) + base - 1, max(js) + base + 2):
            centre = p - base in js
            wanted = (0, 1, 2) if centre else (0, 2)
            wanted = (wanted if displace else ()) + ((3,) if relax and centre else ())
            if not centre and p - 1 - base not in js and p + 1 - base not in js:
                continue
            for f in wanted:
                if once("side", level, f, p):
                    lateral(level, f, p, p in inside)
            if centre and displace:
                for f in (1, 2):
                    lateral_row(level, f, p, low, TOP - 1)
                    lateral_row(level, f, p, high, TOP)

        @pl.loop(0, len(js))
        def _(i):
            j = js[0] + i * (js[1] - js[0])
            p = base + j
            hp = hbase + j
            beyond = g * slab + offset + j >= ng * slab
            for at, start in chunks:
                here = pl.ds(at, CHUNK)
                above, below = pl.ds(at + 1, CHUNK), pl.ds(at - 1, CHUNK)
                flat = pl.ds(start, CHUNK)
                if displace:
                    ux, uy, uz = (UE[level, c, p, here, :] for c in range(3))
                    pair_x = [UE[level, c, p + 1, here, :] + UE[level, c, p - 1, here, :] for c in range(3)]
                    pair_y = [UE[level, c, p, above, :] + UE[level, c, p, below, :] for c in range(3)]
                    pair_z = [SB[c, p, flat, :] for c in range(3)]

                    def divided_yz(q, hq):
                        return (
                            UE[level, 1, q, above, :] - UE[level, 1, q, below, :]
                            + ZB[2, q, here, :] - HH[hq, here, :]
                        )

                    def divided_xz(at_rows):
                        return (
                            UE[level, 0, p + 1, at_rows, :] - UE[level, 0, p - 1, at_rows, :]
                            + ZB[2, p, at_rows, :] - HH[hp, at_rows, :]
                        )

                    cross_x = divided_yz(p + 1, hp + 1) - divided_yz(p - 1, hp - 1)
                    cross_y = divided_xz(above) - divided_xz(below)
                    cross_z = (
                        ZB[0, p + 1, here, :] - ZB[0, p - 1, here, :]
                        + ZB[1, p, above, :] - ZB[1, p, below, :]
                        - GZ[hp, flat, :]
                    )
                    new_x = 0.12 * ux + 0.28 * pair_x[0] + 0.08 * (pair_y[0] + pair_z[0]) + 0.05 * cross_x
                    new_y = 0.12 * uy + 0.28 * pair_y[1] + 0.08 * (pair_x[1] + pair_z[1]) + 0.05 * cross_y
                    new_z = 0.12 * uz + 0.28 * pair_z[2] + 0.08 * (pair_x[2] + pair_y[2]) + 0.05 * cross_z
                    for f, value in enumerate((new_x, new_y, new_z)):
                        if offset:
                            value = jnp.where(beyond, 0.0, value)
                        UE[level + 1, f, 1 + j, here, :] = value
                if relax:
                    v = UE[level, 3, p, here, :]
                    c = CC[hp, here, :]
                    flux = CZP[hp, flat, :] * (PZP[p, flat, :] - v) + CZM[hp, flat, :] * (PZM[p, flat, :] - v)
                    for q, hq, r in ((p + 1, hp + 1, here), (p - 1, hp - 1, here), (p, hp, above), (p, hp, below)):
                        flux = flux + (CC[hq, r, :] + c) * (UE[level, 3, q, r, :] - v)
                    new_v = v + flux
                    if offset:
                        new_v = jnp.where(beyond, 1.0, new_v)
                    UE[level + 1, 3, 1 + j, here, :] = new_v

    def h_of(phase):
        return phase * phase * (3.0 - 2.0 * phase)

    def pack_phase(step):
        pack([(p, PH, (step, 1 + p)) for p in range(slab)])
        SCP[step, 1] = TT[pl.ds(0, slab, stride=2), :]
        SCP[step, 0] = TT[pl.ds(1, slab, stride=2), :]

    def send_phase_rims(step, dg):
        sent = []
        for dz in (-1, 1):
            sent.append(
                wires.send(
                    SCP.at[step, 0 if dz < 0 else 1],
                    RCP.at[step, -dg, 1 if dz < 0 else 0],
                    dg, 0, dz,
                )
            )
        for dy, src, dst in ((-1, TOP, high), (1, TOP + rows - 1, low)):
            sent.append(
                wires.send(
                    PH.at[step, pl.ds(1, slab), pl.ds(src, 1)],
                    PH.at[step, pl.ds(1 - dg * slab, slab), pl.ds(dst, 1)],
                    dg, dy, 0,
                )
            )
        return sent

    def send_phase_planes(step, moves):
        return [
            wires.send(
                PH.at[step, pl.ds(src, count), own], PH.at[step, pl.ds(dst, count), own], dg, 0, 0
            )
            for dg, src, dst, count in moves
        ]

    def unpack_phase(step, slot):
        TS[pl.ds(0, slab, stride=2), :] = RCP[step, slot, 1]
        TS[pl.ds(1, slab, stride=2), :] = RCP[step, slot, 0]
        HP[slot] = jnp.transpose(TS[...])

    def derive(step, p, centre):
        slot = 0 if p <= slab else 1
        for at, start in chunks:
            flat = pl.ds(start, CHUNK)
            phase = PH[step, p, pl.ds(at, CHUNK), :]
            h = h_of(phase)
            c = 0.0075 + 0.0675 * h
            HH[p, pl.ds(at, CHUNK), :] = 0.52 * h
            CC[p, pl.ds(at, CHUNK), :] = c
            if centre:
                behind, ahead = sides(phase, HP[slot, flat, :], 2 * (p - 1 - slot * slab))
                h_behind, h_ahead = h_of(behind), h_of(ahead)
                GZ[p, flat, :] = 0.52 * (h_ahead - h_behind)
                CZP[p, flat, :] = c + (0.0075 + 0.0675 * h_ahead)
                CZM[p, flat, :] = c + (0.0075 + 0.0675 * h_behind)
                PZ[p, flat, :] = ahead + behind
        if centre:
            for at in (low, high):
                h = h_of(PH[step, p, pl.ds(at, 1), :])
                HH[p, pl.ds(at, 1), :] = 0.52 * h
                CC[p, pl.ds(at, 1), :] = 0.0075 + 0.0675 * h

    def phase_update(step, level, base, hbase, offset, js, store):
        for j in js:
            if once("side", level, 2, base + j):
                lateral(level, 2, base + j, True)

        @pl.loop(0, len(js))
        def _(i):
            j = js[0] + i * (js[1] - js[0])
            p = base + j
            hp = hbase + j
            beyond = g * slab + offset + j >= ng * slab
            for at, start in chunks:
                here = pl.ds(at, CHUNK)
                above, below = pl.ds(at + 1, CHUNK), pl.ds(at - 1, CHUNK)
                flat = pl.ds(start, CHUNK)
                twice = (
                    UE[level, 0, p + 1, here, :] - UE[level, 0, p - 1, here, :]
                    + UE[level, 1, p, above, :] - UE[level, 1, p, below, :]
                    + ZB[2, p, here, :]
                )
                over = UE[level, 3, p, here, :] - 0.5 + 0.325 * twice - 0.375 * HH[hp, here, :]
                drive = jnp.exp(over) - jnp.exp(-over)
                phase = PH[step, hp, here, :]
                nearby = (
                    PH[step, hp + 1, here, :] + PH[step, hp - 1, here, :]
                    + PH[step, hp, above, :] + PH[step, hp, below, :]
                    + PZ[hp, flat, :] - 6.0 * phase
                )
                well = phase * (1.0 - phase)
                change = nearby - well * (2.0 * (1.0 - 2.0 * phase) + 3.0 * drive)
                value = phase + 0.05 * change
                if offset:
                    value = jnp.where(beyond, 0.0, value)
                store(j, at, start, value)

    count = len([p for p in partners if p[0] == 0])
    total = count + sum(
        9 * jnp.where(ok, 1, 0) for ok in (g > 0, g < ng - 1)
    ) + sum(jnp.where(ok, 1, 0) for ok in (g > 1, g < ng - 2))
    pack_phase(0)
    loads[0].wait()
    loads[1].wait()
    pack_level(0, (1, 2, 3, 4))
    pl.semaphore_wait(barrier, total)

    phase_flat = send_phase_rims(0, 0)
    flat_u = send_flat_u(0)
    flat_v = send_flat_v(0)
    far_u = send_both_ways_u(0)
    phase_far = send_phase_planes(0, ((-1, 1, 5, 1), (1, 4, 0, 1)))
    far_v = send_both_ways_v(0)
    pin_outside()
    wires.receive(phase_flat)
    unpack_phase(0, 0)
    for p in (1, 2, 3, 4):
        derive(0, p, True)
    for level in range(3):
        wires.receive(flat_u)
        unpack(level, 0, 0, 3 * slab)
        sweep(level, 1, 1, 0, (1, 2), relax=False)
        pack_level(level + 1, (2, 3), (0, 1, 2))
        wires.receive(flat_v)
        unpack(level, 0, 3 * slab, slab)
        sweep(level, 1, 1, 0, (1, 2), displace=False)
        pack_level(level + 1, (2, 3), (3,))
        wires.receive(far_u)
        if level == 0:
            wires.receive(phase_far)
            derive(0, 0, False)
            derive(0, 5, False)
        unpack(level, 1, 0, 3)
        unpack(level, 2, 3 * (slab - 1), 3)
        sweep(level, 1, 1, 0, (0, 3), relax=False)
        pack_level(level + 1, (1, 4), (0, 1, 2))
        flat_u = send_flat_u(level + 1)
        if level < 2:
            far_u = send_both_ways_u(level + 1)
        else:
            ends = [planes(3, 0, 4, 0, 1), planes(3, 0, 1, 5, -1)]
        wires.receive(far_v)
        sweep(level, 1, 1, 0, (0, 3), displace=False)
        pack_level(level + 1, (1, 4), (3,))
        flat_v = send_flat_v(level + 1)
        if level < 2:
            far_v = send_both_ways_v(level + 1)

    far = send_rims_back(3)
    far.append(planes(3, pl.ds(1, 3), 1, 5, -1))
    wires.receive(flat_u)
    unpack(3, 0, 0, 3 * slab)

    def keep(j, at, start, value):
        PH[1, 1 + j, pl.ds(at, CHUNK), :] = value

    phase_update(0, 3, 1, 1, 0, (1, 2), keep)
    wires.receive(ends)
    phase_update(0, 3, 1, 1, 0, (0, 3), keep)
    pack_phase(1)
    phase_flat = send_phase_rims(1, 0)
    phase_far = send_phase_rims(1, -1)
    phase_far += send_phase_planes(1, ((-1, 1, 5, 2),))
    far.append(planes(3, every, 2, 6, -1))
    phase_later = send_phase_planes(1, ((-1, 3, 7, 2), (-2, 1, 9, 1)))

    wires.receive(flat_v)
    unpack(3, 0, 3 * slab, slab)
    wires.receive(phase_flat)
    unpack_phase(1, 0)
    derive(1, 1, False)
    for p in (2, 3, 4):
        derive(1, p, True)
    for level in (3, 4, 5):
        hbase, offset = level - 1, level - 2
        if level > 3:
            wires.receive(flat)
            unpack(level, 0, 0, 3 * slab)
            unpack(level, 0, 3 * slab, slab)
        sweep(level, 2, hbase, offset, (0, 1))
        pack_level(level + 1, (1, 2))
        if level < 5:
            next_far = send_rims_back(level + 1)
            next_far.append(planes(level + 1, every, 1, 5, -1))
            next_far.append(planes(level + 1, 0, 2, 6, -1))
        else:
            next_far = [column(6, dz, 1, pl.ds(0, 3), -1) for dz in (-1, 1)]
            for dy in (-1, 1):
                next_far.append(row(6, dy, pl.ds(1, 1), pl.ds(1, 1), pl.ds(5, 1), -1))
            next_far.append(planes(6, every, 1, 5, -1))
        if level == 3:
            wires.receive(phase_far)
            unpack_phase(1, 1)
            derive(1, 5, True)
            derive(1, 6, True)
        elif level == 4:
            wires.receive(phase_later)
            derive(1, 7, True)
        wires.receive(far)
        unpack(level, 1, 0, 6)
        unpack(level, 1, 3 * slab, 2)
        if level == 5:
            derive(1, 8, True)
        sweep(level, 2, hbase, offset, (2, 3))
        if level < 5:
            pack_level(level + 1, (3, 4))
            flat = send_flat_u(level + 1) + send_flat_v(level + 1)
            next_far.append(planes(level + 1, pl.ds(1, 3), 2, 6, -1))
        else:
            pack_level(6, (3, 4), (0, 1, 2))
            flat = [column(6, dz, 0, u_pairs, 0) for dz in (-1, 1)]
            flat += [row(6, dy, pl.ds(1, 1), mine, mine, 0) for dy in (-1, 1)]
            next_far.append(planes(6, 0, 2, 6, -1))
        far = next_far

    def finish(j, at, start, value):
        out[0, j, pl.ds(start, CHUNK), :] = value

    def hand_over(p):
        out[1, p - 2] = UE[6, 3, p, own, :]
        for c in range(3):
            out[2 + c, p - 2] = UE[6, c, p, own, :]

    for p in range(2, 5):
        hand_over(p)
    wires.receive(flat)
    unpack(6, 0, 0, 3 * slab)
    phase_update(1, 6, 2, 5, 4, (0, 1), finish)
    wires.receive(far)
    unpack(6, 1, 0, 3)
    hand_over(5)
    phase_update(1, 6, 2, 5, 4, (2, 3), finish)
    wires.drain()
    assert wires.count == COPIES, wires.count


def deliver(packed, phase, potential, displacement, sem):
    copies = [
        pltpu.make_async_copy(packed.at[0], phase, sem.at[0]),
        pltpu.make_async_copy(packed.at[1], potential, sem.at[1]),
        pltpu.make_async_copy(packed.at[pl.ds(2, 3)], displacement, sem.at[2]),
    ]
    for copy in copies:
        copy.start()
    for copy in copies:
        copy.wait()


def solution(mesh):
    ng, ny, nz = (mesh.shape[a] for a in ("grow", "cy", "cz"))

    def shards(labels, roughness, potential, displacement):
        slab, rows, lanes = labels.shape
        tall = rows + 2 * TOP
        f32 = jnp.float32
        vmem = pl.BlockSpec(memory_space=pltpu.VMEM)
        hbm = pl.BlockSpec(memory_space=pltpu.HBM)
        scratch = [
            (LEVELS, 4, slab + 3, tall, lanes),
            (LEVELS, 2, 3, slab + 1, 16, lanes),
            (LEVELS, 3, 2, 4 * slab, lanes),
            (LEVELS, 2, 4 * slab, lanes),
            (2, 10, tall, lanes),
            (2, 2, 2, slab, lanes),
            (2, 2, slab, lanes),
            (10, tall, lanes),
            (10, tall, lanes),
            (10, rows, lanes),
            (10, rows, lanes),
            (10, rows, lanes),
            (10, rows, lanes),
            (3, slab + 3, tall, lanes),
            (3, slab + 3, rows, lanes),
            (slab + 3, rows, lanes),
            (slab + 3, rows, lanes),
            (lanes, lanes),
            (lanes, lanes),
            (5, lanes, lanes),
            (2, lanes, lanes),
        ]
        packed = pl.pallas_call(
            functools.partial(kernel, ng, ny, nz),
            out_shape=jax.ShapeDtypeStruct((5,) + labels.shape, f32),
            in_specs=[hbm] * 4,
            out_specs=vmem,
            scratch_shapes=[pltpu.VMEM(shape, f32) for shape in scratch]
            + [
                pltpu.VMEM(labels.shape, jnp.int32),
                pltpu.VMEM(labels.shape, f32),
                pltpu.SemaphoreType.DMA((COPIES,)),
                pltpu.SemaphoreType.DMA((COPIES,)),
                pltpu.SemaphoreType.DMA((4,)),
            ],
            compiler_params=pltpu.CompilerParams(
                collective_id=0,
                has_side_effects=True,
                vmem_limit_bytes=40 * 1024 * 1024,
            ),
            name="filament",
        )(*(pltpu.with_memory_space_constraint(a, pltpu.HBM) for a in (labels, roughness, potential, displacement)))
        return pl.pallas_call(
            deliver,
            out_shape=(
                jax.ShapeDtypeStruct(labels.shape, f32),
                jax.ShapeDtypeStruct(labels.shape, f32),
                jax.ShapeDtypeStruct(displacement.shape, f32),
            ),
            in_specs=[pl.BlockSpec(memory_space=pl.ANY)],
            out_specs=(hbm,) * 3,
            scratch_shapes=[pltpu.SemaphoreType.DMA((3,))],
            compiler_params=pltpu.CompilerParams(vmem_limit_bytes=4 * 1024 * 1024),
            name="deliver",
        )(packed)

    placed = P("grow", "cy", "cz")
    vector = P(None, "grow", "cy", "cz")
    return jax.shard_map(
        shards,
        mesh=mesh,
        in_specs=(placed, placed, placed, vector),
        out_specs=(placed, placed, vector),
        check_vma=False,
    )
```

```python
import functools

import jax
import jax.numpy as jnp
from jax import lax
from jax.experimental import pallas as pl
from jax.experimental.pallas import tpu as pltpu
from jax.sharding import PartitionSpec as P

MESH = pl.DeviceIdType.MESH
LANES = 128
TOP = 8
CHUNK = 32
LEVELS = 7
COPIES = 175


class Wires:
    def __init__(self, send_sem, recv_sem, place):
        self.send_sem, self.recv_sem = send_sem, recv_sem
        self.g, self.y, self.z, self.ng, self.ny, self.nz = place
        self.count = 0
        self.pending = []

    def send(self, src, dst, dg, dy, dz):
        index = self.count
        self.count += 1
        target = (
            self.g + dg,
            lax.rem(self.y + dy + self.ny, self.ny),
            lax.rem(self.z + dz + self.nz, self.nz),
        )
        copy = pltpu.make_async_remote_copy(
            src_ref=src,
            dst_ref=dst,
            send_sem=self.send_sem.at[index],
            recv_sem=self.recv_sem.at[index],
            device_id=target,
            device_id_type=MESH,
        )
        self.when_valid(dg, copy.start)
        self.pending.append((dg, copy))
        return (dg, copy)

    def when_valid(self, dg, action):
        if dg == 0:
            action()
        else:
            ok = self.g + dg >= 0 if dg < 0 else self.g + dg < self.ng
            pl.when(ok)(action)

    def receive(self, messages):
        for dg, copy in messages:
            self.when_valid(-dg, copy.wait_recv)

    def drain(self):
        for dg, copy in self.pending:
            self.when_valid(dg, copy.wait_send)


def kernel(
    ng, ny, nz,
    lab, rough, pot, disp,
    out,
    UE, CE, RCU, SCU, PH, RCP, SCP,
    HH, CC, GZ, CZP, CZM, PZ, ZB, SB, PZP, PZM, TS, TT, HT, HP,
    LAB, ROU,
    send_sem, recv_sem, load_sem,
):
    g, y, z = lax.axis_index("grow"), lax.axis_index("cy"), lax.axis_index("cz")
    wires = Wires(send_sem, recv_sem, (g, y, z, ng, ny, nz))
    slab = lab.shape[0]
    rows = lab.shape[1]
    low, high = TOP - 1, TOP + rows
    own = pl.ds(TOP, rows)
    pairs = 4 * slab
    f32 = jnp.float32

    barrier = pltpu.get_barrier_semaphore()
    around = [(a, b) for a in (-1, 0, 1) for b in (-1, 0, 1)]
    partners = [(0, a, b) for a, b in around if (a, b) != (0, 0)]
    partners += [(s, a, b) for s in (-1, 1) for a, b in around]
    partners += [(-2, 0, 0), (2, 0, 0)]
    for dg, dy, dz in partners:
        def greet(dg=dg, dy=dy, dz=dz):
            pl.semaphore_signal(
                barrier,
                inc=1,
                device_id=(
                    g + dg,
                    lax.rem(y + dy + ny, ny),
                    lax.rem(z + dz + nz, nz),
                ),
                device_id_type=MESH,
            )
        wires.when_valid(dg, greet)

    loads = [
        pltpu.make_async_copy(
            disp, UE.at[0, pl.ds(0, 3), pl.ds(1, slab), own], load_sem.at[0]
        ),
        pltpu.make_async_copy(pot, UE.at[0, 3, pl.ds(1, slab), own], load_sem.at[1]),
        pltpu.make_async_copy(lab, LAB, load_sem.at[2]),
        pltpu.make_async_copy(rough, ROU, load_sem.at[3]),
    ]
    for load in loads:
        load.start()
    loads[2].wait()
    loads[3].wait()
    for p in range(slab):
        mark = LAB[p].astype(f32)
        part = 0.3 * ROU[p]
        PH[0, 1 + p, own, :] = mark * (1.0 - part) + (1.0 - mark) * part

    plane_shape = UE.shape[3:]

    def pin_outside():
        @pl.when(g == 0)
        def _():
            for level in range(4):
                for f in range(4):
                    UE[level, f, 0] = jnp.zeros(plane_shape, f32)
                RCU[level, 2] = jnp.zeros(RCU.shape[2:], f32)
            PH[0, 0] = jnp.ones(plane_shape, f32)

        @pl.when(g == ng - 1)
        def _():
            is_pot = lax.broadcasted_iota(jnp.int32, (pairs, LANES), 0) >= 3 * slab
            for level in range(LEVELS):
                for f in range(4):
                    for p in (5, 6):
                        UE[level, f, p] = jnp.full(plane_shape, 1.0 if f == 3 else 0.0, f32)
                CE[level, :, :, 4] = jnp.zeros((2, 3, 16, LANES), f32)
                for side in range(2):
                    RCU[level, 1, side] = jnp.where(is_pot, 1.0, 0.0)
            PH[0, 5] = jnp.zeros(plane_shape, f32)
            for p in range(5, 10):
                PH[1, p] = jnp.zeros(plane_shape, f32)
            RCP[1, 1] = jnp.zeros(RCP.shape[2:], f32)

        @pl.when(g == ng - 2)
        def _():
            PH[1, 9] = jnp.zeros(plane_shape, f32)

    lane = lax.broadcasted_iota(jnp.int32, (CHUNK, LANES), 1)
    lane_row = lax.broadcasted_iota(jnp.int32, (1, LANES), 1)
    chunks = [(TOP + start, start) for start in range(0, rows, CHUNK)]

    def pack(planes):
        for at, start in chunks:
            tile = None
            for k, ref, index in planes:
                moved = pltpu.roll(ref[index + (pl.ds(at, CHUNK), slice(None))], 2 * k + 1, 1)
                tile = moved if tile is None else jnp.where(lane // 2 == k, moved, tile)
            TS[pl.ds(start, CHUNK), :] = tile
        TT[...] = jnp.transpose(TS[...])

    def pair(f, q):
        return 3 * slab + q - 1 if f == 3 else 3 * (q - 1) + f

    def pack_level(level, planes, fields=(0, 1, 2, 3)):
        pack([(pair(f, q), UE, (level, f, q)) for q in planes for f in fields])
        for q in planes:
            for f in fields:
                if f in (0, 3):
                    first, size = pair(f, q), 1 if f == 3 else 3
                    for side in (0, 1):
                        SCU[level, side, pl.ds(first, size)] = TT[
                            pl.ds(2 * first + 1 - side, size, stride=2), :
                        ]

    def row(level, dy, fields, here, there, dg):
        src, dst = (TOP, high) if dy < 0 else (TOP + rows - 1, low)
        return wires.send(
            UE.at[level, fields, here, pl.ds(src, 1)],
            UE.at[level, fields, there, pl.ds(dst, 1)],
            dg, dy, 0,
        )

    def corner(level, dy, dz, here, there, dg):
        src, dst = (TOP, TOP) if dy < 0 else (TOP + rows - 1, TOP - 1)
        return wires.send(
            UE.at[level, pl.ds(0, 3), here, pl.ds(src, 1)],
            CE.at[level, 0 if dz > 0 else 1, :, there, pl.ds(dst, 1)],
            dg, dy, dz,
        )

    def column(level, dz, slot, which, dg):
        return wires.send(
            SCU.at[level, 0 if dz < 0 else 1, which],
            RCU.at[level, slot, 1 if dz < 0 else 0, which],
            dg, 0, dz,
        )

    def planes(level, fields, here, there, dg):
        return wires.send(
            UE.at[level, fields, here, own], UE.at[level, fields, there, own], dg, 0, 0
        )

    every, mine = pl.ds(0, 4), pl.ds(1, slab)
    u_fields, v_field = pl.ds(0, 3), pl.ds(3, 1)
    u_pairs, v_pairs = pl.ds(0, 3 * slab), pl.ds(3 * slab, slab)

    def send_flat_u(level):
        sent = [column(level, dz, 0, u_pairs, 0) for dz in (-1, 1)]
        for dy in (-1, 1):
            sent.append(row(level, dy, u_fields, mine, mine, 0))
            for dz in (-1, 1):
                sent.append(corner(level, dy, dz, mine, pl.ds(0, slab), 0))
        return sent

    def send_flat_v(level):
        sent = [column(level, dz, 0, v_pairs, 0) for dz in (-1, 1)]
        return sent + [row(level, dy, v_field, mine, mine, 0) for dy in (-1, 1)]

    def send_both_ways_u(level):
        sent = []
        for dg, here, there, slot in ((-1, 1, 5, 1), (1, 4, 0, 2)):
            for dz in (-1, 1):
                sent.append(column(level, dz, slot, pl.ds(3 * (here - 1), 3), dg))
            for dy in (-1, 1):
                sent.append(row(level, dy, pl.ds(0, 2), pl.ds(here, 1), pl.ds(there, 1), dg))
        for dg, here, there in ((-1, 1, 5), (1, 4, 0)):
            sent.append(planes(level, u_fields, here, there, dg))
        return sent

    def send_both_ways_v(level):
        return [planes(level, 3, here, there, dg) for dg, here, there in ((-1, 1, 5), (1, 4, 0))]

    def send_rims_back(level):
        two = pl.ds(1, 2), pl.ds(5, 2)
        sent = []
        for dz in (-1, 1):
            sent.append(column(level, dz, 1, pl.ds(0, 6), -1))
            sent.append(column(level, dz, 1, pl.ds(3 * slab, 2), -1))
        for dy in (-1, 1):
            sent.append(row(level, dy, every, *two, -1))
            for dz in (-1, 1):
                sent.append(corner(level, dy, dz, pl.ds(1, 1), pl.ds(4, 1), -1))
        return sent

    def unpack(level, slot, first, size):
        TS[pl.ds(2 * first, size, stride=2), :] = RCU[level, slot, 1, pl.ds(first, size)]
        TS[pl.ds(2 * first + 1, size, stride=2), :] = RCU[level, slot, 0, pl.ds(first, size)]
        HT[slot if first < 3 * slab else 3 + slot] = jnp.transpose(TS[...])

    def halo_lane(f, p):
        slot, q = (2, slab) if p == 0 else (0, p) if p <= slab else (1, p - slab)
        return slot + (3 if f == 3 else 0), 2 * pair(f, q)

    def sides(values, halo, at_lane):
        halo = pltpu.roll(halo, (2 * LANES - at_lane - 1) % LANES, 1)
        behind = jnp.where(lane == 0, halo, pltpu.roll(values, 1, 1))
        ahead = jnp.where(lane == LANES - 1, halo, pltpu.roll(values, LANES - 1, 1))
        return behind, ahead

    def lateral(level, f, p, centre):
        slot, at_lane = halo_lane(f, p)
        for at, start in chunks:
            flat = pl.ds(start, CHUNK)
            values = UE[level, f, p, pl.ds(at, CHUNK), :]
            behind, ahead = sides(values, HT[slot, flat, :], at_lane)
            if f == 3:
                PZP[p, flat, :] = ahead
                PZM[p, flat, :] = behind
            else:
                ZB[f, p, pl.ds(at, CHUNK), :] = ahead - behind
                if centre:
                    SB[f, p, flat, :] = ahead + behind

    def lateral_row(level, f, p, at, corner_at):
        values = UE[level, f, p, pl.ds(at, 1), :]
        left = CE[level, 0, f, p - 1, pl.ds(corner_at, 1), :]
        right = CE[level, 1, f, p - 1, pl.ds(corner_at, 1), :]
        behind = jnp.where(lane_row == 0, pltpu.roll(left, 1, 1), pltpu.roll(values, 1, 1))
        ahead = jnp.where(
            lane_row == LANES - 1,
            pltpu.roll(right, LANES - 1, 1),
            pltpu.roll(values, LANES - 1, 1),
        )
        ZB[f, p, pl.ds(at, 1), :] = ahead - behind

    def each(js):
        if len(js) == 1:
            return lambda body: body(js[0])
        return lambda body: pl.loop(0, len(js))(lambda i: body(js[0] + i * (js[1] - js[0])))

    ready = set()

    def once(*key):
        fresh = key not in ready
        ready.add(key)
        return fresh

    def sweep(level, base, hbase, offset, js, displace=True, relax=True):
        inside = range(base, base + slab)
        for p in range(min(js) + base - 1, max(js) + base + 2):
            centre = p - base in js
            wanted = (0, 1, 2) if centre else (0, 2)
            wanted = (wanted if displace else ()) + ((3,) if relax and centre else ())
            if not centre and p - 1 - base not in js and p + 1 - base not in js:
                continue
            for f in wanted:
                if once("side", level, f, p):
                    lateral(level, f, p, p in inside)
            if centre and displace:
                for f in (1, 2):
                    lateral_row(level, f, p, low, TOP - 1)
                    lateral_row(level, f, p, high, TOP)

        @each(js)
        def _(j):
            p = base + j
            hp = hbase + j
            beyond = g * slab + offset + j >= ng * slab
            for at, start in chunks:
                here = pl.ds(at, CHUNK)
                above, below = pl.ds(at + 1, CHUNK), pl.ds(at - 1, CHUNK)
                flat = pl.ds(start, CHUNK)
                if displace:
                    ux, uy, uz = (UE[level, c, p, here, :] for c in range(3))
                    pair_x = [UE[level, c, p + 1, here, :] + UE[level, c, p - 1, here, :] for c in range(3)]
                    pair_y = [UE[level, c, p, above, :] + UE[level, c, p, below, :] for c in range(3)]
                    pair_z = [SB[c, p, flat, :] for c in range(3)]

                    def divided_yz(q, hq):
                        return (
                            UE[level, 1, q, above, :] - UE[level, 1, q, below, :]
                            + ZB[2, q, here, :] - HH[hq, here, :]
                        )

                    def divided_xz(at_rows):
                        return (
                            UE[level, 0, p + 1, at_rows, :] - UE[level, 0, p - 1, at_rows, :]
                            + ZB[2, p, at_rows, :] - HH[hp, at_rows, :]
                        )

                    cross_x = divided_yz(p + 1, hp + 1) - divided_yz(p - 1, hp - 1)
                    cross_y = divided_xz(above) - divided_xz(below)
                    cross_z = (
                        ZB[0, p + 1, here, :] - ZB[0, p - 1, here, :]
                        + ZB[1, p, above, :] - ZB[1, p, below, :]
                        - GZ[hp, flat, :]
                    )
                    new_x = 0.12 * ux + 0.28 * pair_x[0] + 0.08 * (pair_y[0] + pair_z[0]) + 0.05 * cross_x
                    new_y = 0.12 * uy + 0.28 * pair_y[1] + 0.08 * (pair_x[1] + pair_z[1]) + 0.05 * cross_y
                    new_z = 0.12 * uz + 0.28 * pair_z[2] + 0.08 * (pair_x[2] + pair_y[2]) + 0.05 * cross_z
                    for f, value in enumerate((new_x, new_y, new_z)):
                        if offset:
                            value = jnp.where(beyond, 0.0, value)
                        UE[level + 1, f, 1 + j, here, :] = value
                if relax:
                    v = UE[level, 3, p, here, :]
                    c = CC[hp, here, :]
                    flux = CZP[hp, flat, :] * (PZP[p, flat, :] - v) + CZM[hp, flat, :] * (PZM[p, flat, :] - v)
                    for q, hq, r in ((p + 1, hp + 1, here), (p - 1, hp - 1, here), (p, hp, above), (p, hp, below)):
                        flux = flux + (CC[hq, r, :] + c) * (UE[level, 3, q, r, :] - v)
                    new_v = v + flux
                    if offset:
                        new_v = jnp.where(beyond, 1.0, new_v)
                    UE[level + 1, 3, 1 + j, here, :] = new_v

    def h_of(phase):
        return phase * phase * (3.0 - 2.0 * phase)

    def pack_phase(step):
        pack([(p, PH, (step, 1 + p)) for p in range(slab)])
        SCP[step, 1] = TT[pl.ds(0, slab, stride=2), :]
        SCP[step, 0] = TT[pl.ds(1, slab, stride=2), :]

    def send_phase_rims(step, dg):
        sent = []
        for dz in (-1, 1):
            sent.append(
                wires.send(
                    SCP.at[step, 0 if dz < 0 else 1],
                    RCP.at[step, -dg, 1 if dz < 0 else 0],
                    dg, 0, dz,
                )
            )
        for dy, src, dst in ((-1, TOP, high), (1, TOP + rows - 1, low)):
            sent.append(
                wires.send(
                    PH.at[step, pl.ds(1, slab), pl.ds(src, 1)],
                    PH.at[step, pl.ds(1 - dg * slab, slab), pl.ds(dst, 1)],
                    dg, dy, 0,
                )
            )
        return sent

    def send_phase_planes(step, moves):
        return [
            wires.send(
                PH.at[step, pl.ds(src, count), own], PH.at[step, pl.ds(dst, count), own], dg, 0, 0
            )
            for dg, src, dst, count in moves
        ]

    def unpack_phase(step, slot):
        TS[pl.ds(0, slab, stride=2), :] = RCP[step, slot, 1]
        TS[pl.ds(1, slab, stride=2), :] = RCP[step, slot, 0]
        HP[slot] = jnp.transpose(TS[...])

    def derive(step, p, centre):
        slot = 0 if p <= slab else 1
        for at, start in chunks:
            flat = pl.ds(start, CHUNK)
            phase = PH[step, p, pl.ds(at, CHUNK), :]
            h = h_of(phase)
            c = 0.0075 + 0.0675 * h
            HH[p, pl.ds(at, CHUNK), :] = 0.52 * h
            CC[p, pl.ds(at, CHUNK), :] = c
            if centre:
                behind, ahead = sides(phase, HP[slot, flat, :], 2 * (p - 1 - slot * slab))
                h_behind, h_ahead = h_of(behind), h_of(ahead)
                GZ[p, flat, :] = 0.52 * (h_ahead - h_behind)
                CZP[p, flat, :] = c + (0.0075 + 0.0675 * h_ahead)
                CZM[p, flat, :] = c + (0.0075 + 0.0675 * h_behind)
                PZ[p, flat, :] = ahead + behind
        if centre:
            for at in (low, high):
                h = h_of(PH[step, p, pl.ds(at, 1), :])
                HH[p, pl.ds(at, 1), :] = 0.52 * h
                CC[p, pl.ds(at, 1), :] = 0.0075 + 0.0675 * h

    def phase_update(step, level, base, hbase, offset, js, store):
        for j in js:
            if once("side", level, 2, base + j):
                lateral(level, 2, base + j, True)

        @each(js)
        def _(j):
            p = base + j
            hp = hbase + j
            beyond = g * slab + offset + j >= ng * slab
            for at, start in chunks:
                here = pl.ds(at, CHUNK)
                above, below = pl.ds(at + 1, CHUNK), pl.ds(at - 1, CHUNK)
                flat = pl.ds(start, CHUNK)
                twice = (
                    UE[level, 0, p + 1, here, :] - UE[level, 0, p - 1, here, :]
                    + UE[level, 1, p, above, :] - UE[level, 1, p, below, :]
                    + ZB[2, p, here, :]
                )
                over = UE[level, 3, p, here, :] - 0.5 + 0.325 * twice - 0.375 * HH[hp, here, :]
                drive = jnp.exp(over) - jnp.exp(-over)
                phase = PH[step, hp, here, :]
                nearby = (
                    PH[step, hp + 1, here, :] + PH[step, hp - 1, here, :]
                    + PH[step, hp, above, :] + PH[step, hp, below, :]
                    + PZ[hp, flat, :] - 6.0 * phase
                )
                well = phase * (1.0 - phase)
                change = nearby - well * (2.0 * (1.0 - 2.0 * phase) + 3.0 * drive)
                value = phase + 0.05 * change
                if offset:
                    value = jnp.where(beyond, 0.0, value)
                store(j, at, start, value)

    count = len([p for p in partners if p[0] == 0])
    total = count + sum(
        9 * jnp.where(ok, 1, 0) for ok in (g > 0, g < ng - 1)
    ) + sum(jnp.where(ok, 1, 0) for ok in (g > 1, g < ng - 2))
    pack_phase(0)
    loads[0].wait()
    loads[1].wait()
    pack_level(0, (1, 2, 3, 4))
    pl.semaphore_wait(barrier, total)

    phase_flat = send_phase_rims(0, 0)
    flat_u = send_flat_u(0)
    flat_v = send_flat_v(0)
    far_u = send_both_ways_u(0)
    phase_far = send_phase_planes(0, ((-1, 1, 5, 1), (1, 4, 0, 1)))
    far_v = send_both_ways_v(0)
    pin_outside()
    wires.receive(phase_flat)
    unpack_phase(0, 0)
    for p in (1, 2, 3, 4):
        derive(0, p, True)
    for level in range(3):
        wires.receive(flat_u)
        unpack(level, 0, 0, 3 * slab)
        sweep(level, 1, 1, 0, (1, 2), relax=False)
        pack_level(level + 1, (2, 3), (0, 1, 2))
        seen = set(ready)
        for core in (0, 1):

            @pl.when(lax.rem(g, 2) == core)
            def _(core=core):
                ready.clear()
                ready.update(seen)
                for right in (True, False) if core == 0 else (False, True):
                    wires.receive([m for m in far_u if (m[0] < 0) == right])
                    if level == 0:
                        wires.receive([m for m in phase_far if (m[0] < 0) == right])
                        derive(0, 5 if right else 0, False)
                    if right:
                        unpack(level, 1, 0, 3)
                    else:
                        unpack(level, 2, 3 * (slab - 1), 3)
                    sweep(level, 1, 1, 0, (3,) if right else (0,), relax=False)

        pack_level(level + 1, (1, 4), (0, 1, 2))
        flat_u = send_flat_u(level + 1)
        if level < 2:
            far_u = send_both_ways_u(level + 1)
        else:
            ends = [planes(3, 0, 4, 0, 1), planes(3, 0, 1, 5, -1)]
        wires.receive(flat_v)
        wires.receive(far_v)
        unpack(level, 0, 3 * slab, slab)
        sweep(level, 1, 1, 0, (0, 1, 2, 3), displace=False)
        pack_level(level + 1, (1, 2, 3, 4), (3,))
        flat_v = send_flat_v(level + 1)
        if level < 2:
            far_v = send_both_ways_v(level + 1)

    far = send_rims_back(3)
    far.append(planes(3, pl.ds(1, 3), 1, 5, -1))
    wires.receive(flat_u)
    unpack(3, 0, 0, 3 * slab)

    def keep(j, at, start, value):
        PH[1, 1 + j, pl.ds(at, CHUNK), :] = value

    phase_update(0, 3, 1, 1, 0, (1, 2), keep)
    wires.receive(ends)
    phase_update(0, 3, 1, 1, 0, (0, 3), keep)
    pack_phase(1)
    phase_flat = send_phase_rims(1, 0)
    phase_far = send_phase_rims(1, -1)
    phase_far += send_phase_planes(1, ((-1, 1, 5, 2),))
    far.append(planes(3, every, 2, 6, -1))
    phase_later = send_phase_planes(1, ((-1, 3, 7, 2), (-2, 1, 9, 1)))

    wires.receive(flat_v)
    unpack(3, 0, 3 * slab, slab)
    wires.receive(phase_flat)
    unpack_phase(1, 0)
    derive(1, 1, False)
    for p in (2, 3, 4):
        derive(1, p, True)
    for level in (3, 4, 5):
        hbase, offset = level - 1, level - 2
        if level > 3:
            wires.receive(flat)
            unpack(level, 0, 0, 3 * slab)
            unpack(level, 0, 3 * slab, slab)
        sweep(level, 2, hbase, offset, (0, 1))
        pack_level(level + 1, (1, 2))
        if level < 5:
            next_far = send_rims_back(level + 1)
            next_far.append(planes(level + 1, every, 1, 5, -1))
            next_far.append(planes(level + 1, 0, 2, 6, -1))
        else:
            next_far = [column(6, dz, 1, pl.ds(0, 3), -1) for dz in (-1, 1)]
            for dy in (-1, 1):
                next_far.append(row(6, dy, pl.ds(1, 1), pl.ds(1, 1), pl.ds(5, 1), -1))
            next_far.append(planes(6, every, 1, 5, -1))
        if level == 3:
            wires.receive(phase_far)
            unpack_phase(1, 1)
            derive(1, 5, True)
            derive(1, 6, True)
        elif level == 4:
            wires.receive(phase_later)
            derive(1, 7, True)
        wires.receive(far)
        unpack(level, 1, 0, 6)
        unpack(level, 1, 3 * slab, 2)
        if level == 5:
            derive(1, 8, True)
        sweep(level, 2, hbase, offset, (2, 3))
        if level < 5:
            pack_level(level + 1, (3, 4))
            flat = send_flat_u(level + 1) + send_flat_v(level + 1)
            next_far.append(planes(level + 1, pl.ds(1, 3), 2, 6, -1))
        else:
            pack_level(6, (3, 4), (0, 1, 2))
            flat = [column(6, dz, 0, u_pairs, 0) for dz in (-1, 1)]
            flat += [row(6, dy, pl.ds(1, 1), mine, mine, 0) for dy in (-1, 1)]
            next_far.append(planes(6, 0, 2, 6, -1))
        far = next_far

    def finish(j, at, start, value):
        out[0, j, pl.ds(start, CHUNK), :] = value

    def hand_over(p):
        out[1, p - 2] = UE[6, 3, p, own, :]
        for c in range(3):
            out[2 + c, p - 2] = UE[6, c, p, own, :]

    for p in range(2, 5):
        hand_over(p)
    wires.receive(flat)
    unpack(6, 0, 0, 3 * slab)
    phase_update(1, 6, 2, 5, 4, (0, 1), finish)
    wires.receive(far)
    unpack(6, 1, 0, 3)
    hand_over(5)
    phase_update(1, 6, 2, 5, 4, (2, 3), finish)
    wires.drain()
    assert wires.count == COPIES, wires.count


def deliver(packed, phase, potential, displacement, sem):
    copies = [
        pltpu.make_async_copy(packed.at[0], phase, sem.at[0]),
        pltpu.make_async_copy(packed.at[1], potential, sem.at[1]),
        pltpu.make_async_copy(packed.at[pl.ds(2, 3)], displacement, sem.at[2]),
    ]
    for copy in copies:
        copy.start()
    for copy in copies:
        copy.wait()


def solution(mesh):
    ng, ny, nz = (mesh.shape[a] for a in ("grow", "cy", "cz"))

    def shards(labels, roughness, potential, displacement):
        slab, rows, lanes = labels.shape
        tall = rows + 2 * TOP
        f32 = jnp.float32
        vmem = pl.BlockSpec(memory_space=pltpu.VMEM)
        hbm = pl.BlockSpec(memory_space=pltpu.HBM)
        scratch = [
            (LEVELS, 4, slab + 3, tall, lanes),
            (LEVELS, 2, 3, slab + 1, 16, lanes),
            (LEVELS, 3, 2, 4 * slab, lanes),
            (LEVELS, 2, 4 * slab, lanes),
            (2, 10, tall, lanes),
            (2, 2, 2, slab, lanes),
            (2, 2, slab, lanes),
            (10, tall, lanes),
            (10, tall, lanes),
            (10, rows, lanes),
            (10, rows, lanes),
            (10, rows, lanes),
            (10, rows, lanes),
            (3, slab + 3, tall, lanes),
            (3, slab + 3, rows, lanes),
            (slab + 3, rows, lanes),
            (slab + 3, rows, lanes),
            (lanes, lanes),
            (lanes, lanes),
            (5, lanes, lanes),
            (2, lanes, lanes),
        ]
        packed = pl.pallas_call(
            functools.partial(kernel, ng, ny, nz),
            out_shape=jax.ShapeDtypeStruct((5,) + labels.shape, f32),
            in_specs=[hbm] * 4,
            out_specs=vmem,
            scratch_shapes=[pltpu.VMEM(shape, f32) for shape in scratch]
            + [
                pltpu.VMEM(labels.shape, jnp.int32),
                pltpu.VMEM(labels.shape, f32),
                pltpu.SemaphoreType.DMA((COPIES,)),
                pltpu.SemaphoreType.DMA((COPIES,)),
                pltpu.SemaphoreType.DMA((4,)),
            ],
            compiler_params=pltpu.CompilerParams(
                collective_id=0,
                has_side_effects=True,
                vmem_limit_bytes=40 * 1024 * 1024,
            ),
            name="filament",
        )(*(pltpu.with_memory_space_constraint(a, pltpu.HBM) for a in (labels, roughness, potential, displacement)))
        return pl.pallas_call(
            deliver,
            out_shape=(
                jax.ShapeDtypeStruct(labels.shape, f32),
                jax.ShapeDtypeStruct(labels.shape, f32),
                jax.ShapeDtypeStruct(displacement.shape, f32),
            ),
            in_specs=[pl.BlockSpec(memory_space=pl.ANY)],
            out_specs=(hbm,) * 3,
            scratch_shapes=[pltpu.SemaphoreType.DMA((3,))],
            compiler_params=pltpu.CompilerParams(vmem_limit_bytes=4 * 1024 * 1024),
            name="deliver",
        )(packed)

    placed = P("grow", "cy", "cz")
    vector = P(None, "grow", "cy", "cz")
    return jax.shard_map(
        shards,
        mesh=mesh,
        in_specs=(placed, placed, placed, vector),
        out_specs=(placed, placed, vector),
        check_vma=False,
    )
```

```python
import functools

import jax
import jax.numpy as jnp
from jax import lax
from jax.experimental import pallas as pl
from jax.experimental.pallas import tpu as pltpu
from jax.sharding import PartitionSpec as P

MESH = pl.DeviceIdType.MESH
LANES = 128
TOP = 8
CHUNK = 32
LEVELS = 7
COPIES = 173


class Wires:
    def __init__(self, send_sem, recv_sem, place):
        self.send_sem, self.recv_sem = send_sem, recv_sem
        self.g, self.y, self.z, self.ng, self.ny, self.nz = place
        self.count = 0
        self.pending = []

    def send(self, src, dst, dg, dy, dz):
        index = self.count
        self.count += 1
        target = (
            self.g + dg,
            lax.rem(self.y + dy + self.ny, self.ny),
            lax.rem(self.z + dz + self.nz, self.nz),
        )
        copy = pltpu.make_async_remote_copy(
            src_ref=src,
            dst_ref=dst,
            send_sem=self.send_sem.at[index],
            recv_sem=self.recv_sem.at[index],
            device_id=target,
            device_id_type=MESH,
        )
        self.when_valid(dg, copy.start)
        self.pending.append((dg, copy))
        return (dg, copy, dy != 0)

    def when_valid(self, dg, action):
        if dg == 0:
            action()
        else:
            ok = self.g + dg >= 0 if dg < 0 else self.g + dg < self.ng
            pl.when(ok)(action)

    def receive(self, messages):
        for dg, copy, _ in messages:
            self.when_valid(-dg, copy.wait_recv)

    def drain(self):
        for dg, copy in self.pending:
            self.when_valid(dg, copy.wait_send)


def kernel(
    ng, ny, nz,
    lab, rough, pot, disp,
    out,
    UE, CE, RCU, SCU, PH, RCP, SCP,
    HH, CC, GZ, CZP, CZM, PZ, ZB, SB, PZP, PZM, TS, TT, HT, HP,
    LAB, ROU,
    send_sem, recv_sem, load_sem,
):
    g, y, z = lax.axis_index("grow"), lax.axis_index("cy"), lax.axis_index("cz")
    wires = Wires(send_sem, recv_sem, (g, y, z, ng, ny, nz))
    slab = lab.shape[0]
    rows = lab.shape[1]
    low, high = TOP - 1, TOP + rows
    own = pl.ds(TOP, rows)
    pairs = 4 * slab
    f32 = jnp.float32

    barrier = pltpu.get_barrier_semaphore()
    around = [(a, b) for a in (-1, 0, 1) for b in (-1, 0, 1)]
    partners = [(0, a, b) for a, b in around if (a, b) != (0, 0)]
    partners += [(s, a, b) for s in (-1, 1) for a, b in around]
    partners += [(-2, 0, 0), (2, 0, 0)]
    for dg, dy, dz in partners:
        def greet(dg=dg, dy=dy, dz=dz):
            pl.semaphore_signal(
                barrier,
                inc=1,
                device_id=(
                    g + dg,
                    lax.rem(y + dy + ny, ny),
                    lax.rem(z + dz + nz, nz),
                ),
                device_id_type=MESH,
            )
        wires.when_valid(dg, greet)

    loads = [
        pltpu.make_async_copy(
            disp, UE.at[0, pl.ds(0, 3), pl.ds(1, slab), own], load_sem.at[0]
        ),
        pltpu.make_async_copy(pot, UE.at[0, 3, pl.ds(1, slab), own], load_sem.at[1]),
        pltpu.make_async_copy(lab, LAB, load_sem.at[2]),
        pltpu.make_async_copy(rough, ROU, load_sem.at[3]),
    ]
    for load in loads:
        load.start()
    loads[2].wait()
    loads[3].wait()
    for p in range(slab):
        mark = LAB[p].astype(f32)
        part = 0.3 * ROU[p]
        PH[0, 1 + p, own, :] = mark * (1.0 - part) + (1.0 - mark) * part

    plane_shape = UE.shape[3:]

    def pin_outside():
        @pl.when(g == 0)
        def _():
            for level in range(4):
                for f in range(4):
                    UE[level, f, 0] = jnp.zeros(plane_shape, f32)
                RCU[level, 2] = jnp.zeros(RCU.shape[2:], f32)
            PH[0, 0] = jnp.ones(plane_shape, f32)

        @pl.when(g == ng - 1)
        def _():
            is_pot = lax.broadcasted_iota(jnp.int32, (pairs, LANES), 0) >= 3 * slab
            for level in range(LEVELS):
                for f in range(4):
                    for p in (5, 6):
                        UE[level, f, p] = jnp.full(plane_shape, 1.0 if f == 3 else 0.0, f32)
                CE[level, :, :, 4] = jnp.zeros((2, 3, 16, LANES), f32)
                for side in range(2):
                    RCU[level, 1, side] = jnp.where(is_pot, 1.0, 0.0)
            PH[0, 5] = jnp.zeros(plane_shape, f32)
            for p in range(5, 10):
                PH[1, p] = jnp.zeros(plane_shape, f32)
            RCP[1, 1] = jnp.zeros(RCP.shape[2:], f32)

        @pl.when(g == ng - 2)
        def _():
            PH[1, 9] = jnp.zeros(plane_shape, f32)

    lane = lax.broadcasted_iota(jnp.int32, (CHUNK, LANES), 1)
    lane_row = lax.broadcasted_iota(jnp.int32, (1, LANES), 1)
    chunks = [(TOP + start, start) for start in range(0, rows, CHUNK)]

    def pack(planes):
        for at, start in chunks:
            tile = None
            for k, ref, index in planes:
                moved = pltpu.roll(ref[index + (pl.ds(at, CHUNK), slice(None))], 2 * k + 1, 1)
                tile = moved if tile is None else jnp.where(lane // 2 == k, moved, tile)
            TS[pl.ds(start, CHUNK), :] = tile
        TT[...] = jnp.transpose(TS[...])

    def pair(f, q):
        return 3 * slab + q - 1 if f == 3 else 3 * (q - 1) + f

    def pack_level(level, planes, fields=(0, 1, 2, 3)):
        pack([(pair(f, q), UE, (level, f, q)) for q in planes for f in fields])
        for q in planes:
            for f in fields:
                if f in (0, 3):
                    first, size = pair(f, q), 1 if f == 3 else 3
                    for side in (0, 1):
                        SCU[level, side, pl.ds(first, size)] = TT[
                            pl.ds(2 * first + 1 - side, size, stride=2), :
                        ]

    def row(level, dy, fields, here, there, dg):
        src, dst = (TOP, high) if dy < 0 else (TOP + rows - 1, low)
        return wires.send(
            UE.at[level, fields, here, pl.ds(src, 1)],
            UE.at[level, fields, there, pl.ds(dst, 1)],
            dg, dy, 0,
        )

    def straight(messages):
        return [m for m in messages if not m[2]]

    def across(messages):
        return [m for m in messages if m[2]]

    def corner(level, dy, dz, here, there, dg):
        src, dst = (TOP, TOP) if dy < 0 else (TOP + rows - 1, TOP - 1)
        return wires.send(
            UE.at[level, pl.ds(0, 3), here, pl.ds(src, 1)],
            CE.at[level, 0 if dz > 0 else 1, :, there, pl.ds(dst, 1)],
            dg, dy, dz,
        )

    def column(level, dz, slot, which, dg):
        return wires.send(
            SCU.at[level, 0 if dz < 0 else 1, which],
            RCU.at[level, slot, 1 if dz < 0 else 0, which],
            dg, 0, dz,
        )

    def planes(level, fields, here, there, dg):
        return wires.send(
            UE.at[level, fields, here, own], UE.at[level, fields, there, own], dg, 0, 0
        )

    every, mine = pl.ds(0, 4), pl.ds(1, slab)
    u_fields, v_field = pl.ds(0, 3), pl.ds(3, 1)
    u_pairs, v_pairs = pl.ds(0, 3 * slab), pl.ds(3 * slab, slab)

    def send_flat_u(level):
        sent = [column(level, dz, 0, u_pairs, 0) for dz in (-1, 1)]
        for dy in (-1, 1):
            sent.append(row(level, dy, u_fields, mine, mine, 0))
            for dz in (-1, 1):
                sent.append(corner(level, dy, dz, mine, pl.ds(0, slab), 0))
        return sent

    def send_flat_v(level):
        sent = [column(level, dz, 0, v_pairs, 0) for dz in (-1, 1)]
        return sent + [row(level, dy, v_field, mine, mine, 0) for dy in (-1, 1)]

    def send_both_ways_u(level):
        sent = []
        for dg, here, there, slot in ((-1, 1, 5, 1), (1, 4, 0, 2)):
            for dz in (-1, 1):
                sent.append(column(level, dz, slot, pl.ds(3 * (here - 1), 3), dg))
            for dy in (-1, 1):
                sent.append(row(level, dy, pl.ds(0, 2), pl.ds(here, 1), pl.ds(there, 1), dg))
        for dg, here, there in ((-1, 1, 5), (1, 4, 0)):
            sent.append(planes(level, u_fields, here, there, dg))
        return sent

    def send_both_ways_v(level):
        return [planes(level, 3, here, there, dg) for dg, here, there in ((-1, 1, 5), (1, 4, 0))]

    def send_rims_back(level):
        two = pl.ds(1, 2), pl.ds(5, 2)
        sent = []
        for dz in (-1, 1):
            sent.append(column(level, dz, 1, pl.ds(0, 6), -1))
            sent.append(column(level, dz, 1, pl.ds(3 * slab, 2), -1))
        for dy in (-1, 1):
            sent.append(row(level, dy, every, *two, -1))
            for dz in (-1, 1):
                sent.append(corner(level, dy, dz, pl.ds(1, 1), pl.ds(4, 1), -1))
        return sent

    def unpack(level, slot, first, size):
        TS[pl.ds(2 * first, size, stride=2), :] = RCU[level, slot, 1, pl.ds(first, size)]
        TS[pl.ds(2 * first + 1, size, stride=2), :] = RCU[level, slot, 0, pl.ds(first, size)]
        HT[slot if first < 3 * slab else 3 + slot] = jnp.transpose(TS[...])

    def unpack_both(level, slot, count):
        for first, size in ((0, 3 * count), (3 * slab, count)):
            TS[pl.ds(2 * first, size, stride=2), :] = RCU[level, slot, 1, pl.ds(first, size)]
            TS[pl.ds(2 * first + 1, size, stride=2), :] = RCU[level, slot, 0, pl.ds(first, size)]
        HT[slot] = jnp.transpose(TS[...])

    def halo_lane(level, f, p):
        slot, q = (2, slab) if p == 0 else (0, p) if p <= slab else (1, p - slab)
        apart = f == 3 and (level < 3 or level == 3 and slot == 0)
        return slot + (3 if apart else 0), 2 * pair(f, q)

    def sides(values, halo, at_lane):
        halo = pltpu.roll(halo, (2 * LANES - at_lane - 1) % LANES, 1)
        behind = jnp.where(lane == 0, halo, pltpu.roll(values, 1, 1))
        ahead = jnp.where(lane == LANES - 1, halo, pltpu.roll(values, LANES - 1, 1))
        return behind, ahead

    def lateral(level, f, p, centre):
        slot, at_lane = halo_lane(level, f, p)
        for at, start in chunks:
            flat = pl.ds(start, CHUNK)
            values = UE[level, f, p, pl.ds(at, CHUNK), :]
            behind, ahead = sides(values, HT[slot, flat, :], at_lane)
            if f == 3:
                PZP[p, flat, :] = ahead
                PZM[p, flat, :] = behind
            else:
                ZB[f, p, pl.ds(at, CHUNK), :] = ahead - behind
                if centre:
                    SB[f, p, flat, :] = ahead + behind

    def lateral_row(level, f, p, at, corner_at):
        values = UE[level, f, p, pl.ds(at, 1), :]
        left = CE[level, 0, f, p - 1, pl.ds(corner_at, 1), :]
        right = CE[level, 1, f, p - 1, pl.ds(corner_at, 1), :]
        behind = jnp.where(lane_row == 0, pltpu.roll(left, 1, 1), pltpu.roll(values, 1, 1))
        ahead = jnp.where(
            lane_row == LANES - 1,
            pltpu.roll(right, LANES - 1, 1),
            pltpu.roll(values, LANES - 1, 1),
        )
        ZB[f, p, pl.ds(at, 1), :] = ahead - behind

    def each(js):
        if len(js) == 1:
            return lambda body: body(js[0])
        return lambda body: pl.loop(0, len(js))(lambda i: body(js[0] + i * (js[1] - js[0])))

    ready = set()

    def once(*key):
        fresh = key not in ready
        ready.add(key)
        return fresh

    def sweep(level, base, hbase, offset, js, displace=True, relax=True, gate=()):
        inside = range(base, base + slab)
        for p in range(min(js) + base - 1, max(js) + base + 2):
            centre = p - base in js
            wanted = (0, 1, 2) if centre else (0, 2)
            wanted = (wanted if displace else ()) + ((3,) if relax and centre else ())
            if not centre and p - 1 - base not in js and p + 1 - base not in js:
                continue
            for f in wanted:
                if once("side", level, f, p):
                    lateral(level, f, p, p in inside)
        wires.receive(gate)
        for p in (base + j for j in js if displace):
            for f in (1, 2):
                lateral_row(level, f, p, low, TOP - 1)
                lateral_row(level, f, p, high, TOP)

        @each(js)
        def _(j):
            p = base + j
            hp = hbase + j
            beyond = g * slab + offset + j >= ng * slab
            for at, start in chunks:
                here = pl.ds(at, CHUNK)
                above, below = pl.ds(at + 1, CHUNK), pl.ds(at - 1, CHUNK)
                flat = pl.ds(start, CHUNK)
                if displace:
                    ux, uy, uz = (UE[level, c, p, here, :] for c in range(3))
                    pair_x = [UE[level, c, p + 1, here, :] + UE[level, c, p - 1, here, :] for c in range(3)]
                    pair_y = [UE[level, c, p, above, :] + UE[level, c, p, below, :] for c in range(3)]
                    pair_z = [SB[c, p, flat, :] for c in range(3)]

                    def divided_yz(q, hq):
                        return (
                            UE[level, 1, q, above, :] - UE[level, 1, q, below, :]
                            + ZB[2, q, here, :] - HH[hq, here, :]
                        )

                    def divided_xz(at_rows):
                        return (
                            UE[level, 0, p + 1, at_rows, :] - UE[level, 0, p - 1, at_rows, :]
                            + ZB[2, p, at_rows, :] - HH[hp, at_rows, :]
                        )

                    cross_x = divided_yz(p + 1, hp + 1) - divided_yz(p - 1, hp - 1)
                    cross_y = divided_xz(above) - divided_xz(below)
                    cross_z = (
                        ZB[0, p + 1, here, :] - ZB[0, p - 1, here, :]
                        + ZB[1, p, above, :] - ZB[1, p, below, :]
                        - GZ[hp, flat, :]
                    )
                    new_x = 0.12 * ux + 0.28 * pair_x[0] + 0.08 * (pair_y[0] + pair_z[0]) + 0.05 * cross_x
                    new_y = 0.12 * uy + 0.28 * pair_y[1] + 0.08 * (pair_x[1] + pair_z[1]) + 0.05 * cross_y
                    new_z = 0.12 * uz + 0.28 * pair_z[2] + 0.08 * (pair_x[2] + pair_y[2]) + 0.05 * cross_z
                    for f, value in enumerate((new_x, new_y, new_z)):
                        if offset:
                            value = jnp.where(beyond, 0.0, value)
                        UE[level + 1, f, 1 + j, here, :] = value
                if relax:
                    v = UE[level, 3, p, here, :]
                    c = CC[hp, here, :]
                    flux = CZP[hp, flat, :] * (PZP[p, flat, :] - v) + CZM[hp, flat, :] * (PZM[p, flat, :] - v)
                    for q, hq, r in ((p + 1, hp + 1, here), (p - 1, hp - 1, here), (p, hp, above), (p, hp, below)):
                        flux = flux + (CC[hq, r, :] + c) * (UE[level, 3, q, r, :] - v)
                    new_v = v + flux
                    if offset:
                        new_v = jnp.where(beyond, 1.0, new_v)
                    UE[level + 1, 3, 1 + j, here, :] = new_v

    def h_of(phase):
        return phase * phase * (3.0 - 2.0 * phase)

    def pack_phase(step):
        pack([(p, PH, (step, 1 + p)) for p in range(slab)])
        SCP[step, 1] = TT[pl.ds(0, slab, stride=2), :]
        SCP[step, 0] = TT[pl.ds(1, slab, stride=2), :]

    def send_phase_rims(step, dg):
        sent = []
        for dz in (-1, 1):
            sent.append(
                wires.send(
                    SCP.at[step, 0 if dz < 0 else 1],
                    RCP.at[step, -dg, 1 if dz < 0 else 0],
                    dg, 0, dz,
                )
            )
        for dy, src, dst in ((-1, TOP, high), (1, TOP + rows - 1, low)):
            sent.append(
                wires.send(
                    PH.at[step, pl.ds(1, slab), pl.ds(src, 1)],
                    PH.at[step, pl.ds(1 - dg * slab, slab), pl.ds(dst, 1)],
                    dg, dy, 0,
                )
            )
        return sent

    def send_phase_planes(step, moves):
        return [
            wires.send(
                PH.at[step, pl.ds(src, count), own], PH.at[step, pl.ds(dst, count), own], dg, 0, 0
            )
            for dg, src, dst, count in moves
        ]

    def unpack_phase(step, slot):
        TS[pl.ds(0, slab, stride=2), :] = RCP[step, slot, 1]
        TS[pl.ds(1, slab, stride=2), :] = RCP[step, slot, 0]
        HP[slot] = jnp.transpose(TS[...])

    def derive(step, p, centre):
        slot = 0 if p <= slab else 1
        for at, start in chunks:
            flat = pl.ds(start, CHUNK)
            phase = PH[step, p, pl.ds(at, CHUNK), :]
            h = h_of(phase)
            c = 0.0075 + 0.0675 * h
            HH[p, pl.ds(at, CHUNK), :] = 0.52 * h
            CC[p, pl.ds(at, CHUNK), :] = c
            if centre:
                behind, ahead = sides(phase, HP[slot, flat, :], 2 * (p - 1 - slot * slab))
                h_behind, h_ahead = h_of(behind), h_of(ahead)
                GZ[p, flat, :] = 0.52 * (h_ahead - h_behind)
                CZP[p, flat, :] = c + (0.0075 + 0.0675 * h_ahead)
                CZM[p, flat, :] = c + (0.0075 + 0.0675 * h_behind)
                PZ[p, flat, :] = ahead + behind
        if centre:
            for at in (low, high):
                h = h_of(PH[step, p, pl.ds(at, 1), :])
                HH[p, pl.ds(at, 1), :] = 0.52 * h
                CC[p, pl.ds(at, 1), :] = 0.0075 + 0.0675 * h

    def phase_update(step, level, base, hbase, offset, js, store):
        for j in js:
            if once("side", level, 2, base + j):
                lateral(level, 2, base + j, True)

        @each(js)
        def _(j):
            p = base + j
            hp = hbase + j
            beyond = g * slab + offset + j >= ng * slab
            for at, start in chunks:
                here = pl.ds(at, CHUNK)
                above, below = pl.ds(at + 1, CHUNK), pl.ds(at - 1, CHUNK)
                flat = pl.ds(start, CHUNK)
                twice = (
                    UE[level, 0, p + 1, here, :] - UE[level, 0, p - 1, here, :]
                    + UE[level, 1, p, above, :] - UE[level, 1, p, below, :]
                    + ZB[2, p, here, :]
                )
                over = UE[level, 3, p, here, :] - 0.5 + 0.325 * twice - 0.375 * HH[hp, here, :]
                drive = jnp.exp(over) - jnp.exp(-over)
                phase = PH[step, hp, here, :]
                nearby = (
                    PH[step, hp + 1, here, :] + PH[step, hp - 1, here, :]
                    + PH[step, hp, above, :] + PH[step, hp, below, :]
                    + PZ[hp, flat, :] - 6.0 * phase
                )
                well = phase * (1.0 - phase)
                change = nearby - well * (2.0 * (1.0 - 2.0 * phase) + 3.0 * drive)
                value = phase + 0.05 * change
                if offset:
                    value = jnp.where(beyond, 0.0, value)
                store(j, at, start, value)

    count = len([p for p in partners if p[0] == 0])
    total = count + sum(
        9 * jnp.where(ok, 1, 0) for ok in (g > 0, g < ng - 1)
    ) + sum(jnp.where(ok, 1, 0) for ok in (g > 1, g < ng - 2))
    pack_phase(0)
    loads[0].wait()
    loads[1].wait()
    pack_level(0, (1, 2, 3, 4))
    pl.semaphore_wait(barrier, total)

    phase_flat = send_phase_rims(0, 0)
    flat_u = send_flat_u(0)
    flat_v = send_flat_v(0)
    far_u = send_both_ways_u(0)
    phase_far = send_phase_planes(0, ((-1, 1, 5, 1), (1, 4, 0, 1)))
    far_v = send_both_ways_v(0)
    pin_outside()
    wires.receive(phase_flat)
    unpack_phase(0, 0)
    for p in (1, 2, 3, 4):
        derive(0, p, True)
    for level in range(3):
        wires.receive(straight(flat_u))
        unpack(level, 0, 0, 3 * slab)
        sweep(level, 1, 1, 0, (1, 2), relax=False, gate=across(flat_u))
        pack_level(level + 1, (2, 3), (0, 1, 2))
        seen = set(ready)
        for core in (0, 1):

            @pl.when(lax.rem(g, 2) == core)
            def _(core=core):
                ready.clear()
                ready.update(seen)
                for right in (True, False) if core == 0 else (False, True):
                    side = [m for m in far_u if (m[0] < 0) == right]
                    wires.receive(straight(side))
                    if level == 0:
                        wires.receive([m for m in phase_far if (m[0] < 0) == right])
                        derive(0, 5 if right else 0, False)
                    if right:
                        unpack(level, 1, 0, 3)
                    else:
                        unpack(level, 2, 3 * (slab - 1), 3)
                    sweep(
                        level, 1, 1, 0, (3,) if right else (0,), relax=False, gate=across(side)
                    )

        pack_level(level + 1, (1, 4), (0, 1, 2))
        flat_u = send_flat_u(level + 1)
        if level < 2:
            far_u = send_both_ways_u(level + 1)
        else:
            ends = [planes(3, 0, 4, 0, 1), planes(3, 0, 1, 5, -1)]
        wires.receive(flat_v)
        wires.receive(far_v)
        unpack(level, 0, 3 * slab, slab)
        sweep(level, 1, 1, 0, (0, 1, 2, 3), displace=False)
        pack_level(level + 1, (1, 2, 3, 4), (3,))
        flat_v = send_flat_v(level + 1)
        if level < 2:
            far_v = send_both_ways_v(level + 1)

    far = send_rims_back(3)
    far.append(planes(3, pl.ds(1, 3), 1, 5, -1))
    wires.receive(flat_u)
    unpack(3, 0, 0, 3 * slab)

    def keep(j, at, start, value):
        PH[1, 1 + j, pl.ds(at, CHUNK), :] = value

    phase_update(0, 3, 1, 1, 0, (1, 2), keep)
    wires.receive(ends)
    phase_update(0, 3, 1, 1, 0, (0, 3), keep)
    pack_phase(1)
    phase_flat = send_phase_rims(1, 0)
    phase_far = send_phase_rims(1, -1)
    phase_far += send_phase_planes(1, ((-1, 1, 5, 2),))
    far.append(planes(3, every, 2, 6, -1))
    phase_later = send_phase_planes(1, ((-1, 3, 7, 2), (-2, 1, 9, 1)))

    wires.receive(flat_v)
    unpack(3, 0, 3 * slab, slab)
    wires.receive(phase_flat)
    unpack_phase(1, 0)
    derive(1, 1, False)
    for p in (2, 3, 4):
        derive(1, p, True)
    for level in (3, 4, 5):
        hbase, offset = level - 1, level - 2
        if level > 3:
            wires.receive(straight(flat))
            unpack_both(level, 0, slab)
        sweep(level, 2, hbase, offset, (0, 1), gate=across(flat) if level > 3 else ())
        pack_level(level + 1, (1, 2))
        if level < 5:
            next_far = send_rims_back(level + 1)
        else:
            next_far = [column(6, dz, 1, pl.ds(0, 3), -1) for dz in (-1, 1)]
            for dy in (-1, 1):
                next_far.append(row(6, dy, pl.ds(1, 1), pl.ds(1, 1), pl.ds(5, 1), -1))
        if level == 3:
            wires.receive(phase_far)
            unpack_phase(1, 1)
            derive(1, 5, True)
            derive(1, 6, True)
        elif level == 4:
            wires.receive(phase_later)
            derive(1, 7, True)
        wires.receive(straight(far))
        unpack_both(level, 1, 2)
        if level == 5:
            derive(1, 8, True)
        sweep(level, 2, hbase, offset, (2, 3), gate=across(far))
        if level < 5:
            pack_level(level + 1, (3, 4))
            flat = send_flat_u(level + 1) + send_flat_v(level + 1)
            next_far.append(planes(level + 1, every, 1, 5, -1))
            next_far.append(planes(level + 1, every, 2, 6, -1))
        else:
            pack_level(6, (3, 4), (0, 1, 2))
            flat = [column(6, dz, 0, u_pairs, 0) for dz in (-1, 1)]
            flat += [row(6, dy, pl.ds(1, 1), mine, mine, 0) for dy in (-1, 1)]
            next_far.append(planes(6, every, 1, 5, -1))
            next_far.append(planes(6, 0, 2, 6, -1))
        far = next_far

    def finish(j, at, start, value):
        out[0, j, pl.ds(start, CHUNK), :] = value

    def hand_over(p):
        out[1, p - 2] = UE[6, 3, p, own, :]
        for c in range(3):
            out[2 + c, p - 2] = UE[6, c, p, own, :]

    for p in range(2, 5):
        hand_over(p)
    wires.receive(flat)
    unpack(6, 0, 0, 3 * slab)
    phase_update(1, 6, 2, 5, 4, (0, 1), finish)
    wires.receive(far)
    unpack(6, 1, 0, 3)
    hand_over(5)
    phase_update(1, 6, 2, 5, 4, (2, 3), finish)
    wires.drain()
    assert wires.count == COPIES, wires.count


def deliver(packed, phase, potential, displacement, sem):
    copies = [
        pltpu.make_async_copy(packed.at[0], phase, sem.at[0]),
        pltpu.make_async_copy(packed.at[1], potential, sem.at[1]),
        pltpu.make_async_copy(packed.at[pl.ds(2, 3)], displacement, sem.at[2]),
    ]
    for copy in copies:
        copy.start()
    for copy in copies:
        copy.wait()


def solution(mesh):
    ng, ny, nz = (mesh.shape[a] for a in ("grow", "cy", "cz"))

    def shards(labels, roughness, potential, displacement):
        slab, rows, lanes = labels.shape
        tall = rows + 2 * TOP
        f32 = jnp.float32
        vmem = pl.BlockSpec(memory_space=pltpu.VMEM)
        hbm = pl.BlockSpec(memory_space=pltpu.HBM)
        scratch = [
            (LEVELS, 4, slab + 3, tall, lanes),
            (LEVELS, 2, 3, slab + 1, 16, lanes),
            (LEVELS, 3, 2, 4 * slab, lanes),
            (LEVELS, 2, 4 * slab, lanes),
            (2, 10, tall, lanes),
            (2, 2, 2, slab, lanes),
            (2, 2, slab, lanes),
            (10, tall, lanes),
            (10, tall, lanes),
            (10, rows, lanes),
            (10, rows, lanes),
            (10, rows, lanes),
            (10, rows, lanes),
            (3, slab + 3, tall, lanes),
            (3, slab + 3, rows, lanes),
            (slab + 3, rows, lanes),
            (slab + 3, rows, lanes),
            (lanes, lanes),
            (lanes, lanes),
            (5, lanes, lanes),
            (2, lanes, lanes),
        ]
        packed = pl.pallas_call(
            functools.partial(kernel, ng, ny, nz),
            out_shape=jax.ShapeDtypeStruct((5,) + labels.shape, f32),
            in_specs=[hbm] * 4,
            out_specs=vmem,
            scratch_shapes=[pltpu.VMEM(shape, f32) for shape in scratch]
            + [
                pltpu.VMEM(labels.shape, jnp.int32),
                pltpu.VMEM(labels.shape, f32),
                pltpu.SemaphoreType.DMA((COPIES,)),
                pltpu.SemaphoreType.DMA((COPIES,)),
                pltpu.SemaphoreType.DMA((4,)),
            ],
            compiler_params=pltpu.CompilerParams(
                collective_id=0,
                has_side_effects=True,
                vmem_limit_bytes=40 * 1024 * 1024,
            ),
            name="filament",
        )(*(pltpu.with_memory_space_constraint(a, pltpu.HBM) for a in (labels, roughness, potential, displacement)))
        return pl.pallas_call(
            deliver,
            out_shape=(
                jax.ShapeDtypeStruct(labels.shape, f32),
                jax.ShapeDtypeStruct(labels.shape, f32),
                jax.ShapeDtypeStruct(displacement.shape, f32),
            ),
            in_specs=[pl.BlockSpec(memory_space=pl.ANY)],
            out_specs=(hbm,) * 3,
            scratch_shapes=[pltpu.SemaphoreType.DMA((3,))],
            compiler_params=pltpu.CompilerParams(vmem_limit_bytes=4 * 1024 * 1024),
            name="deliver",
        )(packed)

    placed = P("grow", "cy", "cz")
    vector = P(None, "grow", "cy", "cz")
    return jax.shard_map(
        shards,
        mesh=mesh,
        in_specs=(placed, placed, placed, vector),
        out_specs=(placed, placed, vector),
        check_vma=False,
    )
```

```python
import functools

import jax
import jax.numpy as jnp
from jax import lax
from jax.experimental import pallas as pl
from jax.experimental.pallas import tpu as pltpu
from jax.sharding import PartitionSpec as P

MESH = pl.DeviceIdType.MESH
LANES = 128
TOP = 8
CHUNK = 32
LEVELS = 7
COPIES = 183


class Wires:
    def __init__(self, send_sem, recv_sem, place):
        self.send_sem, self.recv_sem = send_sem, recv_sem
        self.g, self.y, self.z, self.ng, self.ny, self.nz = place
        self.count = 0
        self.pending = []

    def send(self, src, dst, dg, dy, dz):
        index = self.count
        self.count += 1
        target = (
            self.g + dg,
            lax.rem(self.y + dy + self.ny, self.ny),
            lax.rem(self.z + dz + self.nz, self.nz),
        )
        copy = pltpu.make_async_remote_copy(
            src_ref=src,
            dst_ref=dst,
            send_sem=self.send_sem.at[index],
            recv_sem=self.recv_sem.at[index],
            device_id=target,
            device_id_type=MESH,
        )
        self.when_valid(dg, copy.start)
        self.pending.append((dg, copy))
        return (dg, copy, dy != 0)

    def when_valid(self, dg, action):
        if dg == 0:
            action()
        else:
            ok = self.g + dg >= 0 if dg < 0 else self.g + dg < self.ng
            pl.when(ok)(action)

    def receive(self, messages):
        for dg, copy, _ in messages:
            self.when_valid(-dg, copy.wait_recv)

    def drain(self):
        for dg, copy in self.pending:
            self.when_valid(dg, copy.wait_send)


def kernel(
    ng, ny, nz,
    lab, rough, pot, disp,
    out,
    UE, CS, CR, RCU, SCU, PH, RCP, SCP,
    HH, CC, GZ, CZP, CZM, PZ, ZB, SB, PZP, PZM, TS, TT, HT, HP,
    LAB, ROU,
    send_sem, recv_sem, load_sem,
):
    g, y, z = lax.axis_index("grow"), lax.axis_index("cy"), lax.axis_index("cz")
    wires = Wires(send_sem, recv_sem, (g, y, z, ng, ny, nz))
    slab = lab.shape[0]
    rows = lab.shape[1]
    low, high = TOP - 1, TOP + rows
    own = pl.ds(TOP, rows)
    pairs = 4 * slab
    f32 = jnp.float32

    barrier = pltpu.get_barrier_semaphore()
    around = [(a, b) for a in (-1, 0, 1) for b in (-1, 0, 1)]
    partners = [(0, a, b) for a, b in around if (a, b) != (0, 0)]
    partners += [(s, a, b) for s in (-1, 1) for a, b in around]
    partners += [(-2, 0, 0), (2, 0, 0)]
    for dg, dy, dz in partners:
        def greet(dg=dg, dy=dy, dz=dz):
            pl.semaphore_signal(
                barrier,
                inc=1,
                device_id=(
                    g + dg,
                    lax.rem(y + dy + ny, ny),
                    lax.rem(z + dz + nz, nz),
                ),
                device_id_type=MESH,
            )
        wires.when_valid(dg, greet)

    loads = [
        pltpu.make_async_copy(
            disp, UE.at[0, pl.ds(0, 3), pl.ds(1, slab), own], load_sem.at[0]
        ),
        pltpu.make_async_copy(pot, UE.at[0, 3, pl.ds(1, slab), own], load_sem.at[1]),
        pltpu.make_async_copy(lab, LAB, load_sem.at[2]),
        pltpu.make_async_copy(rough, ROU, load_sem.at[3]),
    ]
    for load in loads:
        load.start()
    loads[2].wait()
    loads[3].wait()
    for p in range(slab):
        mark = LAB[p].astype(f32)
        part = 0.3 * ROU[p]
        PH[0, 1 + p, own, :] = mark * (1.0 - part) + (1.0 - mark) * part

    plane_shape = UE.shape[3:]

    def pin_outside():
        @pl.when(g == 0)
        def _():
            for level in range(4):
                for f in range(4):
                    UE[level, f, 0] = jnp.zeros(plane_shape, f32)
                RCU[level, 2] = jnp.zeros(RCU.shape[2:], f32)
            PH[0, 0] = jnp.ones(plane_shape, f32)

        @pl.when(g == ng - 1)
        def _():
            is_pot = lax.broadcasted_iota(jnp.int32, (pairs, LANES), 0) >= 3 * slab
            for level in range(LEVELS):
                for f in range(4):
                    for p in (5, 6):
                        UE[level, f, p] = jnp.full(plane_shape, 1.0 if f == 3 else 0.0, f32)
                CR[level, pl.ds(4, 4)] = jnp.zeros((4, LANES), f32)
                for side in range(2):
                    RCU[level, 1, side] = jnp.where(is_pot, 1.0, 0.0)
            PH[0, 5] = jnp.zeros(plane_shape, f32)
            for p in range(5, 10):
                PH[1, p] = jnp.zeros(plane_shape, f32)
            RCP[1, 1] = jnp.zeros(RCP.shape[2:], f32)

        @pl.when(g == ng - 2)
        def _():
            PH[1, 9] = jnp.zeros(plane_shape, f32)

    lane = lax.broadcasted_iota(jnp.int32, (CHUNK, LANES), 1)
    lane_row = lax.broadcasted_iota(jnp.int32, (1, LANES), 1)
    chunks = [(TOP + start, start) for start in range(0, rows, CHUNK)]

    def pack(planes):
        for at, start in chunks:
            tile = None
            for k, ref, index in planes:
                moved = pltpu.roll(ref[index + (pl.ds(at, CHUNK), slice(None))], 2 * k + 1, 1)
                tile = moved if tile is None else jnp.where(lane // 2 == k, moved, tile)
            TS[pl.ds(start, CHUNK), :] = tile
        TT[...] = jnp.transpose(TS[...])

    def pair(f, q):
        return 3 * slab + q - 1 if f == 3 else 3 * (q - 1) + f

    def pack_level(level, planes, fields=(0, 1, 2, 3)):
        pack([(pair(f, q), UE, (level, f, q)) for q in planes for f in fields])
        if 0 in fields:
            mask = functools.reduce(
                jnp.logical_or, [lane_row // 2 == pair(f, q) for q in planes for f in range(3)]
            )
            fresh = once("corner", level)
            for end, at in enumerate((0, rows - 1)):
                values = TS[pl.ds(at, 1), :]
                if planes == (1, 2):
                    CS[level, pl.ds(2 + end, 1), :] = values
                if not fresh:
                    values = jnp.where(mask, values, CS[level, pl.ds(end, 1), :])
                CS[level, pl.ds(end, 1), :] = values
        for q in planes:
            for f in fields:
                if f in (0, 3):
                    first, size = pair(f, q), 1 if f == 3 else 3
                    for side in (0, 1):
                        SCU[level, side, pl.ds(first, size)] = TT[
                            pl.ds(2 * first + 1 - side, size, stride=2), :
                        ]

    def row(level, dy, fields, here, there, dg):
        src, dst = (TOP, high) if dy < 0 else (TOP + rows - 1, low)
        return wires.send(
            UE.at[level, fields, here, pl.ds(src, 1)],
            UE.at[level, fields, there, pl.ds(dst, 1)],
            dg, dy, 0,
        )

    def straight(messages):
        return [m for m in messages if m and not m[2]]

    def across(messages):
        return [m for m in messages if m and m[2]]

    def corner(level, dy, dz, kept, slot, dg):
        src = kept + (0 if dy < 0 else 1)
        dst = 4 * slot + (0 if dz > 0 else 2) + (0 if dy > 0 else 1)
        return wires.send(
            CS.at[level, pl.ds(src, 1)], CR.at[level, pl.ds(dst, 1)], dg, dy, dz
        )

    def column(level, dz, slot, which, dg):
        return wires.send(
            SCU.at[level, 0 if dz < 0 else 1, which],
            RCU.at[level, slot, 1 if dz < 0 else 0, which],
            dg, 0, dz,
        )

    def planes(level, fields, here, there, dg):
        return wires.send(
            UE.at[level, fields, here, own], UE.at[level, fields, there, own], dg, 0, 0
        )

    every, mine = pl.ds(0, 4), pl.ds(1, slab)
    u_fields, v_field = pl.ds(0, 3), pl.ds(3, 1)
    u_pairs, v_pairs = pl.ds(0, 3 * slab), pl.ds(3 * slab, slab)

    def send_flat_u(level):
        sent = [column(level, dz, 0, u_pairs, 0) for dz in (-1, 1)]
        for dy in (-1, 1):
            sent.append(row(level, dy, u_fields, mine, mine, 0))
            for dz in (-1, 1):
                sent.append(corner(level, dy, dz, 0, 0, 0))
        return sent

    def send_flat_v(level):
        sent = [column(level, dz, 0, v_pairs, 0) for dz in (-1, 1)]
        return sent + [row(level, dy, v_field, mine, mine, 0) for dy in (-1, 1)]

    def send_both_ways_u(level):
        sent = []
        for dg, here, there, slot in ((-1, 1, 5, 1), (1, 4, 0, 2)):
            for dz in (-1, 1):
                sent.append(column(level, dz, slot, pl.ds(3 * (here - 1), 3), dg))
            for dy in (-1, 1):
                sent.append(row(level, dy, pl.ds(0, 2), pl.ds(here, 1), pl.ds(there, 1), dg))
        for dg, here, there in ((-1, 1, 5), (1, 4, 0)):
            sent.append(planes(level, u_fields, here, there, dg))
        return sent

    def send_both_ways_v(level):
        return [planes(level, 3, here, there, dg) for dg, here, there in ((-1, 1, 5), (1, 4, 0))]

    two_back = pl.ds(1, 2), pl.ds(5, 2)

    def send_rims_back_u(level):
        sent = [column(level, dz, 1, pl.ds(0, 6), -1) for dz in (-1, 1)]
        for dy in (-1, 1):
            sent.append(row(level, dy, u_fields, *two_back, -1))
            for dz in (-1, 1):
                sent.append(corner(level, dy, dz, 0 if level == 3 else 2, 1, -1))
        return sent

    def send_back_v(level):
        sent = [column(level, dz, 1, pl.ds(3 * slab, 2), -1) for dz in (-1, 1)]
        sent += [row(level, dy, v_field, *two_back, -1) for dy in (-1, 1)]
        sent.append(planes(level, 3, *two_back, -1))
        return sent

    def unpack(level, slot, first, size):
        TS[pl.ds(2 * first, size, stride=2), :] = RCU[level, slot, 1, pl.ds(first, size)]
        TS[pl.ds(2 * first + 1, size, stride=2), :] = RCU[level, slot, 0, pl.ds(first, size)]
        HT[slot if first < 3 * slab else 3 + slot] = jnp.transpose(TS[...])

    def halo_lane(f, p):
        slot, q = (2, slab) if p == 0 else (0, p) if p <= slab else (1, p - slab)
        return slot + (3 if f == 3 else 0), 2 * pair(f, q)

    def sides(values, halo, at_lane):
        halo = pltpu.roll(halo, (2 * LANES - at_lane - 1) % LANES, 1)
        behind = jnp.where(lane == 0, halo, pltpu.roll(values, 1, 1))
        ahead = jnp.where(lane == LANES - 1, halo, pltpu.roll(values, LANES - 1, 1))
        return behind, ahead

    def lateral(level, f, p, centre):
        slot, at_lane = halo_lane(f, p)
        for at, start in chunks:
            flat = pl.ds(start, CHUNK)
            values = UE[level, f, p, pl.ds(at, CHUNK), :]
            behind, ahead = sides(values, HT[slot, flat, :], at_lane)
            if f == 3:
                PZP[p, flat, :] = ahead
                PZM[p, flat, :] = behind
            else:
                ZB[f, p, pl.ds(at, CHUNK), :] = ahead - behind
                if centre:
                    SB[f, p, flat, :] = ahead + behind

    def lateral_row(level, f, p, at, end):
        slot, q = (0, p) if p <= slab else (1, p - slab)
        k = pair(f, q)
        values = UE[level, f, p, pl.ds(at, 1), :]
        left = CR[level, pl.ds(4 * slot + end, 1), :]
        right = CR[level, pl.ds(4 * slot + 2 + end, 1), :]
        behind = jnp.where(
            lane_row == 0, pltpu.roll(left, (LANES - 2 * k) % LANES, 1), pltpu.roll(values, 1, 1)
        )
        ahead = jnp.where(
            lane_row == LANES - 1,
            pltpu.roll(right, LANES - 2 - 2 * k, 1),
            pltpu.roll(values, LANES - 1, 1),
        )
        ZB[f, p, pl.ds(at, 1), :] = ahead - behind

    def each(js):
        if len(js) == 1:
            return lambda body: body(js[0])
        return lambda body: pl.loop(0, len(js))(lambda i: body(js[0] + i * (js[1] - js[0])))

    ready = set()

    def once(*key):
        fresh = key not in ready
        ready.add(key)
        return fresh

    def sweep(level, base, hbase, offset, js, displace=True, relax=True, gate=()):
        inside = range(base, base + slab)
        for p in range(min(js) + base - 1, max(js) + base + 2):
            centre = p - base in js
            wanted = (0, 1, 2) if centre else (0, 2)
            wanted = (wanted if displace else ()) + ((3,) if relax and centre else ())
            if not centre and p - 1 - base not in js and p + 1 - base not in js:
                continue
            for f in wanted:
                if once("side", level, f, p):
                    lateral(level, f, p, p in inside)
        wires.receive(gate)
        for p in (base + j for j in js if displace):
            for f in (1, 2):
                lateral_row(level, f, p, low, 0)
                lateral_row(level, f, p, high, 1)

        @each(js)
        def _(j):
            p = base + j
            hp = hbase + j
            beyond = g * slab + offset + j >= ng * slab
            for at, start in chunks:
                here = pl.ds(at, CHUNK)
                above, below = pl.ds(at + 1, CHUNK), pl.ds(at - 1, CHUNK)
                flat = pl.ds(start, CHUNK)
                if displace:
                    ux, uy, uz = (UE[level, c, p, here, :] for c in range(3))
                    pair_x = [UE[level, c, p + 1, here, :] + UE[level, c, p - 1, here, :] for c in range(3)]
                    pair_y = [UE[level, c, p, above, :] + UE[level, c, p, below, :] for c in range(3)]
                    pair_z = [SB[c, p, flat, :] for c in range(3)]

                    def divided_yz(q, hq):
                        return (
                            UE[level, 1, q, above, :] - UE[level, 1, q, below, :]
                            + ZB[2, q, here, :] - HH[hq, here, :]
                        )

                    def divided_xz(at_rows):
                        return (
                            UE[level, 0, p + 1, at_rows, :] - UE[level, 0, p - 1, at_rows, :]
                            + ZB[2, p, at_rows, :] - HH[hp, at_rows, :]
                        )

                    cross_x = divided_yz(p + 1, hp + 1) - divided_yz(p - 1, hp - 1)
                    cross_y = divided_xz(above) - divided_xz(below)
                    cross_z = (
                        ZB[0, p + 1, here, :] - ZB[0, p - 1, here, :]
                        + ZB[1, p, above, :] - ZB[1, p, below, :]
                        - GZ[hp, flat, :]
                    )
                    new_x = 0.12 * ux + 0.28 * pair_x[0] + 0.08 * (pair_y[0] + pair_z[0]) + 0.05 * cross_x
                    new_y = 0.12 * uy + 0.28 * pair_y[1] + 0.08 * (pair_x[1] + pair_z[1]) + 0.05 * cross_y
                    new_z = 0.12 * uz + 0.28 * pair_z[2] + 0.08 * (pair_x[2] + pair_y[2]) + 0.05 * cross_z
                    for f, value in enumerate((new_x, new_y, new_z)):
                        if offset:
                            value = jnp.where(beyond, 0.0, value)
                        UE[level + 1, f, 1 + j, here, :] = value
                if relax:
                    v = UE[level, 3, p, here, :]
                    c = CC[hp, here, :]
                    flux = CZP[hp, flat, :] * (PZP[p, flat, :] - v) + CZM[hp, flat, :] * (PZM[p, flat, :] - v)
                    for q, hq, r in ((p + 1, hp + 1, here), (p - 1, hp - 1, here), (p, hp, above), (p, hp, below)):
                        flux = flux + (CC[hq, r, :] + c) * (UE[level, 3, q, r, :] - v)
                    new_v = v + flux
                    if offset:
                        new_v = jnp.where(beyond, 1.0, new_v)
                    UE[level + 1, 3, 1 + j, here, :] = new_v

    def h_of(phase):
        return phase * phase * (3.0 - 2.0 * phase)

    def pack_phase(step):
        pack([(p, PH, (step, 1 + p)) for p in range(slab)])
        SCP[step, 1] = TT[pl.ds(0, slab, stride=2), :]
        SCP[step, 0] = TT[pl.ds(1, slab, stride=2), :]

    def send_phase_rims(step, dg):
        sent = []
        for dz in (-1, 1):
            sent.append(
                wires.send(
                    SCP.at[step, 0 if dz < 0 else 1],
                    RCP.at[step, -dg, 1 if dz < 0 else 0],
                    dg, 0, dz,
                )
            )
        for dy, src, dst in ((-1, TOP, high), (1, TOP + rows - 1, low)):
            sent.append(
                wires.send(
                    PH.at[step, pl.ds(1, slab), pl.ds(src, 1)],
                    PH.at[step, pl.ds(1 - dg * slab, slab), pl.ds(dst, 1)],
                    dg, dy, 0,
                )
            )
        return sent

    def send_phase_planes(step, moves):
        return [
            wires.send(
                PH.at[step, pl.ds(src, count), own], PH.at[step, pl.ds(dst, count), own], dg, 0, 0
            )
            for dg, src, dst, count in moves
        ]

    def unpack_phase(step, slot):
        TS[pl.ds(0, slab, stride=2), :] = RCP[step, slot, 1]
        TS[pl.ds(1, slab, stride=2), :] = RCP[step, slot, 0]
        HP[slot] = jnp.transpose(TS[...])

    def derive(step, p, centre):
        slot = 0 if p <= slab else 1
        for at, start in chunks:
            flat = pl.ds(start, CHUNK)
            phase = PH[step, p, pl.ds(at, CHUNK), :]
            h = h_of(phase)
            c = 0.0075 + 0.0675 * h
            HH[p, pl.ds(at, CHUNK), :] = 0.52 * h
            CC[p, pl.ds(at, CHUNK), :] = c
            if centre:
                behind, ahead = sides(phase, HP[slot, flat, :], 2 * (p - 1 - slot * slab))
                h_behind, h_ahead = h_of(behind), h_of(ahead)
                GZ[p, flat, :] = 0.52 * (h_ahead - h_behind)
                CZP[p, flat, :] = c + (0.0075 + 0.0675 * h_ahead)
                CZM[p, flat, :] = c + (0.0075 + 0.0675 * h_behind)
                PZ[p, flat, :] = ahead + behind
        if centre:
            for at in (low, high):
                h = h_of(PH[step, p, pl.ds(at, 1), :])
                HH[p, pl.ds(at, 1), :] = 0.52 * h
                CC[p, pl.ds(at, 1), :] = 0.0075 + 0.0675 * h

    def phase_update(step, level, base, hbase, offset, js, store):
        for j in js:
            if once("side", level, 2, base + j):
                lateral(level, 2, base + j, True)

        @each(js)
        def _(j):
            p = base + j
            hp = hbase + j
            beyond = g * slab + offset + j >= ng * slab
            for at, start in chunks:
                here = pl.ds(at, CHUNK)
                above, below = pl.ds(at + 1, CHUNK), pl.ds(at - 1, CHUNK)
                flat = pl.ds(start, CHUNK)
                twice = (
                    UE[level, 0, p + 1, here, :] - UE[level, 0, p - 1, here, :]
                    + UE[level, 1, p, above, :] - UE[level, 1, p, below, :]
                    + ZB[2, p, here, :]
                )
                over = UE[level, 3, p, here, :] - 0.5 + 0.325 * twice - 0.375 * HH[hp, here, :]
                drive = jnp.exp(over) - jnp.exp(-over)
                phase = PH[step, hp, here, :]
                nearby = (
                    PH[step, hp + 1, here, :] + PH[step, hp - 1, here, :]
                    + PH[step, hp, above, :] + PH[step, hp, below, :]
                    + PZ[hp, flat, :] - 6.0 * phase
                )
                well = phase * (1.0 - phase)
                change = nearby - well * (2.0 * (1.0 - 2.0 * phase) + 3.0 * drive)
                value = phase + 0.05 * change
                if offset:
                    value = jnp.where(beyond, 0.0, value)
                store(j, at, start, value)

    count = len([p for p in partners if p[0] == 0])
    total = count + sum(
        9 * jnp.where(ok, 1, 0) for ok in (g > 0, g < ng - 1)
    ) + sum(jnp.where(ok, 1, 0) for ok in (g > 1, g < ng - 2))
    pack_phase(0)
    loads[0].wait()
    loads[1].wait()
    pack_level(0, (1, 2, 3, 4))
    pl.semaphore_wait(barrier, total)

    phase_flat = send_phase_rims(0, 0)
    flat_u = send_flat_u(0)
    flat_v = send_flat_v(0)
    far_u = send_both_ways_u(0)
    phase_far = send_phase_planes(0, ((-1, 1, 5, 1), (1, 4, 0, 1)))
    far_v = send_both_ways_v(0)
    pin_outside()
    wires.receive(phase_flat)
    unpack_phase(0, 0)
    for p in (1, 2, 3, 4):
        derive(0, p, True)
    for level in range(3):
        wires.receive(straight(flat_u))
        unpack(level, 0, 0, 3 * slab)
        sweep(level, 1, 1, 0, (1, 2), relax=False, gate=across(flat_u))
        pack_level(level + 1, (2, 3), (0, 1, 2))
        seen = set(ready)
        for core in (0, 1):

            @pl.when(lax.rem(g, 2) == core)
            def _(core=core):
                ready.clear()
                ready.update(seen)
                for right in (True, False) if core == 0 else (False, True):
                    side = [m for m in far_u if m and (m[0] < 0) == right]
                    wires.receive(straight(side))
                    if level == 0:
                        wires.receive([m for m in phase_far if m and (m[0] < 0) == right])
                        derive(0, 5 if right else 0, False)
                    if right:
                        unpack(level, 1, 0, 3)
                    else:
                        unpack(level, 2, 3 * (slab - 1), 3)
                    sweep(
                        level, 1, 1, 0, (3,) if right else (0,), relax=False, gate=across(side)
                    )

        pack_level(level + 1, (1, 4), (0, 1, 2))
        flat_u = send_flat_u(level + 1)
        if level < 2:
            far_u = send_both_ways_u(level + 1)
        else:
            ends = [planes(3, 0, 4, 0, 1), planes(3, 0, 1, 5, -1)]
        wires.receive(flat_v)
        wires.receive(far_v)
        unpack(level, 0, 3 * slab, slab)
        sweep(level, 1, 1, 0, (0, 1, 2, 3), displace=False)
        pack_level(level + 1, (1, 2, 3, 4), (3,))
        flat_v = send_flat_v(level + 1)
        if level < 2:
            far_v = send_both_ways_v(level + 1)

    far_u = send_rims_back_u(3)
    far_u.append(planes(3, pl.ds(1, 2), 1, 5, -1))
    wires.receive(flat_u)
    unpack(3, 0, 0, 3 * slab)

    def keep(j, at, start, value):
        PH[1, 1 + j, pl.ds(at, CHUNK), :] = value

    phase_update(0, 3, 1, 1, 0, (1, 2), keep)
    wires.receive(ends)
    phase_update(0, 3, 1, 1, 0, (0, 3), keep)
    pack_phase(1)
    phase_flat = send_phase_rims(1, 0)
    phase_far = send_phase_rims(1, -1)
    phase_far += send_phase_planes(1, ((-1, 1, 5, 2),))
    last_u = [planes(3, u_fields, 2, 6, -1)]
    far_v = send_back_v(3)
    phase_later = send_phase_planes(1, ((-1, 3, 7, 2), (-2, 1, 9, 1)))

    wires.receive(phase_flat)
    unpack_phase(1, 0)
    derive(1, 1, False)
    for p in (2, 3, 4):
        derive(1, p, True)
    for level in (3, 4, 5):
        hbase, offset = level - 1, level - 2
        if level > 3:
            wires.receive(straight(flat_u))
            unpack(level, 0, 0, 3 * slab)
        sweep(
            level, 2, hbase, offset, (0, 1), relax=False, gate=across(flat_u) if level > 3 else ()
        )
        pack_level(level + 1, (1, 2), (0, 1, 2))
        if level < 5:
            next_u = send_rims_back_u(level + 1)
        else:
            next_u = [column(6, dz, 1, pl.ds(0, 3), -1) for dz in (-1, 1)]
            for dy in (-1, 1):
                next_u.append(row(6, dy, pl.ds(1, 1), pl.ds(1, 1), pl.ds(5, 1), -1))
        if level == 3:
            wires.receive(phase_far)
            unpack_phase(1, 1)
            derive(1, 5, True)
            derive(1, 6, True)
        elif level == 4:
            wires.receive(phase_later)
            derive(1, 7, True)
        wires.receive(straight(far_u))
        unpack(level, 1, 0, 6)
        if level == 5:
            derive(1, 8, True)
        sweep(level, 2, hbase, offset, (2,), relax=False, gate=across(far_u))
        wires.receive(last_u)
        sweep(level, 2, hbase, offset, (3,), relax=False)
        pack_level(level + 1, (3, 4), (0, 1, 2))
        if level < 5:
            flat_u = send_flat_u(level + 1)
        else:
            flat_u = [column(6, dz, 0, u_pairs, 0) for dz in (-1, 1)]
            flat_u += [row(6, dy, pl.ds(1, 1), mine, mine, 0) for dy in (-1, 1)]
        next_u.append(planes(level + 1, u_fields, 1, 5, -1))
        last_u = [planes(level + 1, u_fields if level < 5 else 0, 2, 6, -1)]
        far_u = next_u

        wires.receive(flat_v)
        unpack(level, 0, 3 * slab, slab)
        wires.receive(far_v)
        unpack(level, 1, 3 * slab, 2)
        sweep(level, 2, hbase, offset, (0, 1, 2, 3), displace=False)
        if level < 5:
            pack_level(level + 1, (1, 2, 3, 4), (3,))
            flat_v = send_flat_v(level + 1)
            far_v = send_back_v(level + 1)
        else:
            far_v = [planes(6, 3, 1, 5, -1)]

    def finish(j, at, start, value):
        out[0, j, pl.ds(start, CHUNK), :] = value

    def hand_over(p):
        out[1, p - 2] = UE[6, 3, p, own, :]
        for c in range(3):
            out[2 + c, p - 2] = UE[6, c, p, own, :]

    for p in range(2, 5):
        hand_over(p)
    wires.receive(flat_u)
    unpack(6, 0, 0, 3 * slab)
    phase_update(1, 6, 2, 5, 4, (0, 1), finish)
    wires.receive(far_u)
    wires.receive(last_u)
    wires.receive(far_v)
    unpack(6, 1, 0, 3)
    hand_over(5)
    phase_update(1, 6, 2, 5, 4, (2, 3), finish)
    wires.drain()
    assert wires.count == COPIES, wires.count


def deliver(packed, phase, potential, displacement, sem):
    copies = [
        pltpu.make_async_copy(packed.at[0], phase, sem.at[0]),
        pltpu.make_async_copy(packed.at[1], potential, sem.at[1]),
        pltpu.make_async_copy(packed.at[pl.ds(2, 3)], displacement, sem.at[2]),
    ]
    for copy in copies:
        copy.start()
    for copy in copies:
        copy.wait()


def solution(mesh):
    ng, ny, nz = (mesh.shape[a] for a in ("grow", "cy", "cz"))

    def shards(labels, roughness, potential, displacement):
        slab, rows, lanes = labels.shape
        tall = rows + 2 * TOP
        f32 = jnp.float32
        vmem = pl.BlockSpec(memory_space=pltpu.VMEM)
        hbm = pl.BlockSpec(memory_space=pltpu.HBM)
        scratch = [
            (LEVELS, 4, slab + 3, tall, lanes),
            (LEVELS, 8, lanes),
            (LEVELS, 8, lanes),
            (LEVELS, 3, 2, 4 * slab, lanes),
            (LEVELS, 2, 4 * slab, lanes),
            (2, 10, tall, lanes),
            (2, 2, 2, slab, lanes),
            (2, 2, slab, lanes),
            (10, tall, lanes),
            (10, tall, lanes),
            (10, rows, lanes),
            (10, rows, lanes),
            (10, rows, lanes),
            (10, rows, lanes),
            (3, slab + 3, tall, lanes),
            (3, slab + 3, rows, lanes),
            (slab + 3, rows, lanes),
            (slab + 3, rows, lanes),
            (lanes, lanes),
            (lanes, lanes),
            (5, lanes, lanes),
            (2, lanes, lanes),
        ]
        packed = pl.pallas_call(
            functools.partial(kernel, ng, ny, nz),
            out_shape=jax.ShapeDtypeStruct((5,) + labels.shape, f32),
            in_specs=[hbm] * 4,
            out_specs=vmem,
            scratch_shapes=[pltpu.VMEM(shape, f32) for shape in scratch]
            + [
                pltpu.VMEM(labels.shape, jnp.int32),
                pltpu.VMEM(labels.shape, f32),
                pltpu.SemaphoreType.DMA((COPIES,)),
                pltpu.SemaphoreType.DMA((COPIES,)),
                pltpu.SemaphoreType.DMA((4,)),
            ],
            compiler_params=pltpu.CompilerParams(
                collective_id=0,
                has_side_effects=True,
                vmem_limit_bytes=40 * 1024 * 1024,
            ),
            name="filament",
        )(*(pltpu.with_memory_space_constraint(a, pltpu.HBM) for a in (labels, roughness, potential, displacement)))
        return pl.pallas_call(
            deliver,
            out_shape=(
                jax.ShapeDtypeStruct(labels.shape, f32),
                jax.ShapeDtypeStruct(labels.shape, f32),
                jax.ShapeDtypeStruct(displacement.shape, f32),
            ),
            in_specs=[pl.BlockSpec(memory_space=pl.ANY)],
            out_specs=(hbm,) * 3,
            scratch_shapes=[pltpu.SemaphoreType.DMA((3,))],
            compiler_params=pltpu.CompilerParams(vmem_limit_bytes=4 * 1024 * 1024),
            name="deliver",
        )(packed)

    placed = P("grow", "cy", "cz")
    vector = P(None, "grow", "cy", "cz")
    return jax.shard_map(
        shards,
        mesh=mesh,
        in_specs=(placed, placed, placed, vector),
        out_specs=(placed, placed, vector),
        check_vma=False,
    )
```

```python
import functools

import jax
import jax.numpy as jnp
from jax import lax
from jax.experimental import pallas as pl
from jax.experimental.pallas import tpu as pltpu
from jax.sharding import PartitionSpec as P

MESH = pl.DeviceIdType.MESH
LANES = 128
TOP = 8
CHUNK = 32
LEVELS = 7
SENDS = 64
LANDINGS = 131


class Wires:
    def __init__(self, send_sem, recv_sem, place):
        self.send_sem, self.recv_sem = send_sem, recv_sem
        self.g, self.y, self.z, self.ng, self.ny, self.nz = place
        self.landings = 0
        self.pending = []
        self.keyed = {}

    def send(self, src, dst, dg, dy, dz, key=None):
        index = len(self.pending)
        if index >= SENDS:
            old_dg, old = self.pending[index - SENDS]
            self.when_valid(old_dg, old.wait_send)
        target = (
            self.g + dg,
            lax.rem(self.y + dy + self.ny, self.ny),
            lax.rem(self.z + dz + self.nz, self.nz),
        )
        copy = pltpu.make_async_remote_copy(
            src_ref=src,
            dst_ref=dst,
            send_sem=self.send_sem.at[index % SENDS],
            recv_sem=self.recv_sem.at[self.landing(key)],
            device_id=target,
            device_id_type=MESH,
        )
        self.when_valid(dg, copy.start)
        self.pending.append((dg, copy))
        return (dg, copy, dy != 0)

    def landing(self, key):
        if key is not None:
            uses = self.keyed.setdefault(key, [])
            uses.append(uses[-2] if len(uses) > 1 else self.landings)
            if len(uses) > 2:
                return uses[-1]
        self.landings += 1
        return self.landings - 1

    def when_valid(self, dg, action):
        if dg == 0:
            action()
        else:
            ok = self.g + dg >= 0 if dg < 0 else self.g + dg < self.ng
            pl.when(ok)(action)

    def receive(self, messages):
        for dg, copy, _ in messages:
            self.when_valid(-dg, copy.wait_recv)

    def drain(self):
        for dg, copy in self.pending[-SENDS:]:
            self.when_valid(dg, copy.wait_send)


def kernel(
    ng, ny, nz,
    lab, rough, pot, disp,
    out,
    UE, CS, CR, RCU, SCU, PH, RCP, SCP,
    HH, CC, GZ, CZP, CZM, PZ, ZB, SB, PZP, PZM, TS, TT, HT, HP,
    LAB, ROU,
    send_sem, recv_sem, load_sem,
):
    g, y, z = lax.axis_index("grow"), lax.axis_index("cy"), lax.axis_index("cz")
    wires = Wires(send_sem, recv_sem, (g, y, z, ng, ny, nz))
    slab = lab.shape[0]
    rows = lab.shape[1]
    low, high = TOP - 1, TOP + rows
    own = pl.ds(TOP, rows)
    pairs = 4 * slab
    f32 = jnp.float32

    barrier = pltpu.get_barrier_semaphore()
    around = [(a, b) for a in (-1, 0, 1) for b in (-1, 0, 1)]
    partners = [(0, a, b) for a, b in around if (a, b) != (0, 0)]
    partners += [(s, a, b) for s in (-1, 1) for a, b in around]
    partners += [(-2, 0, 0), (2, 0, 0)]
    for dg, dy, dz in partners:
        def greet(dg=dg, dy=dy, dz=dz):
            pl.semaphore_signal(
                barrier,
                inc=1,
                device_id=(
                    g + dg,
                    lax.rem(y + dy + ny, ny),
                    lax.rem(z + dz + nz, nz),
                ),
                device_id_type=MESH,
            )
        wires.when_valid(dg, greet)

    loads = [
        pltpu.make_async_copy(
            disp, UE.at[0, pl.ds(0, 3), pl.ds(1, slab), own], load_sem.at[0]
        ),
        pltpu.make_async_copy(pot, UE.at[0, 3, pl.ds(1, slab), own], load_sem.at[1]),
        pltpu.make_async_copy(lab, LAB, load_sem.at[2]),
        pltpu.make_async_copy(rough, ROU, load_sem.at[3]),
    ]
    for load in loads:
        load.start()
    loads[2].wait()
    loads[3].wait()
    for p in range(slab):
        mark = LAB[p].astype(f32)
        part = 0.3 * ROU[p]
        PH[0, 1 + p, own, :] = mark * (1.0 - part) + (1.0 - mark) * part

    plane_shape = UE.shape[3:]

    def pin_outside():
        @pl.when(g == 0)
        def _():
            for level in range(4):
                for f in range(4):
                    UE[level, f, 0] = jnp.zeros(plane_shape, f32)
                RCU[level, 2] = jnp.zeros(RCU.shape[2:], f32)
            PH[0, 0] = jnp.ones(plane_shape, f32)

        @pl.when(g == ng - 1)
        def _():
            is_pot = lax.broadcasted_iota(jnp.int32, (pairs, LANES), 0) >= 3 * slab
            for level in range(LEVELS):
                for f in range(4):
                    for p in (5, 6):
                        UE[level, f, p] = jnp.full(plane_shape, 1.0 if f == 3 else 0.0, f32)
                CR[level, pl.ds(4, 4)] = jnp.zeros((4, LANES), f32)
                for side in range(2):
                    RCU[level, 1, side] = jnp.where(is_pot, 1.0, 0.0)
            PH[0, 5] = jnp.zeros(plane_shape, f32)
            for p in range(5, 10):
                PH[1, p] = jnp.zeros(plane_shape, f32)
            RCP[1, 1] = jnp.zeros(RCP.shape[2:], f32)

        @pl.when(g == ng - 2)
        def _():
            PH[1, 9] = jnp.zeros(plane_shape, f32)

    lane = lax.broadcasted_iota(jnp.int32, (CHUNK, LANES), 1)
    lane_row = lax.broadcasted_iota(jnp.int32, (1, LANES), 1)
    chunks = [(TOP + start, start) for start in range(0, rows, CHUNK)]

    def pack(planes):
        for at, start in chunks:
            tile = None
            for k, ref, index in planes:
                moved = pltpu.roll(ref[index + (pl.ds(at, CHUNK), slice(None))], 2 * k + 1, 1)
                tile = moved if tile is None else jnp.where(lane // 2 == k, moved, tile)
            TS[pl.ds(start, CHUNK), :] = tile
        TT[...] = jnp.transpose(TS[...])

    def pair(f, q):
        return 3 * slab + q - 1 if f == 3 else 3 * (q - 1) + f

    def pack_level(level, planes, fields=(0, 1, 2, 3)):
        pack([(pair(f, q), UE, (level, f, q)) for q in planes for f in fields])
        if 0 in fields:
            mask = functools.reduce(
                jnp.logical_or, [lane_row // 2 == pair(f, q) for q in planes for f in range(3)]
            )
            fresh = once("corner", level)
            for end, at in enumerate((0, rows - 1)):
                values = TS[pl.ds(at, 1), :]
                if planes == (1, 2):
                    CS[level, pl.ds(2 + end, 1), :] = values
                if not fresh:
                    values = jnp.where(mask, values, CS[level, pl.ds(end, 1), :])
                CS[level, pl.ds(end, 1), :] = values
        for q in planes:
            for f in fields:
                if f in (0, 3):
                    first, size = pair(f, q), 1 if f == 3 else 3
                    for side in (0, 1):
                        SCU[level, side, pl.ds(first, size)] = TT[
                            pl.ds(2 * first + 1 - side, size, stride=2), :
                        ]

    def row(level, dy, fields, here, there, dg):
        src, dst = (TOP, high) if dy < 0 else (TOP + rows - 1, low)
        return wires.send(
            UE.at[level, fields, here, pl.ds(src, 1)],
            UE.at[level, fields, there, pl.ds(dst, 1)],
            dg, dy, 0,
            None if dg else ("row", dy, fields.start == 3),
        )

    def straight(messages):
        return [m for m in messages if not m[2]]

    def across(messages):
        return [m for m in messages if m[2]]

    def corner(level, dy, dz, kept, slot, dg):
        src = kept + (0 if dy < 0 else 1)
        dst = 4 * slot + (0 if dz > 0 else 2) + (0 if dy > 0 else 1)
        return wires.send(
            CS.at[level, pl.ds(src, 1)], CR.at[level, pl.ds(dst, 1)], dg, dy, dz,
            None if dg else ("corner", dy, dz),
        )

    def column(level, dz, slot, which, dg):
        return wires.send(
            SCU.at[level, 0 if dz < 0 else 1, which],
            RCU.at[level, slot, 1 if dz < 0 else 0, which],
            dg, 0, dz,
            None if dg else ("column", dz, which.start),
        )

    def planes(level, fields, here, there, dg):
        return wires.send(
            UE.at[level, fields, here, own], UE.at[level, fields, there, own], dg, 0, 0
        )

    every, mine = pl.ds(0, 4), pl.ds(1, slab)
    u_fields, v_field = pl.ds(0, 3), pl.ds(3, 1)
    u_pairs, v_pairs = pl.ds(0, 3 * slab), pl.ds(3 * slab, slab)

    def send_flat_u(level):
        sent = [column(level, dz, 0, u_pairs, 0) for dz in (-1, 1)]
        for dy in (-1, 1):
            sent.append(row(level, dy, u_fields, mine, mine, 0))
            for dz in (-1, 1):
                sent.append(corner(level, dy, dz, 0, 0, 0))
        return sent

    def send_flat_v(level):
        sent = [column(level, dz, 0, v_pairs, 0) for dz in (-1, 1)]
        return sent + [row(level, dy, v_field, mine, mine, 0) for dy in (-1, 1)]

    def send_both_ways_u(level):
        sent = []
        for dg, here, there, slot in ((-1, 1, 5, 1), (1, 4, 0, 2)):
            for dz in (-1, 1):
                sent.append(column(level, dz, slot, pl.ds(3 * (here - 1), 3), dg))
            for dy in (-1, 1):
                sent.append(row(level, dy, pl.ds(0, 2), pl.ds(here, 1), pl.ds(there, 1), dg))
        for dg, here, there in ((-1, 1, 5), (1, 4, 0)):
            sent.append(planes(level, u_fields, here, there, dg))
        return sent

    def send_both_ways_v(level):
        return [planes(level, 3, here, there, dg) for dg, here, there in ((-1, 1, 5), (1, 4, 0))]

    two_back = pl.ds(1, 2), pl.ds(5, 2)

    def send_rims_back_u(level):
        sent = [column(level, dz, 1, pl.ds(0, 6), -1) for dz in (-1, 1)]
        for dy in (-1, 1):
            sent.append(row(level, dy, u_fields, *two_back, -1))
            for dz in (-1, 1):
                sent.append(corner(level, dy, dz, 0 if level == 3 else 2, 1, -1))
        return sent

    def send_back_v(level):
        sent = [column(level, dz, 1, pl.ds(3 * slab, 2), -1) for dz in (-1, 1)]
        sent += [row(level, dy, v_field, *two_back, -1) for dy in (-1, 1)]
        sent.append(planes(level, 3, *two_back, -1))
        return sent

    def unpack(level, slot, first, size):
        TS[pl.ds(2 * first, size, stride=2), :] = RCU[level, slot, 1, pl.ds(first, size)]
        TS[pl.ds(2 * first + 1, size, stride=2), :] = RCU[level, slot, 0, pl.ds(first, size)]
        HT[slot if first < 3 * slab else 3 + slot] = jnp.transpose(TS[...])

    def halo_lane(f, p):
        slot, q = (2, slab) if p == 0 else (0, p) if p <= slab else (1, p - slab)
        return slot + (3 if f == 3 else 0), 2 * pair(f, q)

    def sides(values, halo, at_lane):
        halo = pltpu.roll(halo, (2 * LANES - at_lane - 1) % LANES, 1)
        behind = jnp.where(lane == 0, halo, pltpu.roll(values, 1, 1))
        ahead = jnp.where(lane == LANES - 1, halo, pltpu.roll(values, LANES - 1, 1))
        return behind, ahead

    def lateral(level, f, p, centre):
        slot, at_lane = halo_lane(f, p)
        for at, start in chunks:
            flat = pl.ds(start, CHUNK)
            values = UE[level, f, p, pl.ds(at, CHUNK), :]
            behind, ahead = sides(values, HT[slot, flat, :], at_lane)
            if f == 3:
                PZP[p, flat, :] = ahead
                PZM[p, flat, :] = behind
            else:
                ZB[f, p, pl.ds(at, CHUNK), :] = ahead - behind
                if centre:
                    SB[f, p, flat, :] = ahead + behind

    def lateral_row(level, f, p, at, end):
        slot, q = (0, p) if p <= slab else (1, p - slab)
        k = pair(f, q)
        values = UE[level, f, p, pl.ds(at, 1), :]
        left = CR[level, pl.ds(4 * slot + end, 1), :]
        right = CR[level, pl.ds(4 * slot + 2 + end, 1), :]
        behind = jnp.where(
            lane_row == 0, pltpu.roll(left, (LANES - 2 * k) % LANES, 1), pltpu.roll(values, 1, 1)
        )
        ahead = jnp.where(
            lane_row == LANES - 1,
            pltpu.roll(right, LANES - 2 - 2 * k, 1),
            pltpu.roll(values, LANES - 1, 1),
        )
        ZB[f, p, pl.ds(at, 1), :] = ahead - behind

    def each(js):
        if len(js) == 1:
            return lambda body: body(js[0])
        return lambda body: pl.loop(0, len(js))(lambda i: body(js[0] + i * (js[1] - js[0])))

    ready = set()

    def once(*key):
        fresh = key not in ready
        ready.add(key)
        return fresh

    def sweep(level, base, hbase, offset, js, displace=True, relax=True, gate=()):
        inside = range(base, base + slab)
        for p in range(min(js) + base - 1, max(js) + base + 2):
            centre = p - base in js
            wanted = (0, 1, 2) if centre else (0, 2)
            wanted = (wanted if displace else ()) + ((3,) if relax and centre else ())
            if not centre and p - 1 - base not in js and p + 1 - base not in js:
                continue
            for f in wanted:
                if once("side", level, f, p):
                    lateral(level, f, p, p in inside)
        if not callable(gate):
            wires.receive(gate)
        for p in (base + j for j in js if displace):
            for f in (1, 2):
                lateral_row(level, f, p, low, 0)
                lateral_row(level, f, p, high, 1)
        if callable(gate):
            gate()

        @each(js)
        def _(j):
            p = base + j
            hp = hbase + j
            beyond = g * slab + offset + j >= ng * slab
            for at, start in chunks:
                here = pl.ds(at, CHUNK)
                above, below = pl.ds(at + 1, CHUNK), pl.ds(at - 1, CHUNK)
                flat = pl.ds(start, CHUNK)
                if displace:
                    ux, uy, uz = (UE[level, c, p, here, :] for c in range(3))
                    pair_x = [UE[level, c, p + 1, here, :] + UE[level, c, p - 1, here, :] for c in range(3)]
                    pair_y = [UE[level, c, p, above, :] + UE[level, c, p, below, :] for c in range(3)]
                    pair_z = [SB[c, p, flat, :] for c in range(3)]

                    def divided_yz(q, hq):
                        return (
                            UE[level, 1, q, above, :] - UE[level, 1, q, below, :]
                            + ZB[2, q, here, :] - HH[hq, here, :]
                        )

                    def divided_xz(at_rows):
                        return (
                            UE[level, 0, p + 1, at_rows, :] - UE[level, 0, p - 1, at_rows, :]
                            + ZB[2, p, at_rows, :] - HH[hp, at_rows, :]
                        )

                    cross_x = divided_yz(p + 1, hp + 1) - divided_yz(p - 1, hp - 1)
                    cross_y = divided_xz(above) - divided_xz(below)
                    cross_z = (
                        ZB[0, p + 1, here, :] - ZB[0, p - 1, here, :]
                        + ZB[1, p, above, :] - ZB[1, p, below, :]
                        - GZ[hp, flat, :]
                    )
                    new_x = 0.12 * ux + 0.28 * pair_x[0] + 0.08 * (pair_y[0] + pair_z[0]) + 0.05 * cross_x
                    new_y = 0.12 * uy + 0.28 * pair_y[1] + 0.08 * (pair_x[1] + pair_z[1]) + 0.05 * cross_y
                    new_z = 0.12 * uz + 0.28 * pair_z[2] + 0.08 * (pair_x[2] + pair_y[2]) + 0.05 * cross_z
                    for f, value in enumerate((new_x, new_y, new_z)):
                        if offset:
                            value = jnp.where(beyond, 0.0, value)
                        UE[level + 1, f, 1 + j, here, :] = value
                if relax:
                    v = UE[level, 3, p, here, :]
                    c = CC[hp, here, :]
                    flux = CZP[hp, flat, :] * (PZP[p, flat, :] - v) + CZM[hp, flat, :] * (PZM[p, flat, :] - v)
                    for q, hq, r in ((p + 1, hp + 1, here), (p - 1, hp - 1, here), (p, hp, above), (p, hp, below)):
                        flux = flux + (CC[hq, r, :] + c) * (UE[level, 3, q, r, :] - v)
                    new_v = v + flux
                    if offset:
                        new_v = jnp.where(beyond, 1.0, new_v)
                    UE[level + 1, 3, 1 + j, here, :] = new_v

    def h_of(phase):
        return phase * phase * (3.0 - 2.0 * phase)

    def pack_phase(step):
        pack([(p, PH, (step, 1 + p)) for p in range(slab)])
        SCP[step, 1] = TT[pl.ds(0, slab, stride=2), :]
        SCP[step, 0] = TT[pl.ds(1, slab, stride=2), :]

    def send_phase_rims(step, dg):
        sent = []
        for dz in (-1, 1):
            sent.append(
                wires.send(
                    SCP.at[step, 0 if dz < 0 else 1],
                    RCP.at[step, -dg, 1 if dz < 0 else 0],
                    dg, 0, dz,
                )
            )
        for dy, src, dst in ((-1, TOP, high), (1, TOP + rows - 1, low)):
            sent.append(
                wires.send(
                    PH.at[step, pl.ds(1, slab), pl.ds(src, 1)],
                    PH.at[step, pl.ds(1 - dg * slab, slab), pl.ds(dst, 1)],
                    dg, dy, 0,
                )
            )
        return sent

    def send_phase_planes(step, moves):
        return [
            wires.send(
                PH.at[step, pl.ds(src, count), own], PH.at[step, pl.ds(dst, count), own], dg, 0, 0
            )
            for dg, src, dst, count in moves
        ]

    def unpack_phase(step, slot):
        TS[pl.ds(0, slab, stride=2), :] = RCP[step, slot, 1]
        TS[pl.ds(1, slab, stride=2), :] = RCP[step, slot, 0]
        HP[slot] = jnp.transpose(TS[...])

    def derive(step, p, centre):
        derive_own(step, p)
        if centre:
            derive_sides(step, p)

    def derive_own(step, p):
        for at, start in chunks:
            h = h_of(PH[step, p, pl.ds(at, CHUNK), :])
            HH[p, pl.ds(at, CHUNK), :] = 0.52 * h
            CC[p, pl.ds(at, CHUNK), :] = 0.0075 + 0.0675 * h

    def derive_sides(step, p):
        slot = 0 if p <= slab else 1
        for at, start in chunks:
            flat = pl.ds(start, CHUNK)
            c = CC[p, pl.ds(at, CHUNK), :]
            phase = PH[step, p, pl.ds(at, CHUNK), :]
            behind, ahead = sides(phase, HP[slot, flat, :], 2 * (p - 1 - slot * slab))
            h_behind, h_ahead = h_of(behind), h_of(ahead)
            GZ[p, flat, :] = 0.52 * (h_ahead - h_behind)
            CZP[p, flat, :] = c + (0.0075 + 0.0675 * h_ahead)
            CZM[p, flat, :] = c + (0.0075 + 0.0675 * h_behind)
            PZ[p, flat, :] = ahead + behind
        for at in (low, high):
            h = h_of(PH[step, p, pl.ds(at, 1), :])
            HH[p, pl.ds(at, 1), :] = 0.52 * h
            CC[p, pl.ds(at, 1), :] = 0.0075 + 0.0675 * h

    def phase_update(step, level, base, hbase, offset, js, store):
        for j in js:
            if once("side", level, 2, base + j):
                lateral(level, 2, base + j, True)

        @each(js)
        def _(j):
            p = base + j
            hp = hbase + j
            beyond = g * slab + offset + j >= ng * slab
            for at, start in chunks:
                here = pl.ds(at, CHUNK)
                above, below = pl.ds(at + 1, CHUNK), pl.ds(at - 1, CHUNK)
                flat = pl.ds(start, CHUNK)
                twice = (
                    UE[level, 0, p + 1, here, :] - UE[level, 0, p - 1, here, :]
                    + UE[level, 1, p, above, :] - UE[level, 1, p, below, :]
                    + ZB[2, p, here, :]
                )
                over = UE[level, 3, p, here, :] - 0.5 + 0.325 * twice - 0.375 * HH[hp, here, :]
                drive = jnp.exp(over) - jnp.exp(-over)
                phase = PH[step, hp, here, :]
                nearby = (
                    PH[step, hp + 1, here, :] + PH[step, hp - 1, here, :]
                    + PH[step, hp, above, :] + PH[step, hp, below, :]
                    + PZ[hp, flat, :] - 6.0 * phase
                )
                well = phase * (1.0 - phase)
                change = nearby - well * (2.0 * (1.0 - 2.0 * phase) + 3.0 * drive)
                value = phase + 0.05 * change
                if offset:
                    value = jnp.where(beyond, 0.0, value)
                store(j, at, start, value)

    count = len([p for p in partners if p[0] == 0])
    total = count + sum(
        9 * jnp.where(ok, 1, 0) for ok in (g > 0, g < ng - 1)
    ) + sum(jnp.where(ok, 1, 0) for ok in (g > 1, g < ng - 2))
    pack_phase(0)
    loads[0].wait()
    loads[1].wait()
    pack_level(0, (1, 2, 3, 4))
    pl.semaphore_wait(barrier, total)

    phase_flat = send_phase_rims(0, 0)
    flat_u = send_flat_u(0)
    flat_v = send_flat_v(0)
    far_u = send_both_ways_u(0)
    phase_far = send_phase_planes(0, ((-1, 1, 5, 1), (1, 4, 0, 1)))
    far_v = send_both_ways_v(0)
    pin_outside()
    wires.receive(phase_flat)
    unpack_phase(0, 0)
    for p in (1, 2, 3, 4):
        derive(0, p, True)
    for level in range(3):
        wires.receive(straight(flat_u))
        unpack(level, 0, 0, 3 * slab)
        sweep(level, 1, 1, 0, (1, 2), relax=False, gate=across(flat_u))
        pack_level(level + 1, (2, 3), (0, 1, 2))
        seen = set(ready)
        for core in (0, 1):

            @pl.when(lax.rem(g, 2) == core)
            def _(core=core):
                ready.clear()
                ready.update(seen)
                for right in (True, False) if core == 0 else (False, True):
                    side = [m for m in far_u if (m[0] < 0) == right]
                    wires.receive(straight(side))
                    if level == 0:
                        wires.receive([m for m in phase_far if (m[0] < 0) == right])
                        derive(0, 5 if right else 0, False)
                    if right:
                        unpack(level, 1, 0, 3)
                    else:
                        unpack(level, 2, 3 * (slab - 1), 3)
                    sweep(
                        level, 1, 1, 0, (3,) if right else (0,), relax=False, gate=across(side)
                    )

        pack_level(level + 1, (1, 4), (0, 1, 2))
        flat_u = send_flat_u(level + 1)
        if level < 2:
            far_u = send_both_ways_u(level + 1)
        else:
            ends = [planes(3, 0, 4, 0, 1), planes(3, 0, 1, 5, -1)]
        wires.receive(flat_v)
        wires.receive(far_v)
        unpack(level, 0, 3 * slab, slab)
        sweep(level, 1, 1, 0, (0, 1, 2, 3), displace=False)
        pack_level(level + 1, (1, 2, 3, 4), (3,))
        flat_v = send_flat_v(level + 1)
        if level < 2:
            far_v = send_both_ways_v(level + 1)

    far_u = send_rims_back_u(3)
    far_u.append(planes(3, pl.ds(1, 2), 1, 5, -1))
    wires.receive(flat_u)
    unpack(3, 0, 0, 3 * slab)

    def keep(j, at, start, value):
        PH[1, 1 + j, pl.ds(at, CHUNK), :] = value

    phase_update(0, 3, 1, 1, 0, (1, 2), keep)
    wires.receive(ends)
    phase_update(0, 3, 1, 1, 0, (0, 3), keep)
    pack_phase(1)
    phase_flat = send_phase_rims(1, 0)
    phase_far = send_phase_rims(1, -1)
    phase_far += send_phase_planes(1, ((-1, 1, 5, 2),))
    last_u = [planes(3, u_fields, 2, 6, -1)]
    far_v = send_back_v(3)
    phase_later = send_phase_planes(1, ((-1, 3, 7, 2), (-2, 1, 9, 1)))

    for p in (1, 2, 3, 4):
        derive_own(1, p)

    def phase_arrives():
        wires.receive(phase_flat)
        unpack_phase(1, 0)
        derive_sides(1, 2)
        derive_sides(1, 3)

    for level in (3, 4, 5):
        hbase, offset = level - 1, level - 2
        if level > 3:
            wires.receive(straight(flat_u))
            unpack(level, 0, 0, 3 * slab)
        sweep(
            level, 2, hbase, offset, (0, 1), relax=False,
            gate=across(flat_u) if level > 3 else phase_arrives,
        )
        pack_level(level + 1, (1, 2), (0, 1, 2))
        if level < 5:
            next_u = send_rims_back_u(level + 1)
        else:
            next_u = [column(6, dz, 1, pl.ds(0, 3), -1) for dz in (-1, 1)]
            for dy in (-1, 1):
                next_u.append(row(6, dy, pl.ds(1, 1), pl.ds(1, 1), pl.ds(5, 1), -1))
        if level == 3:
            derive_sides(1, 4)
            wires.receive(phase_far)
            unpack_phase(1, 1)
            derive(1, 5, True)
            derive(1, 6, True)
        elif level == 4:
            wires.receive(phase_later)
            derive(1, 7, True)
        wires.receive(straight(far_u))
        unpack(level, 1, 0, 6)
        if level == 5:
            derive(1, 8, True)
        sweep(level, 2, hbase, offset, (2,), relax=False, gate=across(far_u))
        wires.receive(last_u)
        sweep(level, 2, hbase, offset, (3,), relax=False)
        pack_level(level + 1, (3, 4), (0, 1, 2))
        if level < 5:
            flat_u = send_flat_u(level + 1)
        else:
            flat_u = [column(6, dz, 0, u_pairs, 0) for dz in (-1, 1)]
            flat_u += [row(6, dy, pl.ds(1, 1), mine, mine, 0) for dy in (-1, 1)]
        next_u.append(planes(level + 1, u_fields, 1, 5, -1))
        last_u = [planes(level + 1, u_fields if level < 5 else 0, 2, 6, -1)]
        far_u = next_u

        wires.receive(flat_v)
        unpack(level, 0, 3 * slab, slab)
        wires.receive(far_v)
        unpack(level, 1, 3 * slab, 2)
        sweep(level, 2, hbase, offset, (0, 1, 2, 3), displace=False)
        if level < 5:
            pack_level(level + 1, (1, 2, 3, 4), (3,))
            flat_v = send_flat_v(level + 1)
            far_v = send_back_v(level + 1)
        else:
            far_v = [planes(6, 3, 1, 5, -1)]

    def finish(j, at, start, value):
        out[0, j, pl.ds(start, CHUNK), :] = value

    def hand_over(p):
        out[1, p - 2] = UE[6, 3, p, own, :]
        for c in range(3):
            out[2 + c, p - 2] = UE[6, c, p, own, :]

    for p in range(2, 5):
        hand_over(p)
    wires.receive(flat_u)
    unpack(6, 0, 0, 3 * slab)
    phase_update(1, 6, 2, 5, 4, (0, 1), finish)
    wires.receive(far_u)
    wires.receive(last_u)
    wires.receive(far_v)
    unpack(6, 1, 0, 3)
    hand_over(5)
    phase_update(1, 6, 2, 5, 4, (2, 3), finish)
    wires.drain()
    assert wires.landings == LANDINGS, wires.landings


def deliver(packed, phase, potential, displacement, sem):
    copies = [
        pltpu.make_async_copy(packed.at[0], phase, sem.at[0]),
        pltpu.make_async_copy(packed.at[1], potential, sem.at[1]),
        pltpu.make_async_copy(packed.at[pl.ds(2, 3)], displacement, sem.at[2]),
    ]
    for copy in copies:
        copy.start()
    for copy in copies:
        copy.wait()


def solution(mesh):
    ng, ny, nz = (mesh.shape[a] for a in ("grow", "cy", "cz"))

    def shards(labels, roughness, potential, displacement):
        slab, rows, lanes = labels.shape
        tall = rows + 2 * TOP
        f32 = jnp.float32
        vmem = pl.BlockSpec(memory_space=pltpu.VMEM)
        hbm = pl.BlockSpec(memory_space=pltpu.HBM)
        scratch = [
            (LEVELS, 4, slab + 3, tall, lanes),
            (LEVELS, 8, lanes),
            (LEVELS, 8, lanes),
            (LEVELS, 3, 2, 4 * slab, lanes),
            (LEVELS, 2, 4 * slab, lanes),
            (2, 10, tall, lanes),
            (2, 2, 2, slab, lanes),
            (2, 2, slab, lanes),
            (10, tall, lanes),
            (10, tall, lanes),
            (10, rows, lanes),
            (10, rows, lanes),
            (10, rows, lanes),
            (10, rows, lanes),
            (3, slab + 3, tall, lanes),
            (3, slab + 3, rows, lanes),
            (slab + 3, rows, lanes),
            (slab + 3, rows, lanes),
            (lanes, lanes),
            (lanes, lanes),
            (5, lanes, lanes),
            (2, lanes, lanes),
        ]
        packed = pl.pallas_call(
            functools.partial(kernel, ng, ny, nz),
            out_shape=jax.ShapeDtypeStruct((5,) + labels.shape, f32),
            in_specs=[hbm] * 4,
            out_specs=vmem,
            scratch_shapes=[pltpu.VMEM(shape, f32) for shape in scratch]
            + [
                pltpu.VMEM(labels.shape, jnp.int32),
                pltpu.VMEM(labels.shape, f32),
                pltpu.SemaphoreType.DMA((SENDS,)),
                pltpu.SemaphoreType.DMA((LANDINGS,)),
                pltpu.SemaphoreType.DMA((4,)),
            ],
            compiler_params=pltpu.CompilerParams(
                collective_id=0,
                has_side_effects=True,
                vmem_limit_bytes=40 * 1024 * 1024,
            ),
            name="filament",
        )(*(pltpu.with_memory_space_constraint(a, pltpu.HBM) for a in (labels, roughness, potential, displacement)))
        return pl.pallas_call(
            deliver,
            out_shape=(
                jax.ShapeDtypeStruct(labels.shape, f32),
                jax.ShapeDtypeStruct(labels.shape, f32),
                jax.ShapeDtypeStruct(displacement.shape, f32),
            ),
            in_specs=[pl.BlockSpec(memory_space=pl.ANY)],
            out_specs=(hbm,) * 3,
            scratch_shapes=[pltpu.SemaphoreType.DMA((3,))],
            compiler_params=pltpu.CompilerParams(vmem_limit_bytes=4 * 1024 * 1024),
            name="deliver",
        )(packed)

    placed = P("grow", "cy", "cz")
    vector = P(None, "grow", "cy", "cz")
    return jax.shard_map(
        shards,
        mesh=mesh,
        in_specs=(placed, placed, placed, vector),
        out_specs=(placed, placed, vector),
        check_vma=False,
    )
```

```python
import functools

import jax
import jax.numpy as jnp
from jax import lax
from jax.experimental import pallas as pl
from jax.experimental.pallas import tpu as pltpu
from jax.sharding import PartitionSpec as P

MESH = pl.DeviceIdType.MESH
LANES = 128
TOP = 8
CHUNK = 32
LEVELS = 7
SENDS = 32
LANDINGS = 119


class Wires:
    def __init__(self, send_sem, recv_sem, place):
        self.send_sem, self.recv_sem = send_sem, recv_sem
        self.g, self.y, self.z, self.ng, self.ny, self.nz = place
        self.landings = 0
        self.pending = []
        self.keyed = {}

    def send(self, src, dst, dg, dy, dz, key=None):
        index = len(self.pending)
        if index >= SENDS:
            old_dg, old = self.pending[index - SENDS]
            self.when_valid(old_dg, old.wait_send)
        target = (
            self.g + dg,
            lax.rem(self.y + dy + self.ny, self.ny),
            lax.rem(self.z + dz + self.nz, self.nz),
        )
        copy = pltpu.make_async_remote_copy(
            src_ref=src,
            dst_ref=dst,
            send_sem=self.send_sem.at[index % SENDS],
            recv_sem=self.recv_sem.at[self.landing(key)],
            device_id=target,
            device_id_type=MESH,
        )
        self.when_valid(dg, copy.start)
        self.pending.append((dg, copy))
        return (dg, copy, dy != 0)

    def landing(self, key):
        if key is not None:
            uses = self.keyed.setdefault(key, [])
            uses.append(uses[-2] if len(uses) > 1 else self.landings)
            if len(uses) > 2:
                return uses[-1]
        self.landings += 1
        return self.landings - 1

    def when_valid(self, dg, action):
        if dg == 0:
            action()
        else:
            ok = self.g + dg >= 0 if dg < 0 else self.g + dg < self.ng
            pl.when(ok)(action)

    def receive(self, messages):
        for dg, copy, _ in messages:
            self.when_valid(-dg, copy.wait_recv)

    def drain(self):
        for dg, copy in self.pending[-SENDS:]:
            self.when_valid(dg, copy.wait_send)


def kernel(
    ng, ny, nz,
    lab, rough, pot, disp,
    out,
    UE, CS, CR, RCU, SCU, PH, RCP, SCP,
    HH, CC, GZ, CZP, CZM, PZ, ZB, SB, PZP, PZM, TS, TT, HT, HP,
    LAB, ROU,
    send_sem, recv_sem, load_sem,
):
    g, y, z = lax.axis_index("grow"), lax.axis_index("cy"), lax.axis_index("cz")
    wires = Wires(send_sem, recv_sem, (g, y, z, ng, ny, nz))
    slab = lab.shape[0]
    rows = lab.shape[1]
    low, high = TOP - 1, TOP + rows
    own = pl.ds(TOP, rows)
    pairs = 4 * slab
    f32 = jnp.float32

    barrier = pltpu.get_barrier_semaphore()
    around = [(a, b) for a in (-1, 0, 1) for b in (-1, 0, 1)]
    partners = [(0, a, b) for a, b in around if (a, b) != (0, 0)]
    partners += [(s, a, b) for s in (-1, 1) for a, b in around if a * b == 0]
    for dg, dy, dz in partners:
        def greet(dg=dg, dy=dy, dz=dz):
            pl.semaphore_signal(
                barrier,
                inc=1,
                device_id=(
                    g + dg,
                    lax.rem(y + dy + ny, ny),
                    lax.rem(z + dz + nz, nz),
                ),
                device_id_type=MESH,
            )
        wires.when_valid(dg, greet)

    loads = [
        pltpu.make_async_copy(
            disp, UE.at[0, pl.ds(0, 3), pl.ds(1, slab), own], load_sem.at[0]
        ),
        pltpu.make_async_copy(pot, UE.at[0, 3, pl.ds(1, slab), own], load_sem.at[1]),
        pltpu.make_async_copy(lab, LAB, load_sem.at[2]),
        pltpu.make_async_copy(rough, ROU, load_sem.at[3]),
    ]
    for load in loads:
        load.start()
    loads[2].wait()
    loads[3].wait()
    for p in range(slab):
        mark = LAB[p].astype(f32)
        part = 0.3 * ROU[p]
        PH[0, 1 + p, own, :] = mark * (1.0 - part) + (1.0 - mark) * part

    plane_shape = UE.shape[3:]

    def pin_outside():
        @pl.when(g == 0)
        def _():
            for level in range(4):
                for f in range(4):
                    UE[level, f, 0] = jnp.zeros(plane_shape, f32)
                RCU[level, 2] = jnp.zeros(RCU.shape[2:], f32)
            PH[0, 0] = jnp.ones(plane_shape, f32)

        @pl.when(g == ng - 1)
        def _():
            is_pot = lax.broadcasted_iota(jnp.int32, (pairs, LANES), 0) >= 3 * slab
            for level in range(LEVELS):
                for f in range(4):
                    for p in (5, 6):
                        UE[level, f, p] = jnp.full(plane_shape, 1.0 if f == 3 else 0.0, f32)
                CR[level, pl.ds(4, 4)] = jnp.zeros((4, LANES), f32)
                for side in range(2):
                    RCU[level, 1, side] = jnp.where(is_pot, 1.0, 0.0)
            PH[0, 5] = jnp.zeros(plane_shape, f32)
            for p in range(5, 10):
                PH[1, p] = jnp.zeros(plane_shape, f32)
            RCP[1, 1] = jnp.zeros(RCP.shape[2:], f32)

        @pl.when(g == ng - 2)
        def _():
            PH[1, 9] = jnp.zeros(plane_shape, f32)

    lane = lax.broadcasted_iota(jnp.int32, (CHUNK, LANES), 1)
    lane_row = lax.broadcasted_iota(jnp.int32, (1, LANES), 1)
    chunks = [(TOP + start, start) for start in range(0, rows, CHUNK)]

    def pack(planes):
        for at, start in chunks:
            tile = None
            for k, ref, index in planes:
                moved = pltpu.roll(ref[index + (pl.ds(at, CHUNK), slice(None))], 2 * k + 1, 1)
                tile = moved if tile is None else jnp.where(lane // 2 == k, moved, tile)
            TS[pl.ds(start, CHUNK), :] = tile
        TT[...] = jnp.transpose(TS[...])

    def pair(f, q):
        return 3 * slab + q - 1 if f == 3 else 3 * (q - 1) + f

    def pack_level(level, planes, fields=(0, 1, 2, 3)):
        pack([(pair(f, q), UE, (level, f, q)) for q in planes for f in fields])
        if 0 in fields:
            mask = functools.reduce(
                jnp.logical_or, [lane_row // 2 == pair(f, q) for q in planes for f in range(3)]
            )
            fresh = once("corner", level)
            for end, at in enumerate((0, rows - 1)):
                values = TS[pl.ds(at, 1), :]
                if planes == (1, 2):
                    CS[level, pl.ds(2 + end, 1), :] = values
                if not fresh:
                    values = jnp.where(mask, values, CS[level, pl.ds(end, 1), :])
                CS[level, pl.ds(end, 1), :] = values
        for q in planes:
            for f in fields:
                if f in (0, 3):
                    first, size = pair(f, q), 1 if f == 3 else 3
                    for side in (0, 1):
                        SCU[level, side, pl.ds(first, size)] = TT[
                            pl.ds(2 * first + 1 - side, size, stride=2), :
                        ]

    def row(level, dy, fields, here, there, dg):
        src, dst = (TOP, high) if dy < 0 else (TOP + rows - 1, low)
        return wires.send(
            UE.at[level, fields, here, pl.ds(src, 1)],
            UE.at[level, fields, there, pl.ds(dst, 1)],
            dg, dy, 0,
            ("row", dy, fields.start == 3, dg) if dg == 0 or level < 3 else None,
        )

    def straight(messages):
        return [m for m in messages if not m[2]]

    def across(messages):
        return [m for m in messages if m[2]]

    def corner(level, dy, dz, kept, slot, dg):
        src = kept + (0 if dy < 0 else 1)
        dst = 4 * slot + (0 if dz > 0 else 2) + (0 if dy > 0 else 1)
        return wires.send(
            CS.at[level, pl.ds(src, 1)], CR.at[level, pl.ds(dst, 1)], dg, dy, dz,
            None if dg else ("corner", dy, dz),
        )

    def column(level, dz, slot, which, dg):
        return wires.send(
            SCU.at[level, 0 if dz < 0 else 1, which],
            RCU.at[level, slot, 1 if dz < 0 else 0, which],
            dg, 0, dz,
            ("column", dz, which.start, dg) if dg == 0 or level < 3 else None,
        )

    def planes(level, fields, here, there, dg):
        return wires.send(
            UE.at[level, fields, here, own], UE.at[level, fields, there, own], dg, 0, 0,
            ("plane", dg, fields == 3) if level < 3 else None,
        )

    every, mine = pl.ds(0, 4), pl.ds(1, slab)
    u_fields, v_field = pl.ds(0, 3), pl.ds(3, 1)
    u_pairs, v_pairs = pl.ds(0, 3 * slab), pl.ds(3 * slab, slab)

    def send_flat_u(level):
        sent = [column(level, dz, 0, u_pairs, 0) for dz in (-1, 1)]
        for dy in (-1, 1):
            sent.append(row(level, dy, u_fields, mine, mine, 0))
            for dz in (-1, 1):
                sent.append(corner(level, dy, dz, 0, 0, 0))
        return sent

    def send_flat_v(level):
        sent = [column(level, dz, 0, v_pairs, 0) for dz in (-1, 1)]
        return sent + [row(level, dy, v_field, mine, mine, 0) for dy in (-1, 1)]

    def send_both_ways_u(level):
        sent = []
        for dg, here, there, slot in ((-1, 1, 5, 1), (1, 4, 0, 2)):
            for dz in (-1, 1):
                sent.append(column(level, dz, slot, pl.ds(3 * (here - 1), 3), dg))
            for dy in (-1, 1):
                sent.append(row(level, dy, pl.ds(0, 2), pl.ds(here, 1), pl.ds(there, 1), dg))
        for dg, here, there in ((-1, 1, 5), (1, 4, 0)):
            sent.append(planes(level, u_fields, here, there, dg))
        return sent

    def send_both_ways_v(level):
        return [planes(level, 3, here, there, dg) for dg, here, there in ((-1, 1, 5), (1, 4, 0))]

    two_back = pl.ds(1, 2), pl.ds(5, 2)

    def send_rims_back_u(level):
        sent = [column(level, dz, 1, pl.ds(0, 6), -1) for dz in (-1, 1)]
        for dy in (-1, 1):
            sent.append(row(level, dy, u_fields, *two_back, -1))
            for dz in (-1, 1):
                sent.append(corner(level, dy, dz, 0 if level == 3 else 2, 1, -1))
        return sent

    def send_back_v(level):
        sent = [column(level, dz, 1, pl.ds(3 * slab, 2), -1) for dz in (-1, 1)]
        sent += [row(level, dy, v_field, *two_back, -1) for dy in (-1, 1)]
        sent.append(planes(level, 3, *two_back, -1))
        return sent

    def unpack(level, slot, first, size):
        TS[pl.ds(2 * first, size, stride=2), :] = RCU[level, slot, 1, pl.ds(first, size)]
        TS[pl.ds(2 * first + 1, size, stride=2), :] = RCU[level, slot, 0, pl.ds(first, size)]
        HT[slot if first < 3 * slab else 3 + slot] = jnp.transpose(TS[...])

    def halo_lane(f, p):
        slot, q = (2, slab) if p == 0 else (0, p) if p <= slab else (1, p - slab)
        return slot + (3 if f == 3 else 0), 2 * pair(f, q)

    def sides(values, halo, at_lane):
        halo = pltpu.roll(halo, (2 * LANES - at_lane - 1) % LANES, 1)
        behind = jnp.where(lane == 0, halo, pltpu.roll(values, 1, 1))
        ahead = jnp.where(lane == LANES - 1, halo, pltpu.roll(values, LANES - 1, 1))
        return behind, ahead

    def lateral(level, f, p, centre):
        slot, at_lane = halo_lane(f, p)
        for at, start in chunks:
            flat = pl.ds(start, CHUNK)
            values = UE[level, f, p, pl.ds(at, CHUNK), :]
            behind, ahead = sides(values, HT[slot, flat, :], at_lane)
            if f == 3:
                PZP[p, flat, :] = ahead
                PZM[p, flat, :] = behind
            else:
                ZB[f, p, pl.ds(at, CHUNK), :] = ahead - behind
                if centre:
                    SB[f, p, flat, :] = ahead + behind

    def lateral_row(level, f, p, at, end):
        slot, q = (0, p) if p <= slab else (1, p - slab)
        k = pair(f, q)
        values = UE[level, f, p, pl.ds(at, 1), :]
        left = CR[level, pl.ds(4 * slot + end, 1), :]
        right = CR[level, pl.ds(4 * slot + 2 + end, 1), :]
        behind = jnp.where(
            lane_row == 0, pltpu.roll(left, (LANES - 2 * k) % LANES, 1), pltpu.roll(values, 1, 1)
        )
        ahead = jnp.where(
            lane_row == LANES - 1,
            pltpu.roll(right, LANES - 2 - 2 * k, 1),
            pltpu.roll(values, LANES - 1, 1),
        )
        ZB[f, p, pl.ds(at, 1), :] = ahead - behind

    def each(js):
        if len(js) == 1:
            return lambda body: body(js[0])
        return lambda body: pl.loop(0, len(js))(lambda i: body(js[0] + i * (js[1] - js[0])))

    ready = set()

    def once(*key):
        fresh = key not in ready
        ready.add(key)
        return fresh

    def sweep(level, base, hbase, offset, js, displace=True, relax=True, gate=()):
        inside = range(base, base + slab)
        for p in range(min(js) + base - 1, max(js) + base + 2):
            centre = p - base in js
            wanted = (0, 1, 2) if centre else (0, 2)
            wanted = (wanted if displace else ()) + ((3,) if relax and centre else ())
            if not centre and p - 1 - base not in js and p + 1 - base not in js:
                continue
            for f in wanted:
                if once("side", level, f, p):
                    lateral(level, f, p, p in inside)
        if not callable(gate):
            wires.receive(gate)
        for p in (base + j for j in js if displace):
            for f in (1, 2):
                lateral_row(level, f, p, low, 0)
                lateral_row(level, f, p, high, 1)
        if callable(gate):
            gate()

        @each(js)
        def _(j):
            p = base + j
            hp = hbase + j
            beyond = g * slab + offset + j >= ng * slab
            for at, start in chunks:
                here = pl.ds(at, CHUNK)
                above, below = pl.ds(at + 1, CHUNK), pl.ds(at - 1, CHUNK)
                flat = pl.ds(start, CHUNK)
                if displace:
                    ux, uy, uz = (UE[level, c, p, here, :] for c in range(3))
                    pair_x = [UE[level, c, p + 1, here, :] + UE[level, c, p - 1, here, :] for c in range(3)]
                    pair_y = [UE[level, c, p, above, :] + UE[level, c, p, below, :] for c in range(3)]
                    pair_z = [SB[c, p, flat, :] for c in range(3)]

                    def divided_yz(q, hq):
                        return (
                            UE[level, 1, q, above, :] - UE[level, 1, q, below, :]
                            + ZB[2, q, here, :] - HH[hq, here, :]
                        )

                    def divided_xz(at_rows):
                        return (
                            UE[level, 0, p + 1, at_rows, :] - UE[level, 0, p - 1, at_rows, :]
                            + ZB[2, p, at_rows, :] - HH[hp, at_rows, :]
                        )

                    cross_x = divided_yz(p + 1, hp + 1) - divided_yz(p - 1, hp - 1)
                    cross_y = divided_xz(above) - divided_xz(below)
                    cross_z = (
                        ZB[0, p + 1, here, :] - ZB[0, p - 1, here, :]
                        + ZB[1, p, above, :] - ZB[1, p, below, :]
                        - GZ[hp, flat, :]
                    )
                    new_x = 0.12 * ux + 0.28 * pair_x[0] + 0.08 * (pair_y[0] + pair_z[0]) + 0.05 * cross_x
                    new_y = 0.12 * uy + 0.28 * pair_y[1] + 0.08 * (pair_x[1] + pair_z[1]) + 0.05 * cross_y
                    new_z = 0.12 * uz + 0.28 * pair_z[2] + 0.08 * (pair_x[2] + pair_y[2]) + 0.05 * cross_z
                    for f, value in enumerate((new_x, new_y, new_z)):
                        if offset:
                            value = jnp.where(beyond, 0.0, value)
                        UE[level + 1, f, 1 + j, here, :] = value
                if relax:
                    v = UE[level, 3, p, here, :]
                    c = CC[hp, here, :]
                    flux = CZP[hp, flat, :] * (PZP[p, flat, :] - v) + CZM[hp, flat, :] * (PZM[p, flat, :] - v)
                    for q, hq, r in ((p + 1, hp + 1, here), (p - 1, hp - 1, here), (p, hp, above), (p, hp, below)):
                        flux = flux + (CC[hq, r, :] + c) * (UE[level, 3, q, r, :] - v)
                    new_v = v + flux
                    if offset:
                        new_v = jnp.where(beyond, 1.0, new_v)
                    UE[level + 1, 3, 1 + j, here, :] = new_v

    def h_of(phase):
        return phase * phase * (3.0 - 2.0 * phase)

    def pack_phase(step):
        pack([(p, PH, (step, 1 + p)) for p in range(slab)])
        SCP[step, 1] = TT[pl.ds(0, slab, stride=2), :]
        SCP[step, 0] = TT[pl.ds(1, slab, stride=2), :]

    def send_phase_rims(step, dg):
        sent = []
        for dz in (-1, 1):
            sent.append(
                wires.send(
                    SCP.at[step, 0 if dz < 0 else 1],
                    RCP.at[step, -dg, 1 if dz < 0 else 0],
                    dg, 0, dz,
                )
            )
        for dy, src, dst in ((-1, TOP, high), (1, TOP + rows - 1, low)):
            sent.append(
                wires.send(
                    PH.at[step, pl.ds(1, slab), pl.ds(src, 1)],
                    PH.at[step, pl.ds(1 - dg * slab, slab), pl.ds(dst, 1)],
                    dg, dy, 0,
                )
            )
        return sent

    def send_phase_planes(step, moves):
        return [
            wires.send(
                PH.at[step, pl.ds(src, count), own], PH.at[step, pl.ds(dst, count), own], dg, 0, 0
            )
            for dg, src, dst, count in moves
        ]

    def unpack_phase(step, slot):
        TS[pl.ds(0, slab, stride=2), :] = RCP[step, slot, 1]
        TS[pl.ds(1, slab, stride=2), :] = RCP[step, slot, 0]
        HP[slot] = jnp.transpose(TS[...])

    def derive(step, p, centre):
        derive_own(step, p)
        if centre:
            derive_sides(step, p)

    def derive_own(step, p):
        for at, start in chunks:
            h = h_of(PH[step, p, pl.ds(at, CHUNK), :])
            HH[p, pl.ds(at, CHUNK), :] = 0.52 * h
            CC[p, pl.ds(at, CHUNK), :] = 0.0075 + 0.0675 * h

    def derive_sides(step, p):
        slot = 0 if p <= slab else 1
        for at, start in chunks:
            flat = pl.ds(start, CHUNK)
            c = CC[p, pl.ds(at, CHUNK), :]
            phase = PH[step, p, pl.ds(at, CHUNK), :]
            behind, ahead = sides(phase, HP[slot, flat, :], 2 * (p - 1 - slot * slab))
            h_behind, h_ahead = h_of(behind), h_of(ahead)
            GZ[p, flat, :] = 0.52 * (h_ahead - h_behind)
            CZP[p, flat, :] = c + (0.0075 + 0.0675 * h_ahead)
            CZM[p, flat, :] = c + (0.0075 + 0.0675 * h_behind)
            PZ[p, flat, :] = ahead + behind
        for at in (low, high):
            h = h_of(PH[step, p, pl.ds(at, 1), :])
            HH[p, pl.ds(at, 1), :] = 0.52 * h
            CC[p, pl.ds(at, 1), :] = 0.0075 + 0.0675 * h

    def phase_update(step, level, base, hbase, offset, js, store):
        for j in js:
            if once("side", level, 2, base + j):
                lateral(level, 2, base + j, True)

        @each(js)
        def _(j):
            p = base + j
            hp = hbase + j
            beyond = g * slab + offset + j >= ng * slab
            for at, start in chunks:
                here = pl.ds(at, CHUNK)
                above, below = pl.ds(at + 1, CHUNK), pl.ds(at - 1, CHUNK)
                flat = pl.ds(start, CHUNK)
                twice = (
                    UE[level, 0, p + 1, here, :] - UE[level, 0, p - 1, here, :]
                    + UE[level, 1, p, above, :] - UE[level, 1, p, below, :]
                    + ZB[2, p, here, :]
                )
                over = UE[level, 3, p, here, :] - 0.5 + 0.325 * twice - 0.375 * HH[hp, here, :]
                drive = jnp.exp(over) - jnp.exp(-over)
                phase = PH[step, hp, here, :]
                nearby = (
                    PH[step, hp + 1, here, :] + PH[step, hp - 1, here, :]
                    + PH[step, hp, above, :] + PH[step, hp, below, :]
                    + PZ[hp, flat, :] - 6.0 * phase
                )
                well = phase * (1.0 - phase)
                change = nearby - well * (2.0 * (1.0 - 2.0 * phase) + 3.0 * drive)
                value = phase + 0.05 * change
                if offset:
                    value = jnp.where(beyond, 0.0, value)
                store(j, at, start, value)

    count = len([p for p in partners if p[0] == 0])
    total = count + sum(
        5 * jnp.where(ok, 1, 0) for ok in (g > 0, g < ng - 1)
    )
    pack_phase(0)
    loads[0].wait()
    loads[1].wait()
    pack_level(0, (1, 2, 3, 4), (0, 1, 2))
    pl.semaphore_wait(barrier, total)

    phase_flat = send_phase_rims(0, 0)
    flat_u = send_flat_u(0)
    far_u = send_both_ways_u(0)
    pack_level(0, (1, 2, 3, 4), (3,))
    flat_v = send_flat_v(0)
    phase_far = send_phase_planes(0, ((-1, 1, 5, 1), (1, 4, 0, 1)))
    far_v = send_both_ways_v(0)
    pin_outside()
    wires.receive(phase_flat)
    unpack_phase(0, 0)
    for p in (1, 2, 3, 4):
        derive(0, p, True)
    for level in range(3):
        wires.receive(straight(flat_u))
        unpack(level, 0, 0, 3 * slab)
        sweep(level, 1, 1, 0, (1, 2), relax=False, gate=across(flat_u))
        pack_level(level + 1, (2, 3), (0, 1, 2))
        seen = set(ready)
        for core in (0, 1):

            @pl.when(lax.rem(g, 2) == core)
            def _(core=core):
                ready.clear()
                ready.update(seen)
                for right in (True, False) if core == 0 else (False, True):
                    side = [m for m in far_u if (m[0] < 0) == right]
                    wires.receive(straight(side))
                    if level == 0:
                        wires.receive([m for m in phase_far if (m[0] < 0) == right])
                        derive(0, 5 if right else 0, False)
                    if right:
                        unpack(level, 1, 0, 3)
                    else:
                        unpack(level, 2, 3 * (slab - 1), 3)
                    sweep(
                        level, 1, 1, 0, (3,) if right else (0,), relax=False, gate=across(side)
                    )

        pack_level(level + 1, (1, 4), (0, 1, 2))
        flat_u = send_flat_u(level + 1)
        if level < 2:
            far_u = send_both_ways_u(level + 1)
        else:
            ends = [planes(3, 0, 4, 0, 1), planes(3, 0, 1, 5, -1)]
        wires.receive(flat_v)
        wires.receive(far_v)
        unpack(level, 0, 3 * slab, slab)
        sweep(level, 1, 1, 0, (0, 1, 2, 3), displace=False)
        pack_level(level + 1, (1, 2, 3, 4), (3,))
        flat_v = send_flat_v(level + 1)
        if level < 2:
            far_v = send_both_ways_v(level + 1)

    far_u = send_rims_back_u(3)
    far_u.append(planes(3, pl.ds(1, 2), 1, 5, -1))
    wires.receive(flat_u)
    unpack(3, 0, 0, 3 * slab)

    def keep(j, at, start, value):
        PH[1, 1 + j, pl.ds(at, CHUNK), :] = value

    phase_update(0, 3, 1, 1, 0, (1, 2), keep)
    wires.receive(ends)
    phase_update(0, 3, 1, 1, 0, (0, 3), keep)
    pack_phase(1)
    phase_flat = send_phase_rims(1, 0)
    phase_far = send_phase_rims(1, -1)
    phase_far += send_phase_planes(1, ((-1, 1, 5, 2),))
    last_u = [planes(3, u_fields, 2, 6, -1)]
    far_v = send_back_v(3)
    phase_later = send_phase_planes(1, ((-1, 3, 7, 2), (-2, 1, 9, 1)))

    for p in (1, 2, 3, 4):
        derive_own(1, p)

    def phase_arrives():
        wires.receive(phase_flat)
        unpack_phase(1, 0)
        derive_sides(1, 2)
        derive_sides(1, 3)

    for level in (3, 4, 5):
        hbase, offset = level - 1, level - 2
        if level > 3:
            wires.receive(straight(flat_u))
            unpack(level, 0, 0, 3 * slab)
        sweep(
            level, 2, hbase, offset, (0, 1), relax=False,
            gate=across(flat_u) if level > 3 else phase_arrives,
        )
        pack_level(level + 1, (1, 2), (0, 1, 2))
        if level < 5:
            next_u = send_rims_back_u(level + 1)
        else:
            next_u = [column(6, dz, 1, pl.ds(0, 3), -1) for dz in (-1, 1)]
            for dy in (-1, 1):
                next_u.append(row(6, dy, pl.ds(1, 1), pl.ds(1, 1), pl.ds(5, 1), -1))
        if level == 3:
            derive_sides(1, 4)
            wires.receive(phase_far)
            unpack_phase(1, 1)
            derive(1, 5, True)
            derive(1, 6, True)
        elif level == 4:
            wires.receive(phase_later)
            derive(1, 7, True)
        wires.receive(straight(far_u))
        unpack(level, 1, 0, 6)
        if level == 5:
            derive(1, 8, True)
        sweep(level, 2, hbase, offset, (2,), relax=False, gate=across(far_u))
        wires.receive(last_u)
        sweep(level, 2, hbase, offset, (3,), relax=False)
        pack_level(level + 1, (3, 4), (0, 1, 2))
        if level < 5:
            flat_u = send_flat_u(level + 1)
        else:
            flat_u = [column(6, dz, 0, u_pairs, 0) for dz in (-1, 1)]
            flat_u += [row(6, dy, pl.ds(1, 1), mine, mine, 0) for dy in (-1, 1)]
        next_u.append(planes(level + 1, u_fields, 1, 5, -1))
        last_u = [planes(level + 1, u_fields if level < 5 else 0, 2, 6, -1)]
        far_u = next_u

        wires.receive(flat_v)
        unpack(level, 0, 3 * slab, slab)
        wires.receive(far_v)
        unpack(level, 1, 3 * slab, 2)
        sweep(level, 2, hbase, offset, (0, 1, 2, 3), displace=False)
        if level < 5:
            pack_level(level + 1, (1, 2, 3, 4), (3,))
            flat_v = send_flat_v(level + 1)
            far_v = send_back_v(level + 1)
        else:
            far_v = [planes(6, 3, 1, 5, -1)]

    def finish(j, at, start, value):
        out[0, j, pl.ds(start, CHUNK), :] = value

    def hand_over(p):
        out[1, p - 2] = UE[6, 3, p, own, :]
        for c in range(3):
            out[2 + c, p - 2] = UE[6, c, p, own, :]

    for p in range(2, 5):
        hand_over(p)
    wires.receive(flat_u)
    unpack(6, 0, 0, 3 * slab)
    phase_update(1, 6, 2, 5, 4, (0, 1), finish)
    wires.receive(far_u)
    wires.receive(last_u)
    wires.receive(far_v)
    unpack(6, 1, 0, 3)
    hand_over(5)
    phase_update(1, 6, 2, 5, 4, (2, 3), finish)
    wires.drain()
    assert wires.landings == LANDINGS, wires.landings


def deliver(packed, phase, potential, displacement, sem):
    copies = [
        pltpu.make_async_copy(packed.at[0], phase, sem.at[0]),
        pltpu.make_async_copy(packed.at[1], potential, sem.at[1]),
        pltpu.make_async_copy(packed.at[pl.ds(2, 3)], displacement, sem.at[2]),
    ]
    for copy in copies:
        copy.start()
    for copy in copies:
        copy.wait()


def solution(mesh):
    ng, ny, nz = (mesh.shape[a] for a in ("grow", "cy", "cz"))

    def shards(labels, roughness, potential, displacement):
        slab, rows, lanes = labels.shape
        tall = rows + 2 * TOP
        f32 = jnp.float32
        vmem = pl.BlockSpec(memory_space=pltpu.VMEM)
        hbm = pl.BlockSpec(memory_space=pltpu.HBM)
        scratch = [
            (LEVELS, 4, slab + 3, tall, lanes),
            (LEVELS, 8, lanes),
            (LEVELS, 8, lanes),
            (LEVELS, 3, 2, 4 * slab, lanes),
            (LEVELS, 2, 4 * slab, lanes),
            (2, 10, tall, lanes),
            (2, 2, 2, slab, lanes),
            (2, 2, slab, lanes),
            (10, tall, lanes),
            (10, tall, lanes),
            (10, rows, lanes),
            (10, rows, lanes),
            (10, rows, lanes),
            (10, rows, lanes),
            (3, slab + 3, tall, lanes),
            (3, slab + 3, rows, lanes),
            (slab + 3, rows, lanes),
            (slab + 3, rows, lanes),
            (lanes, lanes),
            (lanes, lanes),
            (5, lanes, lanes),
            (2, lanes, lanes),
        ]
        packed = pl.pallas_call(
            functools.partial(kernel, ng, ny, nz),
            out_shape=jax.ShapeDtypeStruct((5,) + labels.shape, f32),
            in_specs=[hbm] * 4,
            out_specs=vmem,
            scratch_shapes=[pltpu.VMEM(shape, f32) for shape in scratch]
            + [
                pltpu.VMEM(labels.shape, jnp.int32),
                pltpu.VMEM(labels.shape, f32),
                pltpu.SemaphoreType.DMA((SENDS,)),
                pltpu.SemaphoreType.DMA((LANDINGS,)),
                pltpu.SemaphoreType.DMA((4,)),
            ],
            compiler_params=pltpu.CompilerParams(
                collective_id=0,
                has_side_effects=True,
                vmem_limit_bytes=40 * 1024 * 1024,
            ),
            name="filament",
        )(*(pltpu.with_memory_space_constraint(a, pltpu.HBM) for a in (labels, roughness, potential, displacement)))
        return pl.pallas_call(
            deliver,
            out_shape=(
                jax.ShapeDtypeStruct(labels.shape, f32),
                jax.ShapeDtypeStruct(labels.shape, f32),
                jax.ShapeDtypeStruct(displacement.shape, f32),
            ),
            in_specs=[pl.BlockSpec(memory_space=pl.ANY)],
            out_specs=(hbm,) * 3,
            scratch_shapes=[pltpu.SemaphoreType.DMA((3,))],
            compiler_params=pltpu.CompilerParams(vmem_limit_bytes=4 * 1024 * 1024),
            name="deliver",
        )(packed)

    placed = P("grow", "cy", "cz")
    vector = P(None, "grow", "cy", "cz")
    return jax.shard_map(
        shards,
        mesh=mesh,
        in_specs=(placed, placed, placed, vector),
        out_specs=(placed, placed, vector),
        check_vma=False,
    )
```
